256 devices in a mesh: dp: 8 (over x, core), ctx: 32 (over y, z).
Axes of the slice: x: 4, y: 4, z: 8, core: 2. Of those that a mesh axis runs over, the one named last changes fastest.
Arguments:
- features: bfloat16 [8, 4096, 6144], P('dp', 'ctx'), may hold values from -6 to 6
- upstream: bfloat16 [8, 4096, 2048], P('dp', 'ctx'), may hold values from -6 to 6
- lengths: int32 [8, 8], P('dp'), may hold values from 1 to 2048, 4096 in all within a row
- conv_taps: float32 [3, 6144], replicated, may hold values from -3 to 3
- residues: float32 [16, 2048], P(None, 'ctx'), may hold values from -0.12 to 0.12
- log_rate: float32 [16, 2048], P(None, 'ctx'), may hold values from -13.2 to -3.5
- skip_gain: float32 [2048], P('ctx'), may hold values from -4 to 4
Outputs:
- grad_features: bfloat16 [8, 4096, 6144], P('dp', 'ctx')
- grad_taps: float32 [3, 6144], replicated
- grad_residues: float32 [16, 2048], P(None, 'ctx')
- grad_skip: float32 [2048], P('ctx')
The draws below stay inside these ranges and needn't reach their ends.
All inputs are finite; a program needn't handle non-finite values.
Results may differ from the reference program's by a relative error of at most 0.0095.
Values may be sent and summed in bfloat16 or wider, within the bound.
A program may use at most 192 MiB of HBM per device.

```python
import math
import jax
import jax.numpy as jnp
import numpy as np
from jax import lax

CHANNELS = 2048
POLES = 16
BLOCK_ROWS = 128
SEGMENTS = 8
WINDOW_LEN = 4096
WINDOWS = 8


def draw_log_rate(key, part):
    lowest = math.log(2e-06)
    highest = math.log(0.03)
    return jax.random.uniform(key, (POLES, CHANNELS), jnp.float32, lowest, highest)


def levels(rng, extent, pieces, low, largest):
    def one(axis_at, parts):
        heights = jax.random.uniform(jax.random.fold_in(jax.random.fold_in(rng, 6), axis_at), (parts,), jnp.float32, low / len(pieces), largest / len(pieces))
        return jnp.repeat(jnp.exp(heights), extent[axis_at] // parts).reshape((-1,) + (1,) * (len(extent) - axis_at - 1))

    level = one(*pieces[0])
    for cut in pieces[1:]:
        level = level * one(*cut)
    return level


def length_profile(amount, total, reach, lean):
    loads = [(1 << 20) // math.isqrt(standing ** lean) + 1 for standing in range(2, amount + 1)]
    spare, given = total - reach - (amount - 1), [1] * (amount - 1)
    while spare > 0:
        movable = [i for i in range(amount - 1) if given[i] < reach]
        pool, left = sum([loads[i] for i in movable]), spare
        for i in movable:
            addition = min(reach - given[i], max(1, left * loads[i] // pool), spare)
            given[i] = given[i] + addition
            spare = spare - addition
    return np.array([reach] + given)


def uneven(rng, count, total, bound, slope):
    if count == 2:
        one = jax.random.randint(rng, (), max(1, total - bound), min(bound, total - 1) + 1)
        return jnp.stack([one, total - one])
    sizes = jnp.asarray(length_profile(count, total, bound, slope), jnp.int32)
    couples = (count - 1) // 2
    donor, sink = sizes[1:1 + 2 * couples:2], sizes[2:2 + 2 * couples:2]
    room = jnp.minimum(donor - 1, bound - sink)
    passed = jax.random.randint(jax.random.fold_in(rng, 1), (couples,), 0, 1 << 20) % (room + 1)
    sizes = sizes.at[1:1 + 2 * couples:2].set(donor - passed).at[2:2 + 2 * couples:2].set(sink + passed)
    return sizes[jax.random.permutation(jax.random.fold_in(rng, 2), count)]


def normal_values(own_key, shape, spread, most, pieces=(), held_as=jnp.bfloat16):
    entries = spread * jax.random.normal(own_key, shape, jnp.float32)
    if pieces:
        entries = entries * levels(own_key, shape, pieces, -0.22, 0.18)
    return jnp.clip(entries, -most, most).astype(held_as)


def setup_inputs(seed: int = 0) -> dict:
    key_of = jax.random.split(jax.random.key(seed), 8)
    return {
        "features": normal_values(key_of[0], (WINDOWS, WINDOW_LEN, 3 * CHANNELS), 1.0, 6.0, ((0, 8), (1, 32))),
        "upstream": normal_values(key_of[1], (WINDOWS, WINDOW_LEN, CHANNELS), 1.0, 6.0, ((0, 8), (1, 32))),
        "lengths": jax.vmap(lambda own: uneven(own, SEGMENTS, WINDOW_LEN, WINDOW_LEN // 2, 2))(jax.random.split(key_of[2], WINDOWS)).reshape((WINDOWS, SEGMENTS)).astype(jnp.int32),
        "conv_taps": normal_values(key_of[3], (3, 3 * CHANNELS), 0.6, 3.0, (), jnp.float32),
        "residues": normal_values(key_of[4], (POLES, CHANNELS), 0.02, 0.12, ((1, 32),), jnp.float32),
        "log_rate": draw_log_rate(jax.random.fold_in(key_of[7], 71), 0),
        "skip_gain": normal_values(key_of[6], (CHANNELS,), 1.0, 4.0, ((0, 32),), jnp.float32),
    }


def segment_of(positions, bounds):
    return lax.optimization_barrier(jnp.sum((positions[:, None] >= bounds[None, :]).astype(jnp.int32), axis=1))

def segment_masks(positions, bounds, window_len):
    seg_ids = segment_of(positions, bounds)
    keep_one = ((positions >= 1) & (segment_of(positions - 1, bounds) == seg_ids)).astype(jnp.float32)
    keep_two = ((positions >= 2) & (segment_of(positions - 2, bounds) == seg_ids)).astype(jnp.float32)
    next_one = ((positions + 1 < window_len) & (segment_of(positions + 1, bounds) == seg_ids)).astype(jnp.float32)
    next_two = ((positions + 2 < window_len) & (segment_of(positions + 2, bounds) == seg_ids)).astype(jnp.float32)
    return (seg_ids, keep_one, keep_two, next_one, next_two)

def causal_taps(current, before, tap_rows, keep_one, keep_two):
    extended = jnp.concatenate([before, current], axis=0)
    return tap_rows[0] * current + tap_rows[1] * (keep_one[:, None] * extended[1:-1]) + tap_rows[2] * (keep_two[:, None] * extended[:-2])

def transposed_taps(current, after, tap_rows, next_one, next_two):
    extended = jnp.concatenate([current, after], axis=0)
    return tap_rows[0] * current + tap_rows[1] * (next_one[:, None] * extended[1:-1]) + tap_rows[2] * (next_two[:, None] * extended[2:])

def tap_terms(gradient, current, before, keep_one, keep_two):
    extended = jnp.concatenate([before, current], axis=0)
    first = lax.optimization_barrier(jnp.sum(gradient * current, axis=0))
    second = lax.optimization_barrier(jnp.sum(gradient * (keep_one[:, None] * extended[1:-1]), axis=0))
    third = lax.optimization_barrier(jnp.sum(gradient * (keep_two[:, None] * extended[:-2]), axis=0))
    return jnp.stack([first, second, third])

def modal_sweep(source, segment_ids, decay_rate, coeff, other):
    length, chan_count = source.shape
    pole_count = decay_rate.shape[0]
    blocks = length // BLOCK_ROWS
    per_step = 4
    groups = blocks // per_step
    offsets = jnp.arange(BLOCK_ROWS, dtype=jnp.float32)
    rising = jnp.exp(decay_rate[None] * offsets[:, None, None])
    falling = jnp.exp(-decay_rate[None] * offsets[:, None, None])
    causal = offsets[:, None] >= offsets[None, :]

    def group_fn(inputs):
        src_blk, seg_blk, other_blk = inputs
        joined_mask = ((seg_blk[:, :, None] == seg_blk[:, None, :]) & causal[None]).astype(source.dtype)
        lifted = (src_blk[:, :, None, :] * rising[None]).reshape(per_step, BLOCK_ROWS, pole_count * chan_count)
        inner_state = jnp.einsum('pij,pjk->pik', joined_mask, lifted, precision=lax.Precision.HIGHEST)
        inner_state = inner_state.reshape(per_step, BLOCK_ROWS, pole_count, chan_count) * falling[None]
        block_out = jnp.einsum('pimc,mc->pic', inner_state, coeff, precision=lax.Precision.HIGHEST)
        last_row = inner_state[:, -1]
        start_same = (seg_blk == seg_blk[:, :1]).astype(source.dtype)
        partial_sum = jnp.einsum('pic,pimc->mc', other_blk, inner_state, precision=lax.Precision.HIGHEST)
        weights = jnp.einsum('pic,imc->pmc', other_blk * start_same[:, :, None], falling, precision=lax.Precision.HIGHEST)
        return (block_out, last_row, partial_sum, weights)
    src_groups = source.reshape(groups, per_step, BLOCK_ROWS, chan_count)
    seg_groups = segment_ids.reshape(groups, per_step, BLOCK_ROWS)
    other_groups = other.reshape(groups, per_step, BLOCK_ROWS, chan_count)
    block_out, last_row, partial_sum, weights = lax.map(group_fn, (src_groups, seg_groups, other_groups))
    block_out = block_out.reshape(blocks, BLOCK_ROWS, chan_count)
    last_row = last_row.reshape(blocks, pole_count, chan_count)
    weights = weights.reshape(blocks, pole_count, chan_count)
    seg_rows = segment_ids.reshape(blocks, BLOCK_ROWS)
    starts = seg_rows[:, 0]
    finals = seg_rows[:, -1]
    joined = (starts[1:] == finals[:-1]).astype(source.dtype)
    through = (starts[:-1] == finals[:-1]).astype(source.dtype)
    one_step = jnp.exp(-decay_rate)
    block_decay = jnp.exp(-decay_rate * BLOCK_ROWS)
    factors = (joined * through)[:, None, None] * block_decay[None]
    inputs_in = joined[:, None, None] * one_step[None] * last_row[:-1]

    def combine(earlier, later):
        return (earlier[0] * later[0], later[0] * earlier[1] + later[1])
    unused, states = lax.associative_scan(combine, (factors, inputs_in))
    carried = jnp.concatenate([jnp.zeros((1, pole_count, chan_count), source.dtype), states], axis=0)
    start_rows = (seg_rows == starts[:, None]).astype(source.dtype)
    carry_out = jnp.einsum('kmc,imc->kic', carried * coeff[None], falling, precision=lax.Precision.HIGHEST) * start_rows[:, :, None]
    result = (block_out + carry_out).reshape(length, chan_count)
    grad_part = lax.optimization_barrier(jnp.sum(partial_sum, axis=0)) + jnp.einsum('kmc,kmc->mc', weights, carried, precision=lax.Precision.HIGHEST)
    return (result, grad_part)

def reference(features, upstream, lengths, conv_taps, residues, log_rate, skip_gain):
    decay_rate = jnp.exp(log_rate)
    positions = jnp.arange(WINDOW_LEN, dtype=jnp.int32)
    zeros_rows = jnp.zeros((2, 3 * CHANNELS), jnp.float32)
    grad_list = []
    tap_total = jnp.zeros((3, 3 * CHANNELS), jnp.float32)
    resid_total = jnp.zeros((POLES, CHANNELS), jnp.float32)
    skip_total = jnp.zeros((CHANNELS,), jnp.float32)
    for window in range(WINDOWS):
        bounds = jnp.cumsum(lengths[window])[:-1]
        seg_ids, keep_one, keep_two, next_one, next_two = segment_masks(positions, bounds, WINDOW_LEN)
        source = features[window].astype(jnp.float32)
        featured = causal_taps(source, zeros_rows, conv_taps, keep_one, keep_two)
        query = featured[:, :CHANNELS]
        keys = featured[:, CHANNELS:2 * CHANNELS]
        values = featured[:, 2 * CHANNELS:]
        mixed = (keys * values).astype(jnp.bfloat16)
        mixedf = mixed.astype(jnp.float32)
        conv_out, unused = modal_sweep(mixedf, seg_ids, decay_rate, residues, jnp.zeros_like(mixedf))
        output = (conv_out + skip_gain * mixedf).astype(jnp.bfloat16)
        upf = upstream[window].astype(jnp.float32)
        grad_out = (upf * query).astype(jnp.bfloat16)
        gradf = grad_out.astype(jnp.float32)
        adjoint, grad_resid = modal_sweep(gradf[::-1], seg_ids[::-1], decay_rate, residues, mixedf[::-1])
        grad_mixed = (adjoint[::-1] + skip_gain * gradf).astype(jnp.bfloat16)
        dmixf = grad_mixed.astype(jnp.float32)
        resid_total = resid_total + grad_resid
        skip_total = skip_total + lax.optimization_barrier(jnp.sum(mixedf * gradf, axis=0))
        grad_post = jnp.concatenate([upf * output.astype(jnp.float32), dmixf * values, dmixf * keys], axis=1)
        grad_list.append(transposed_taps(grad_post, zeros_rows, conv_taps, next_one, next_two).astype(jnp.bfloat16))
        tap_total = tap_total + tap_terms(grad_post, source, zeros_rows, keep_one, keep_two)
    grad_scale = 1.0 / math.sqrt(WINDOWS * WINDOW_LEN)
    return (jnp.stack(grad_list), tap_total * grad_scale, resid_total * grad_scale, skip_total * grad_scale)
```

```python
import functools
import math

import jax
import jax.numpy as jnp
from jax import lax
from jax.experimental import pallas as pl
from jax.experimental.pallas import tpu as pltpu
from jax.sharding import PartitionSpec as P

MESH = pl.DeviceIdType.MESH
F32 = jnp.float32
BF16 = jnp.bfloat16
LANES = 128
SUBS = 8
GROUP = 4


def row_iota(rows):
    return lax.broadcasted_iota(jnp.int32, (rows, LANES), 0)


def lane_low(rows):
    return lax.broadcasted_iota(jnp.int32, (rows, LANES), 1) < LANES // 2


def swap_halves(x):
    return pltpu.roll(x, LANES // 2, 1)


def join_pair(low, high, first):
    mask = lane_low(low.shape[0])
    if first:
        return jnp.where(mask, low, swap_halves(high))
    return jnp.where(mask, swap_halves(low), high)


def split_pair(a, b):
    mask = lane_low(a.shape[0])
    return jnp.where(mask, a, swap_halves(b)), jnp.where(mask, swap_halves(a), b)


def free_of(bounds, low, high):
    clear = None
    for bound in bounds:
        one = (low > bound) | (high < bound)
        clear = one if clear is None else clear & one
    return jnp.where(clear, 1.0, 0.0).astype(F32)


def kernel(
    ctx,
    dp,
    scale,
    lengths,
    feats,
    upstream,
    taps,
    own,
    own_skip,
    grad_feats,
    grad_taps,
    grad_res,
    grad_skip,
    params,
    skips,
    halo,
    first_out,
    first_in,
    carry_out,
    carry_in,
    prefixes,
    joins,
    source,
    gradient,
    output,
    adjoint,
    decay,
    coeff,
    gain,
    state,
    costate,
    res_sum,
    skip_sum,
    masks,
    edge_out,
    edge_in,
    tail,
    tap_part,
    part_out,
    part_in,
    dp_out,
    dp_in,
    tap_out,
    tap_in,
    send_sem,
    recv_sem,
):
    rows, channels = upstream.shape
    poles = own.shape[0]
    groups = channels // LANES
    halves = groups // SUBS
    half_rows = rows * SUBS
    pole_rows = poles * SUBS
    steps = rows // SUBS
    window = rows * ctx
    me = lax.axis_index("ctx")
    my_dp = lax.axis_index("dp")

    def peer_of(o):
        return lax.rem(me + o, ctx)

    barrier = pltpu.get_barrier_semaphore()

    def greet(o, c):
        pl.semaphore_signal(barrier, inc=1, device_id={"ctx": peer_of(o)}, device_id_type=MESH)
        return c

    lax.fori_loop(1, ctx, greet, 0)

    def greet_dp(o, c):
        pl.semaphore_signal(barrier, inc=1, device_id={"dp": lax.rem(my_dp + o, dp)}, device_id_type=MESH)
        return c

    lax.fori_loop(1, dp, greet_dp, 0)
    pl.semaphore_wait(barrier, ctx - 1 + dp - 1)

    def remote(src, dst, k, to):
        return pltpu.make_async_remote_copy(
            src_ref=src, dst_ref=dst, send_sem=send_sem.at[k], recv_sem=recv_sem.at[k], device_id=to, device_id_type=MESH
        )

    halo_copy = remote(feats.at[pl.ds(rows - SUBS, SUBS)], halo, 0, {"ctx": peer_of(1)})
    halo_copy.start()

    def send_params(o, c):
        to = {"ctx": peer_of(o)}
        remote(own, params.at[me], 1, to).start()
        remote(own_skip, skips.at[me], 2, to).start()
        return c

    lax.fori_loop(1, ctx, send_params, 0)
    params[pl.ds(me, 1)] = own[...][None]
    skips[pl.ds(me, 1)] = own_skip[...][None]

    bounds = [0]
    total = 0
    for j in range(lengths.shape[1] - 1):
        total = total + lengths[0, j]
        bounds.append(total)
    bounds.append(window)
    start = me * rows
    pos = start + row_iota(rows)
    keep_one = free_of(bounds, pos, pos)
    keep_two = free_of(bounds, pos - 1, pos)
    next_one = free_of(bounds, pos + 1, pos + 1)
    next_two = free_of(bounds, pos + 1, pos + 2)
    masks[0] = keep_one
    masks[1] = keep_two
    masks[2] = next_one
    masks[3] = next_two
    masks[4] = free_of(bounds, pos + 1, start + rows - 1 + 0 * pos)
    masks[5] = free_of(bounds, start + 1 + 0 * pos, pos)
    row = row_iota(rows)
    masks[6] = jnp.where(row < rows - 1, next_one, 0.0)
    masks[7] = jnp.where(row < rows - 2, next_two, 0.0)

    low16 = lane_low(poles)

    def join_masks(k, c):
        low = jnp.where(low16, k * rows, (ctx - 1 - k) * rows + 1)
        joins[k] = free_of(bounds, low, low + (rows - 1))
        return c

    lax.fori_loop(0, ctx, join_masks, 0)

    halo_copy.wait()

    def shifted(off):
        f = feats[:, pl.ds(off, LANES)].astype(F32)
        ext = jnp.concatenate([halo[:, pl.ds(off, LANES)].astype(F32), f], axis=0)
        one = masks[0] * pltpu.roll(ext, 1, 0)[SUBS:]
        two = masks[1] * pltpu.roll(ext, 2, 0)[SUBS:]
        return f, one, two

    def featured(off, parts):
        lanes = pl.ds(off, LANES)
        return taps[0:1, lanes] * parts[0] + taps[1:2, lanes] * parts[1] + taps[2:3, lanes] * parts[2]

    def at(i, third):
        return pl.multiple_of(third * channels + i * LANES, LANES)

    def strided(i, count, stride_rows):
        return pl.ds(lax.div(i, SUBS) * stride_rows + lax.rem(i, SUBS), count, stride=SUBS)

    def enter(i, c):
        query = featured(at(i, 0), shifted(at(i, 0)))
        key = featured(at(i, 1), shifted(at(i, 1)))
        value = featured(at(i, 2), shifted(at(i, 2)))
        up = upstream[:, pl.ds(at(i, 0), LANES)].astype(F32)
        source[strided(i, rows, half_rows), :] = (key * value).astype(BF16).astype(F32)
        gradient[strided(i, rows, half_rows), :] = (up * query).astype(BF16).astype(F32)
        return c

    lax.fori_loop(0, groups, enter, 0)

    def wait_all(buf, k, slots):
        pltpu.make_async_copy(buf.at[pl.ds(0, slots)], buf.at[pl.ds(0, slots)], recv_sem.at[k]).wait()

    def wait_sent(buf, k, slots):
        pltpu.make_async_copy(buf.at[pl.ds(0, slots)], buf.at[pl.ds(0, slots)], send_sem.at[k]).wait()

    wait_all(params, 1, ctx - 1)
    wait_all(skips, 2, ctx - 1)

    def spread(i, c):
        low, high = params[2 * i], params[2 * i + 1]
        coeff[strided(i, poles, pole_rows), :] = join_pair(low, high, True)
        decay[strided(i, poles, pole_rows), :] = jnp.exp(-jnp.exp(join_pair(low, high, False)))
        low_s = jnp.broadcast_to(skips[2 * i], (SUBS, LANES))
        high_s = jnp.broadcast_to(skips[2 * i + 1], (SUBS, LANES))
        gain[pl.ds(i, 1), :] = join_pair(low_s, high_s, True)[0:1]
        return c

    lax.fori_loop(0, groups, spread, 0)

    def half_ends(h, c):
        pole_at = pl.ds(pl.multiple_of(h * pole_rows, SUBS), pole_rows)
        fac = decay[pole_at, :].reshape(poles, SUBS, LANES)

        def chunk(k, carry):
            s, u = carry
            back = steps - 1 - k
            x = source[pl.ds(pl.multiple_of(h * half_rows + k * 64, 64), 64), :].reshape(SUBS, SUBS, LANES)
            g = gradient[pl.ds(pl.multiple_of(h * half_rows + back * 64, 64), 64), :].reshape(SUBS, SUBS, LANES)
            mx = masks[4, pl.ds(pl.multiple_of(k * SUBS, SUBS), SUBS), :]
            mg = masks[5, pl.ds(pl.multiple_of(back * SUBS, SUBS), SUBS), :]
            for t in range(SUBS):
                r = SUBS - 1 - t
                s = s * fac + (x[t] * mx[t : t + 1])[None]
                u = u * fac + (g[r] * mg[r : r + 1])[None]
            return s, u

        zero = jnp.zeros((poles, SUBS, LANES), F32)
        s, u = lax.fori_loop(0, steps, chunk, (zero, zero))
        state[pole_at, :] = s.reshape(pole_rows, LANES)
        costate[pole_at, :] = u.reshape(pole_rows, LANES)
        return c

    lax.fori_loop(0, halves, half_ends, 0)

    def pack_first(i, c):
        a = state[strided(i, poles, pole_rows), :]
        b = costate[strided(i, poles, pole_rows), :]
        low, high = split_pair(a, b)
        first_out[2 * i] = low.astype(BF16)
        first_out[2 * i + 1] = high.astype(BF16)
        return c

    lax.fori_loop(0, groups, pack_first, 0)

    def exchange(out, into, k):
        def send(o, c):
            to = peer_of(o)
            remote(out.at[to], into.at[me], k, {"ctx": to}).start()
            return c

        lax.fori_loop(1, ctx, send, 0)
        into[pl.ds(me, 1)] = out[pl.ds(me, 1)]

    exchange(first_out, first_in, 3)
    wait_all(first_in, 3, ctx - 1)

    own_rate = jnp.where(low16, swap_halves(own[...]), own[...])
    block_decay = jnp.exp(-jnp.exp(own_rate) * rows)

    def scan(k, w):
        prefixes[k] = w
        here = jnp.where(low16, first_in[k].astype(F32), first_in[ctx - 1 - k].astype(F32))
        return joins[k] * block_decay * w + here

    lax.fori_loop(0, ctx, scan, jnp.zeros((poles, LANES), F32))

    def pack_carry(k, c):
        carry_out[k] = jnp.where(low16, prefixes[k], prefixes[ctx - 1 - k]).astype(BF16)
        return c

    lax.fori_loop(0, ctx, pack_carry, 0)
    exchange(carry_out, carry_in, 4)
    wait_all(carry_in, 4, ctx - 1)

    def unpack_carry(i, c):
        low, high = carry_in[2 * i].astype(F32), carry_in[2 * i + 1].astype(F32)
        state[strided(i, poles, pole_rows), :] = join_pair(low, high, True)
        costate[strided(i, poles, pole_rows), :] = join_pair(low, high, False)
        return c

    lax.fori_loop(0, groups, unpack_carry, 0)

    res_sum[...] = jnp.zeros_like(res_sum)
    skip_sum[...] = jnp.zeros_like(skip_sum)

    def half_sweep(h, c):
        skip = gain[pl.ds(pl.multiple_of(h * SUBS, SUBS), SUBS), :]

        def chunk(k, c):
            back = steps - 1 - k
            at_x = pl.ds(pl.multiple_of(h * half_rows + k * 64, 64), 64)
            at_g = pl.ds(pl.multiple_of(h * half_rows + back * 64, 64), 64)
            x = source[at_x, :].reshape(SUBS, SUBS, LANES)
            gx = gradient[at_x, :].reshape(SUBS, SUBS, LANES)
            g = gradient[at_g, :].reshape(SUBS, SUBS, LANES)
            keep = masks[0, pl.ds(pl.multiple_of(k * SUBS, SUBS), SUBS), :]
            keep_g = masks[2, pl.ds(pl.multiple_of(back * SUBS, SUBS), SUBS), :]
            out = [skip * x[t] for t in range(SUBS)]
            adj = [skip * g[t] for t in range(SUBS)]
            for p in range(0, poles, GROUP):
                here = pl.ds(pl.multiple_of(h * pole_rows + p * SUBS, SUBS), GROUP * SUBS)
                shape = (GROUP, SUBS, LANES)
                s = state[here, :].reshape(shape)
                u = costate[here, :].reshape(shape)
                fac = decay[here, :].reshape(shape)
                res = coeff[here, :].reshape(shape)
                acc = res_sum[here, :].reshape(shape)
                for t in range(SUBS):
                    r = SUBS - 1 - t
                    s = s * (fac * keep[t : t + 1][None]) + x[t][None]
                    out[t] = out[t] + jnp.sum(res * s, axis=0)
                    acc = acc + s * gx[t][None]
                    u = u * (fac * keep_g[r : r + 1][None]) + g[r][None]
                    adj[r] = adj[r] + jnp.sum(res * u, axis=0)
                state[here, :] = s.reshape(GROUP * SUBS, LANES)
                costate[here, :] = u.reshape(GROUP * SUBS, LANES)
                res_sum[here, :] = acc.reshape(GROUP * SUBS, LANES)
            output[at_x, :] = jnp.stack(out).reshape(SUBS * SUBS, LANES)
            adjoint[at_g, :] = jnp.stack(adj).reshape(SUBS * SUBS, LANES)
            both = pl.ds(pl.multiple_of(h * SUBS, SUBS), SUBS)
            skip_sum[both, :] = skip_sum[both, :] + jnp.sum(x * gx, axis=0)
            return c

        lax.fori_loop(0, steps, chunk, 0)
        return c

    lax.fori_loop(0, halves, half_sweep, 0)

    tap_part[...] = jnp.zeros_like(tap_part)

    def leave(i, c):
        out = output[strided(i, rows, half_rows), :].astype(BF16).astype(F32)
        mixed = adjoint[strided(i, rows, half_rows), :].astype(BF16).astype(F32)
        up = upstream[:, pl.ds(at(i, 0), LANES)].astype(F32)
        parts = [shifted(at(i, third)) for third in range(3)]
        key = featured(at(i, 1), parts[1])
        value = featured(at(i, 2), parts[2])
        here = pl.ds(at(i, 0), LANES)
        for third, post in enumerate((up * out, mixed * value, mixed * key)):
            lanes = pl.ds(at(i, third), LANES)
            for j in range(3):
                tap_part[third * 3 + j : third * 3 + j + 1, here] = jnp.sum(post * parts[third][j], axis=0, keepdims=True)
            edge_out[:, lanes] = post[0:2]
            back = (
                taps[0:1, lanes] * post
                + taps[1:2, lanes] * (masks[6] * pltpu.roll(post, rows - 1, 0))
                + taps[2:3, lanes] * (masks[7] * pltpu.roll(post, rows - 2, 0))
            )
            grad_feats[:, lanes] = back.astype(BF16)
            tail[:, lanes] = back[rows - 16 :]
        tap_part[9:10, here] = skip_sum[pl.ds(i, 1), :]
        return c

    lax.fori_loop(0, groups, leave, 0)
    edge_copy = remote(edge_out, edge_in, 5, {"ctx": peer_of(ctx - 1)})
    edge_copy.start()

    def pack_parts(i, c):
        a = res_sum[strided(i, poles, pole_rows), :]
        b = tap_part[:, pl.ds(at(i, 0), LANES)]
        low, high = split_pair(a, b)
        part_out[2 * i] = low
        part_out[2 * i + 1] = high
        return c

    lax.fori_loop(0, groups, pack_parts, 0)
    exchange(part_out, part_in, 6)

    edge_copy.wait()
    last = row_iota(16)
    one16, two16 = masks[2, rows - 16 :, :], masks[3, rows - 16 :, :]
    first_one = jnp.where(last == 15, one16, 0.0)
    first_two = jnp.where(last == 14, two16, 0.0)
    second_two = jnp.where(last == 15, two16, 0.0)

    def finish(i, c):
        lanes = pl.ds(pl.multiple_of(i * LANES, LANES), LANES)
        one, two = taps[1:2, lanes], taps[2:3, lanes]
        e0, e1 = edge_in[0:1, lanes], edge_in[1:2, lanes]
        done = tail[:, lanes] + (first_one * one + first_two * two) * e0 + (second_two * two) * e1
        grad_feats[rows - 16 :, lanes] = done.astype(BF16)
        return c

    lax.fori_loop(0, 3 * groups, finish, 0)

    wait_all(part_in, 6, ctx - 1)

    def add_parts(k, acc):
        return acc + part_in[k]

    dp_out[...] = lax.fori_loop(0, ctx, add_parts, jnp.zeros((poles, LANES), F32))

    def send_dp(o, c):
        remote(dp_out, dp_in.at[my_dp], 7, {"dp": lax.rem(my_dp + o, dp)}).start()
        return c

    lax.fori_loop(1, dp, send_dp, 0)
    dp_in[pl.ds(my_dp, 1)] = dp_out[...][None]
    wait_all(dp_in, 7, dp - 1)
    whole = dp_in[0]
    for k in range(1, dp):
        whole = whole + dp_in[k]
    whole = whole * scale
    grad_res[...] = whole[:, : LANES // 2]
    turned = swap_halves(whole)
    grad_skip[...] = turned[9:10, : LANES // 2]
    tap_out[...] = jnp.where(lane_low(SUBS), turned[0:8], whole[8:16])

    def send_taps(o, c):
        remote(tap_out, tap_in.at[me], 8, {"ctx": peer_of(o)}).start()
        return c

    lax.fori_loop(1, ctx, send_taps, 0)
    tap_in[pl.ds(me, 1)] = tap_out[...][None]
    wait_all(tap_in, 8, ctx - 1)

    def place_taps(i, c):
        low, high = tap_in[2 * i], tap_in[2 * i + 1]
        first = join_pair(low, high, True)
        last_row = join_pair(low, high, False)[0:1]
        for third in range(3):
            for j in range(3):
                r = third * 3 + j
                grad_taps[j : j + 1, pl.ds(at(i, third), LANES)] = first[r : r + 1] if r < 8 else last_row
        return c

    lax.fori_loop(0, groups, place_taps, 0)

    wait_sent(params, 1, ctx - 1)
    wait_sent(skips, 2, ctx - 1)
    wait_sent(first_in, 3, ctx - 1)
    wait_sent(carry_in, 4, ctx - 1)
    wait_sent(part_in, 6, ctx - 1)
    wait_sent(dp_in, 7, dp - 1)
    wait_sent(tap_in, 8, ctx - 1)


def per_device(features, upstream, lengths, conv_taps, residues, log_rate, skip_gain):
    rows, width = features.shape[1:]
    channels = upstream.shape[2]
    poles = residues.shape[0]
    ctx = lax.axis_size("ctx")
    dp = lax.axis_size("dp")
    scale = 1.0 / math.sqrt(rows * ctx * dp)
    groups = channels // LANES
    own = jnp.concatenate([residues, log_rate], axis=1)
    own_skip = jnp.concatenate([skip_gain, skip_gain])[None]
    vmem = pl.BlockSpec(memory_space=pltpu.VMEM)
    smem = pl.BlockSpec(memory_space=pltpu.SMEM)
    slab = (ctx, poles, LANES)
    wide = pltpu.VMEM((rows * groups, LANES), F32)
    per_pole = pltpu.VMEM((poles * groups, LANES), F32)
    scratch = [
        pltpu.VMEM(slab, F32),
        pltpu.VMEM((ctx, 1, LANES), F32),
        pltpu.VMEM((SUBS, width), BF16),
        pltpu.VMEM(slab, BF16),
        pltpu.VMEM(slab, BF16),
        pltpu.VMEM(slab, BF16),
        pltpu.VMEM(slab, BF16),
        pltpu.VMEM(slab, F32),
        pltpu.VMEM(slab, F32),
        wide,
        wide,
        wide,
        wide,
        per_pole,
        per_pole,
        pltpu.VMEM((groups, LANES), F32),
        per_pole,
        per_pole,
        per_pole,
        pltpu.VMEM((groups, LANES), F32),
        pltpu.VMEM((8, rows, LANES), F32),
        pltpu.VMEM((2, width), F32),
        pltpu.VMEM((2, width), F32),
        pltpu.VMEM((16, width), F32),
        pltpu.VMEM((16, channels), F32),
        pltpu.VMEM(slab, F32),
        pltpu.VMEM(slab, F32),
        pltpu.VMEM((poles, LANES), F32),
        pltpu.VMEM((dp, poles, LANES), F32),
        pltpu.VMEM((SUBS, LANES), F32),
        pltpu.VMEM((ctx, SUBS, LANES), F32),
        pltpu.SemaphoreType.DMA((9,)),
        pltpu.SemaphoreType.DMA((9,)),
    ]
    grad_feats, grad_taps, grad_res, grad_skip = pl.pallas_call(
        functools.partial(kernel, ctx, dp, scale),
        out_shape=(
            jax.ShapeDtypeStruct((rows, width), BF16),
            jax.ShapeDtypeStruct((3, width), F32),
            jax.ShapeDtypeStruct(residues.shape, F32),
            jax.ShapeDtypeStruct((1, residues.shape[1]), F32),
        ),
        in_specs=[smem] + [vmem] * 5,
        out_specs=(vmem,) * 4,
        scratch_shapes=scratch,
        compiler_params=pltpu.CompilerParams(
            collective_id=0, has_side_effects=True, vmem_limit_bytes=48 * 1024 * 1024
        ),
        name="conv_block",
    )(lengths, features[0], upstream[0], conv_taps, own, own_skip)
    return (grad_feats[None], grad_taps, grad_res, grad_skip[0])


def solution(mesh):
    return jax.shard_map(
        per_device,
        mesh=mesh,
        in_specs=(
            P("dp", "ctx", None),
            P("dp", "ctx", None),
            P("dp", None),
            P(),
            P(None, "ctx"),
            P(None, "ctx"),
            P("ctx"),
        ),
        out_specs=(P("dp", "ctx", None), P(), P(None, "ctx"), P("ctx")),
        check_vma=False,
    )
```

```python
import functools
import math

import jax
import jax.numpy as jnp
from jax import lax
from jax.experimental import pallas as pl
from jax.experimental.pallas import tpu as pltpu
from jax.sharding import PartitionSpec as P

MESH = pl.DeviceIdType.MESH
F32 = jnp.float32
BF16 = jnp.bfloat16
LANES = 128
SUBS = 8
GROUP = 4
NEAR = 4


def row_iota(rows):
    return lax.broadcasted_iota(jnp.int32, (rows, LANES), 0)


def lane_low(rows):
    return lax.broadcasted_iota(jnp.int32, (rows, LANES), 1) < LANES // 2


def swap_halves(x):
    return pltpu.roll(x, LANES // 2, 1)


def join_pair(low, high, first):
    mask = lane_low(low.shape[0])
    if first:
        return jnp.where(mask, low, swap_halves(high))
    return jnp.where(mask, swap_halves(low), high)


def split_pair(a, b):
    mask = lane_low(a.shape[0])
    return jnp.where(mask, a, swap_halves(b)), jnp.where(mask, swap_halves(a), b)


def unfold(low, high):
    return jnp.concatenate([join_pair(low, high, True), join_pair(low, high, False)], axis=0)


def fold(x):
    return jnp.where(lane_low(SUBS), x[:SUBS], swap_halves(x[SUBS:]))


def free_of(bounds, low, high):
    clear = None
    for bound in bounds:
        one = (low > bound) | (high < bound)
        clear = one if clear is None else clear & one
    return jnp.where(clear, 1.0, 0.0).astype(F32)


def kernel(
    ctx,
    dp,
    scale,
    lengths,
    feats_in,
    upstream_in,
    taps_in,
    res_in,
    rate_in,
    skip_in,
    grad_feats,
    grad_taps,
    grad_res,
    grad_skip,
    feats,
    upstream,
    taps,
    own_res,
    own_rate,
    own_skip,
    rate_out,
    res_out,
    skip_out,
    rates,
    residues,
    skips,
    halo,
    first_out,
    first_in,
    carry_out,
    carry_in,
    prefixes,
    joins,
    keeps,
    source,
    gradient,
    output,
    adjoint,
    keys,
    values,
    decay,
    coeff,
    powers,
    gain,
    state,
    costate,
    res_sum,
    skip_sum,
    masks,
    edge_out,
    edge_in,
    tail,
    res_part_out,
    res_part_in,
    res_dp_out,
    res_dp_in,
    part_out,
    part_in,
    dp_out,
    dp_in,
    tap_out,
    tap_in,
    load_sem,
    send_sem,
    recv_sem,
):
    rows, channels = upstream.shape
    poles = own_res.shape[0]
    groups = channels // LANES
    halves = groups // SUBS
    half_rows = rows * SUBS
    pole_rows = poles * SUBS
    steps = rows // SUBS
    window = rows * ctx
    me = lax.axis_index("ctx")
    my_dp = lax.axis_index("dp")

    def peer_of(o):
        return lax.rem(me + o, ctx)

    def dp_peer(o):
        return lax.rem(my_dp + o, dp)

    loads = [
        pltpu.make_async_copy(src, dst, load_sem.at[k])
        for k, (src, dst) in enumerate(
            [
                (rate_in, own_rate),
                (res_in, own_res),
                (skip_in, own_skip),
                (taps_in, taps),
                (feats_in, feats),
                (upstream_in, upstream),
            ]
        )
    ]
    for load in loads:
        load.start()
    barrier = pltpu.get_barrier_semaphore()

    def greet(o, c):
        pl.semaphore_signal(barrier, inc=1, device_id={"ctx": peer_of(o)}, device_id_type=MESH)
        return c

    lax.fori_loop(1, ctx, greet, 0)

    def greet_dp(o, c):
        pl.semaphore_signal(barrier, inc=1, device_id={"dp": dp_peer(o)}, device_id_type=MESH)
        return c

    lax.fori_loop(1, dp, greet_dp, 0)

    for load in loads[:3]:
        load.wait()
    rate_out[...] = jnp.concatenate([own_rate[:SUBS, :], own_rate[SUBS:, :]], axis=1)
    res_out[...] = jnp.concatenate([own_res[:SUBS, :], own_res[SUBS:, :]], axis=1)
    skip_out[...] = jnp.concatenate([own_skip[...], own_skip[...]], axis=1)

    bounds = [0]
    total = 0
    for j in range(lengths.shape[1] - 1):
        total = total + lengths[0, j]
        bounds.append(total)
    bounds.append(window)
    start = me * rows
    row = row_iota(rows)
    pos = start + row
    flat = 0 * row
    next_one = free_of(bounds, pos + 1, pos + 1)
    next_two = free_of(bounds, pos + 1, pos + 2)
    masks[0] = free_of(bounds, pos, pos)
    masks[1] = free_of(bounds, pos - 1, pos)
    masks[2] = next_one
    masks[3] = next_two

    pl.semaphore_wait(barrier, ctx - 1 + dp - 1)

    def remote(src, dst, k, to):
        return pltpu.make_async_remote_copy(
            src_ref=src, dst_ref=dst, send_sem=send_sem.at[k], recv_sem=recv_sem.at[k], device_id=to, device_id_type=MESH
        )

    halo_copy = remote(feats_in.at[pl.ds(rows - SUBS, SUBS)], halo, 0, {"ctx": peer_of(1)})
    halo_copy.start()

    def send_rates(o, c):
        remote(rate_out, rates.at[me], 1, {"ctx": peer_of(o)}).start()
        return c

    lax.fori_loop(1, ctx, send_rates, 0)

    def send_others(o, c):
        remote(res_out, residues.at[me], 2, {"ctx": peer_of(o)}).start()
        remote(skip_out, skips.at[me], 3, {"ctx": peer_of(o)}).start()
        return c

    lax.fori_loop(1, ctx, send_others, 0)
    rates[pl.ds(me, 1)] = rate_out[...][None]
    residues[pl.ds(me, 1)] = res_out[...][None]
    skips[pl.ds(me, 1)] = skip_out[...][None]

    masks[4] = free_of(bounds, pos + 1, flat + (start + rows - 1))
    masks[5] = free_of(bounds, flat + (start + 1), pos)
    masks[6] = jnp.where(row < rows - 1, next_one, 0.0)
    masks[7] = jnp.where(row < rows - 2, next_two, 0.0)
    masks[8] = free_of(bounds, flat + start, pos)
    masks[9] = free_of(bounds, pos + 1, flat + (start + rows))

    low16 = lane_low(poles)
    my_rate = jnp.concatenate([own_rate[...], own_rate[...]], axis=1)
    my_decay = jnp.exp(-jnp.exp(my_rate))
    block_decay = jnp.exp(-jnp.exp(my_rate) * rows)

    def join_masks(k, c):
        low = jnp.where(low16, k * rows, (ctx - 1 - k) * rows + 1)
        joins[k] = free_of(bounds, low, low + (rows - 1)) * block_decay
        keeps[k] = free_of(bounds, low, low) * my_decay
        return c

    lax.fori_loop(0, ctx, join_masks, 0)

    my_y, my_z = lax.div(me, 2 * NEAR), lax.rem(lax.div(me, 2), NEAR)

    def group_of(s):
        b, t = lax.div(s, NEAR), lax.rem(s, NEAR)
        upper = lax.div(b, 2)
        z_off = (1 - upper) * (b + 2) + upper * (3 - b)
        y = lax.rem(my_y + t + 2, NEAR)
        return y * NEAR + lax.rem(my_z + z_off, NEAR)

    def at(i, third):
        return pl.multiple_of(third * channels + i * LANES, LANES)

    def strided(s, count, stride_rows):
        return pl.ds(lax.div(s, SUBS) * stride_rows + lax.rem(s, SUBS), count, stride=SUBS)

    for load in loads[3:]:
        load.wait()
    halo_copy.wait()

    def featured(off):
        lanes = pl.ds(off, LANES)
        f = feats[:, lanes].astype(F32)
        ext = jnp.concatenate([halo[:, lanes].astype(F32), f], axis=0)
        one = masks[0] * pltpu.roll(ext, 1, 0)[SUBS:]
        two = masks[1] * pltpu.roll(ext, 2, 0)[SUBS:]
        return taps[0:1, lanes] * f + taps[1:2, lanes] * one + taps[2:3, lanes] * two

    def enter(s, c):
        i = group_of(s)
        query, key, value = (featured(at(i, third)) for third in range(3))
        lanes = pl.ds(at(i, 0), LANES)
        up = upstream[:, lanes].astype(F32)
        keys[:, lanes] = key
        values[:, lanes] = value
        source[strided(s, rows, half_rows), :] = (key * value).astype(BF16).astype(F32)
        gradient[strided(s, rows, half_rows), :] = (up * query).astype(BF16).astype(F32)
        return c

    lax.fori_loop(0, groups, enter, 0)

    def all_slots(buf, sem, slots):
        pltpu.make_async_copy(buf.at[pl.ds(0, slots)], buf.at[pl.ds(0, slots)], sem).wait()

    def wait_all(buf, k, slots):
        all_slots(buf, recv_sem.at[k], slots)

    wait_all(rates, 1, ctx - 1)

    def spread_rates(s, c):
        i = group_of(s)
        decay[strided(s, poles, pole_rows), :] = jnp.exp(-jnp.exp(unfold(rates[2 * i], rates[2 * i + 1])))
        return c

    lax.fori_loop(0, groups, spread_rates, 0, unroll=True)

    def send_slab(out, into, k, to):
        @pl.when(to != me)
        def _():
            remote(out.at[to], into.at[me], k, {"ctx": to}).start()

        @pl.when(to == me)
        def _():
            into[pl.ds(me, 1)] = out[pl.ds(me, 1)]

    def send_slots(out, into, k, low, high):
        def send(s, c):
            i = group_of(s)
            send_slab(out, into, k, 2 * i)
            send_slab(out, into, k, 2 * i + 1)
            return c

        lax.fori_loop(low, high, send, 0)

    for h in range(halves):
        pole_at = pl.ds(h * pole_rows, pole_rows)
        fac = decay[pole_at, :].reshape(poles, SUBS, LANES)

        def chunk(k, carry):
            s, u = carry
            back = steps - 1 - k
            x = source[pl.ds(pl.multiple_of(h * half_rows + k * 64, 64), 64), :].reshape(SUBS, SUBS, LANES)
            g = gradient[pl.ds(pl.multiple_of(h * half_rows + back * 64, 64), 64), :].reshape(SUBS, SUBS, LANES)
            mx = masks[4, pl.ds(pl.multiple_of(k * SUBS, SUBS), SUBS), :]
            mg = masks[5, pl.ds(pl.multiple_of(back * SUBS, SUBS), SUBS), :]
            for t in range(SUBS):
                r = SUBS - 1 - t
                s = s * fac + (x[t] * mx[t : t + 1])[None]
                u = u * fac + (g[r] * mg[r : r + 1])[None]
            return s, u

        zero = jnp.zeros((poles, SUBS, LANES), F32)
        s, u = lax.fori_loop(0, steps, chunk, (zero, zero))
        state[pole_at, :] = s.reshape(pole_rows, LANES)
        costate[pole_at, :] = u.reshape(pole_rows, LANES)

        def pack_first(s, c):
            i = group_of(s)
            low, high = split_pair(state[strided(s, poles, pole_rows), :], costate[strided(s, poles, pole_rows), :])
            first_out[2 * i] = low.astype(BF16)
            first_out[2 * i + 1] = high.astype(BF16)
            return c

        lax.fori_loop(h * SUBS, (h + 1) * SUBS, pack_first, 0, unroll=True)
        send_slots(first_out, first_in, 4, h * SUBS, (h + 1) * SUBS)

    wait_all(residues, 2, ctx - 1)
    wait_all(skips, 3, ctx - 1)

    def spread_others(s, c):
        i = group_of(s)
        coeff[strided(s, poles, pole_rows), :] = unfold(residues[2 * i], residues[2 * i + 1])
        low_s = jnp.broadcast_to(skips[2 * i], (SUBS, LANES))
        high_s = jnp.broadcast_to(skips[2 * i + 1], (SUBS, LANES))
        gain[pl.ds(s, 1), :] = join_pair(low_s, high_s, True)[0:1]
        return c

    lax.fori_loop(0, groups, spread_others, 0, unroll=True)
    state[...] = jnp.zeros_like(state)
    costate[...] = jnp.zeros_like(costate)
    res_sum[...] = jnp.zeros_like(res_sum)
    skip_sum[...] = jnp.zeros_like(skip_sum)

    def raise_powers(h):
        pole_at = pl.ds(h * pole_rows, pole_rows)
        fac = decay[pole_at, :].reshape(poles, SUBS, LANES)

        def step(k, e):
            for t in range(4):
                e = e * fac
                to = pl.multiple_of((h * rows + k * 4 + t) * pole_rows, pole_rows)
                powers[pl.ds(to, pole_rows), :] = e.reshape(pole_rows, LANES)
            return e

        lax.fori_loop(0, rows // 4, step, coeff[pole_at, :].reshape(poles, SUBS, LANES))

    def half_sweep(h):
        both = pl.ds(h * SUBS, SUBS)
        skip = gain[both, :]

        def chunk(k, c):
            back = steps - 1 - k
            at_x = pl.ds(pl.multiple_of(h * half_rows + k * 64, 64), 64)
            at_g = pl.ds(pl.multiple_of(h * half_rows + back * 64, 64), 64)
            x = source[at_x, :].reshape(SUBS, SUBS, LANES)
            gx = gradient[at_x, :].reshape(SUBS, SUBS, LANES)
            g = gradient[at_g, :].reshape(SUBS, SUBS, LANES)
            keep = masks[0, pl.ds(pl.multiple_of(k * SUBS, SUBS), SUBS), :]
            keep_g = masks[2, pl.ds(pl.multiple_of(back * SUBS, SUBS), SUBS), :]
            out = [skip * x[t] for t in range(SUBS)]
            adj = [skip * g[t] for t in range(SUBS)]
            for p in range(0, poles, GROUP):
                here = pl.ds(h * pole_rows + p * SUBS, GROUP * SUBS)
                shape = (GROUP, SUBS, LANES)
                s = state[here, :].reshape(shape)
                u = costate[here, :].reshape(shape)
                fac = decay[here, :].reshape(shape)
                res = coeff[here, :].reshape(shape)
                acc = res_sum[here, :].reshape(shape)
                for t in range(SUBS):
                    r = SUBS - 1 - t
                    s = s * (fac * keep[t : t + 1][None]) + x[t][None]
                    out[t] = out[t] + jnp.sum(res * s, axis=0)
                    acc = acc + s * gx[t][None]
                    u = u * (fac * keep_g[r : r + 1][None]) + g[r][None]
                    adj[r] = adj[r] + jnp.sum(res * u, axis=0)
                state[here, :] = s.reshape(GROUP * SUBS, LANES)
                costate[here, :] = u.reshape(GROUP * SUBS, LANES)
                res_sum[here, :] = acc.reshape(GROUP * SUBS, LANES)
            output[at_x, :] = jnp.stack(out).reshape(SUBS * SUBS, LANES)
            adjoint[at_g, :] = jnp.stack(adj).reshape(SUBS * SUBS, LANES)
            skip_sum[both, :] = skip_sum[both, :] + jnp.sum(x * gx, axis=0)
            return c

        lax.fori_loop(0, steps, chunk, 0)

    raise_powers(0)
    half_sweep(0)

    wait_all(first_in, 4, ctx - 1)

    def scan(k, w):
        prefixes[k] = w
        here = jnp.where(low16, first_in[k].astype(F32), first_in[ctx - 1 - k].astype(F32))
        return joins[k] * w + here

    lax.fori_loop(0, ctx, scan, jnp.zeros((poles, LANES), F32), unroll=True)

    def pack_carry(k, c):
        carry_out[k] = jnp.where(low16, prefixes[k], prefixes[ctx - 1 - k]).astype(BF16)
        return c

    lax.fori_loop(0, ctx, pack_carry, 0, unroll=True)
    send_slots(carry_out, carry_in, 5, 0, groups)

    raise_powers(1)
    half_sweep(1)

    def pack_res(s, c):
        i = group_of(s)
        a = res_sum[strided(s, poles, pole_rows), :]
        low, high = split_pair(a[:SUBS], a[SUBS:])
        res_part_out[2 * i] = low
        res_part_out[2 * i + 1] = high
        return c

    lax.fori_loop(0, groups, pack_res, 0, unroll=True)
    send_slots(res_part_out, res_part_in, 6, 0, groups)

    def carried_terms(k, acc):
        return acc + keeps[k] * prefixes[k] * swap_halves(first_in[k].astype(F32))

    res_carried = fold(lax.fori_loop(0, ctx, carried_terms, jnp.zeros((poles, LANES), F32)))

    wait_all(carry_in, 5, ctx - 1)

    def unpack_carry(s, c):
        i = group_of(s)
        low, high = carry_in[2 * i].astype(F32), carry_in[2 * i + 1].astype(F32)
        state[strided(s, poles, pole_rows), :] = join_pair(low, high, True)
        costate[strided(s, poles, pole_rows), :] = join_pair(low, high, False)
        return c

    lax.fori_loop(0, groups, unpack_carry, 0, unroll=True)

    for h in range(halves):
        pole_at = pl.ds(h * pole_rows, pole_rows)
        s = state[pole_at, :].reshape(poles, SUBS, LANES)
        u = costate[pole_at, :].reshape(poles, SUBS, LANES)

        def add_carry(k, c):
            for j in range(4):
                t = k * 4 + j
                r = rows - 1 - t
                e = powers[pl.ds(pl.multiple_of((h * rows + t) * pole_rows, pole_rows), pole_rows), :]
                e = e.reshape(poles, SUBS, LANES)
                at_t = pl.ds(pl.multiple_of(h * half_rows + t * SUBS, SUBS), SUBS)
                at_r = pl.ds(pl.multiple_of(h * half_rows + r * SUBS, SUBS), SUBS)
                output[at_t, :] = output[at_t, :] + masks[8, pl.ds(t, 1), :] * jnp.sum(e * s, axis=0)
                adjoint[at_r, :] = adjoint[at_r, :] + masks[9, pl.ds(r, 1), :] * jnp.sum(e * u, axis=0)
            return c

        lax.fori_loop(0, rows // 4, add_carry, 0)

    first_keep, first_both, second_both = masks[0, 0:1, :], masks[1, 0:1, :], masks[1, 1:2, :]

    def leave(s, c):
        i = group_of(s)
        here = pl.ds(at(i, 0), LANES)
        out = output[strided(s, rows, half_rows), :].astype(BF16).astype(F32)
        mixed = adjoint[strided(s, rows, half_rows), :].astype(BF16).astype(F32)
        up = upstream[:, here].astype(F32)
        sums = []
        for third, post in enumerate((up * out, mixed * values[:, here], mixed * keys[:, here])):
            lanes = pl.ds(at(i, third), LANES)
            f = feats[:, lanes].astype(F32)
            before = halo[:, lanes].astype(F32)
            one = masks[6] * pltpu.roll(post, rows - 1, 0)
            two = masks[7] * pltpu.roll(post, rows - 2, 0)
            p0, p1 = post[0:1], post[1:2]
            h1, h2 = before[SUBS - 1 :], before[SUBS - 2 : SUBS - 1]
            sums.append(jnp.sum(post * f, axis=0, keepdims=True))
            sums.append(jnp.sum(one * f, axis=0, keepdims=True) + p0 * first_keep * h1)
            sums.append(jnp.sum(two * f, axis=0, keepdims=True) + p0 * first_both * h2 + p1 * second_both * h1)
            edge_out[:, lanes] = post[0:2]
            back = taps[0:1, lanes] * post + taps[1:2, lanes] * one + taps[2:3, lanes] * two
            grad_feats[:, lanes] = back.astype(BF16)
            tail[:, lanes] = back[rows - 16 :]
        top = jnp.concatenate(sums[:SUBS], axis=0)
        rest = jnp.concatenate([sums[SUBS], skip_sum[pl.ds(s, 1), :]] + sums[:6], axis=0)
        low, high = split_pair(top, rest)
        part_out[2 * i] = low
        part_out[2 * i + 1] = high

        @pl.when(s > 0)
        def _():
            j = group_of(s - 1)
            send_slab(part_out, part_in, 9, 2 * j)
            send_slab(part_out, part_in, 9, 2 * j + 1)

        return c

    lax.fori_loop(0, groups, leave, 0)
    edge_copy = remote(edge_out, edge_in, 8, {"ctx": peer_of(ctx - 1)})
    edge_copy.start()
    send_slots(part_out, part_in, 9, groups - 1, groups)

    def sum_slots(buf, count):
        return lax.fori_loop(0, count, lambda k, acc: acc + buf[k], jnp.zeros((SUBS, LANES), F32), unroll=True)

    wait_all(res_part_in, 6, ctx - 1)
    res_dp_out[...] = sum_slots(res_part_in, ctx) + res_carried

    def send_res(o, c):
        remote(res_dp_out, res_dp_in.at[my_dp], 7, {"dp": dp_peer(o)}).start()
        return c

    lax.fori_loop(1, dp, send_res, 0)
    res_dp_in[pl.ds(my_dp, 1)] = res_dp_out[...][None]

    edge_copy.wait()
    last = row_iota(16)
    one16, two16 = masks[2, rows - 16 :, :], masks[3, rows - 16 :, :]
    first_one = jnp.where(last == 15, one16, 0.0)
    first_two = jnp.where(last == 14, two16, 0.0)
    second_two = jnp.where(last == 15, two16, 0.0)

    def finish(i, c):
        lanes = pl.ds(pl.multiple_of(i * LANES, LANES), LANES)
        one, two = taps[1:2, lanes], taps[2:3, lanes]
        e0, e1 = edge_in[0:1, lanes], edge_in[1:2, lanes]
        done = tail[:, lanes] + (first_one * one + first_two * two) * e0 + (second_two * two) * e1
        grad_feats[rows - 16 :, lanes] = done.astype(BF16)
        return c

    wait_all(part_in, 9, ctx - 1)
    dp_out[...] = sum_slots(part_in, ctx)

    def send_dp(o, c):
        remote(dp_out, dp_in.at[my_dp], 10, {"dp": dp_peer(o)}).start()
        return c

    lax.fori_loop(1, dp, send_dp, 0)
    dp_in[pl.ds(my_dp, 1)] = dp_out[...][None]
    wait_all(dp_in, 10, dp - 1)
    whole = sum_slots(dp_in, dp) * scale
    tap_out[...] = whole

    def send_taps(o, c):
        remote(tap_out, tap_in.at[me], 11, {"ctx": peer_of(o)}).start()
        return c

    lax.fori_loop(1, ctx, send_taps, 0)
    tap_in[pl.ds(me, 1)] = whole[None]
    grad_skip[...] = swap_halves(whole)[1:2, : LANES // 2]

    lax.fori_loop(0, 3 * groups, finish, 0)
    wait_all(res_dp_in, 7, dp - 1)
    res_whole = sum_slots(res_dp_in, dp) * scale
    grad_res[:SUBS, :] = res_whole[:, : LANES // 2]
    grad_res[SUBS:, :] = swap_halves(res_whole)[:, : LANES // 2]
    for k, buf, slots in [
        (1, rates, ctx),
        (2, residues, ctx),
        (3, skips, ctx),
        (4, first_in, ctx),
        (5, carry_in, ctx),
        (6, res_part_in, ctx),
        (7, res_dp_in, dp),
        (9, part_in, ctx),
        (10, dp_in, dp),
        (11, tap_in, ctx),
    ]:
        all_slots(buf, send_sem.at[k], slots - 1)

    wait_all(tap_in, 11, ctx - 1)

    def place_taps(i, c):
        low, high = tap_in[2 * i], tap_in[2 * i + 1]
        first = join_pair(low, high, True)
        last_row = join_pair(low, high, False)[0:1]
        for third in range(3):
            for j in range(3):
                r = third * 3 + j
                grad_taps[j : j + 1, pl.ds(at(i, third), LANES)] = first[r : r + 1] if r < SUBS else last_row
        return c

    lax.fori_loop(0, groups, place_taps, 0, unroll=True)


def per_device(features, upstream, lengths, conv_taps, residues, log_rate, skip_gain):
    rows, width = features.shape[1:]
    channels = upstream.shape[2]
    poles, owned = residues.shape
    ctx = lax.axis_size("ctx")
    dp = lax.axis_size("dp")
    scale = 1.0 / math.sqrt(rows * ctx * dp)
    groups = channels // LANES
    vmem = pl.BlockSpec(memory_space=pltpu.VMEM)
    smem = pl.BlockSpec(memory_space=pltpu.SMEM)
    hbm = pl.BlockSpec(memory_space=pltpu.HBM)
    slab = (ctx, poles, LANES)
    folded = (ctx, SUBS, LANES)
    wide = pltpu.VMEM((rows * groups, LANES), F32)
    per_pole = pltpu.VMEM((poles * groups, LANES), F32)
    scratch = [
        pltpu.VMEM((rows, width), BF16),
        pltpu.VMEM((rows, channels), BF16),
        pltpu.VMEM((3, width), F32),
        pltpu.VMEM((poles, owned), F32),
        pltpu.VMEM((poles, owned), F32),
        pltpu.VMEM((1, owned), F32),
        pltpu.VMEM((SUBS, LANES), F32),
        pltpu.VMEM((SUBS, LANES), F32),
        pltpu.VMEM((1, LANES), F32),
        pltpu.VMEM(folded, F32),
        pltpu.VMEM(folded, F32),
        pltpu.VMEM((ctx, 1, LANES), F32),
        pltpu.VMEM((SUBS, width), BF16),
        pltpu.VMEM(slab, BF16),
        pltpu.VMEM(slab, BF16),
        pltpu.VMEM(slab, BF16),
        pltpu.VMEM(slab, BF16),
        pltpu.VMEM(slab, F32),
        pltpu.VMEM(slab, F32),
        pltpu.VMEM(slab, F32),
        wide,
        wide,
        wide,
        wide,
        pltpu.VMEM((rows, channels), F32),
        pltpu.VMEM((rows, channels), F32),
        per_pole,
        per_pole,
        pltpu.VMEM((rows * poles * groups, LANES), F32),
        pltpu.VMEM((groups, LANES), F32),
        per_pole,
        per_pole,
        per_pole,
        pltpu.VMEM((groups, LANES), F32),
        pltpu.VMEM((10, rows, LANES), F32),
        pltpu.VMEM((2, width), F32),
        pltpu.VMEM((2, width), F32),
        pltpu.VMEM((16, width), F32),
        pltpu.VMEM(folded, F32),
        pltpu.VMEM(folded, F32),
        pltpu.VMEM((SUBS, LANES), F32),
        pltpu.VMEM((dp, SUBS, LANES), F32),
        pltpu.VMEM(folded, F32),
        pltpu.VMEM(folded, F32),
        pltpu.VMEM((SUBS, LANES), F32),
        pltpu.VMEM((dp, SUBS, LANES), F32),
        pltpu.VMEM((SUBS, LANES), F32),
        pltpu.VMEM(folded, F32),
        pltpu.SemaphoreType.DMA((6,)),
        pltpu.SemaphoreType.DMA((12,)),
        pltpu.SemaphoreType.DMA((12,)),
    ]
    grad_feats, grad_taps, grad_res, grad_skip = pl.pallas_call(
        functools.partial(kernel, ctx, dp, scale),
        out_shape=(
            jax.ShapeDtypeStruct((rows, width), BF16),
            jax.ShapeDtypeStruct((3, width), F32),
            jax.ShapeDtypeStruct((poles, owned), F32),
            jax.ShapeDtypeStruct((1, owned), F32),
        ),
        in_specs=[smem] + [hbm] * 6,
        out_specs=(vmem,) * 4,
        scratch_shapes=scratch,
        compiler_params=pltpu.CompilerParams(
            collective_id=0, has_side_effects=True, vmem_limit_bytes=56 * 1024 * 1024
        ),
        name="conv_block",
    )(lengths, features[0], upstream[0], conv_taps, residues, log_rate, skip_gain[None])
    return (grad_feats[None], grad_taps, grad_res, grad_skip[0])


def solution(mesh):
    return jax.shard_map(
        per_device,
        mesh=mesh,
        in_specs=(
            P("dp", "ctx", None),
            P("dp", "ctx", None),
            P("dp", None),
            P(),
            P(None, "ctx"),
            P(None, "ctx"),
            P("ctx"),
        ),
        out_specs=(P("dp", "ctx", None), P(), P(None, "ctx"), P("ctx")),
        check_vma=False,
    )
```

```python
import functools
import math

import jax
import jax.numpy as jnp
from jax import lax
from jax.experimental import pallas as pl
from jax.experimental.pallas import tpu as pltpu
from jax.sharding import PartitionSpec as P

MESH = pl.DeviceIdType.MESH
F32 = jnp.float32
BF16 = jnp.bfloat16
LANES = 128
SUBS = 8
GROUP = 4
NEAR = 4


def row_iota(rows):
    return lax.broadcasted_iota(jnp.int32, (rows, LANES), 0)


def lane_low(rows):
    return lax.broadcasted_iota(jnp.int32, (rows, LANES), 1) < LANES // 2


def swap_halves(x):
    return pltpu.roll(x, LANES // 2, 1)


def join_pair(low, high, first):
    mask = lane_low(low.shape[0])
    if first:
        return jnp.where(mask, low, swap_halves(high))
    return jnp.where(mask, swap_halves(low), high)


def split_pair(a, b):
    mask = lane_low(a.shape[0])
    return jnp.where(mask, a, swap_halves(b)), jnp.where(mask, swap_halves(a), b)


def unfold(low, high):
    return jnp.concatenate([join_pair(low, high, True), join_pair(low, high, False)], axis=0)


def fold(x):
    return jnp.where(lane_low(SUBS), x[:SUBS], swap_halves(x[SUBS:]))


def free_of(bounds, low, high):
    clear = None
    for bound in bounds:
        one = (low > bound) | (high < bound)
        clear = one if clear is None else clear & one
    return jnp.where(clear, 1.0, 0.0).astype(F32)


def kernel(
    ctx,
    dp,
    scale,
    lengths,
    feats_in,
    upstream_in,
    taps_in,
    res_in,
    rate_in,
    skip_in,
    grad_feats,
    grad_taps,
    grad_res,
    grad_skip,
    feats,
    upstream,
    taps,
    own_res,
    own_rate,
    own_skip,
    rate_out,
    res_out,
    skip_out,
    rates,
    residues,
    skips,
    halo_out,
    halo,
    first_out,
    first_in,
    carry_out,
    carry_in,
    prefixes,
    joins,
    keeps,
    source,
    gradient,
    output,
    adjoint,
    queries,
    keys,
    values,
    decay,
    coeff,
    powers,
    gain,
    state,
    costate,
    res_sum,
    skip_sum,
    masks,
    edge_out,
    edge_in,
    tail,
    res_part_out,
    res_part_in,
    res_dp_out,
    res_dp_in,
    part_out,
    part_in,
    dp_out,
    dp_in,
    tap_out,
    tap_in,
    load_sem,
    send_sem,
    recv_sem,
):
    rows, channels = upstream.shape
    poles = own_res.shape[0]
    groups = channels // LANES
    halves = groups // SUBS
    half_rows = rows * SUBS
    pole_rows = poles * SUBS
    steps = rows // SUBS
    window = rows * ctx
    me = lax.axis_index("ctx")
    my_dp = lax.axis_index("dp")

    def peer_of(o):
        return lax.rem(me + o, ctx)

    def far_first(o):
        k, j = lax.div(o, 4), lax.rem(o, 4)
        z_off = 4 + (1 - 2 * lax.rem(k, 2)) * lax.div(k + 1, 2)
        y_off = 2 + (1 - 2 * lax.rem(j, 2)) * lax.div(j + 1, 2)
        y = lax.rem(lax.div(me, 8) + y_off, 4)
        return y * 8 + lax.rem(lax.rem(me, 8) + z_off, 8)

    def dp_peer(o):
        return lax.rem(my_dp + o, dp)

    loads = [
        pltpu.make_async_copy(src, dst, load_sem.at[k])
        for k, (src, dst) in enumerate(
            [
                (rate_in, own_rate),
                (res_in, own_res),
                (skip_in, own_skip),
                (taps_in, taps),
                (feats_in, feats),
                (upstream_in, upstream),
            ]
        )
    ]
    for load in loads:
        load.start()
    barrier = pltpu.get_barrier_semaphore()

    def greet(o, c):
        pl.semaphore_signal(barrier, inc=1, device_id={"ctx": peer_of(o)}, device_id_type=MESH)
        return c

    lax.fori_loop(1, ctx, greet, 0)

    def greet_dp(o, c):
        pl.semaphore_signal(barrier, inc=1, device_id={"dp": dp_peer(o)}, device_id_type=MESH)
        return c

    lax.fori_loop(1, dp, greet_dp, 0)

    for load in loads[:3]:
        load.wait()
    rate_out[...] = jnp.concatenate([own_rate[:SUBS, :], own_rate[SUBS:, :]], axis=1)
    res_out[...] = jnp.concatenate([own_res[:SUBS, :], own_res[SUBS:, :]], axis=1)
    skip_out[...] = jnp.concatenate([own_skip[...], own_skip[...]], axis=1)

    bounds = [0]
    total = 0
    for j in range(lengths.shape[1] - 1):
        total = total + lengths[0, j]
        bounds.append(total)
    bounds.append(window)
    start = me * rows
    row = row_iota(rows)
    pos = start + row
    flat = 0 * row
    next_one = free_of(bounds, pos + 1, pos + 1)
    next_two = free_of(bounds, pos + 1, pos + 2)
    masks[0] = free_of(bounds, pos, pos)
    masks[1] = free_of(bounds, pos - 1, pos)
    masks[2] = next_one
    masks[3] = next_two

    masks[4] = free_of(bounds, pos + 1, flat + (start + rows - 1))
    masks[5] = free_of(bounds, flat + (start + 1), pos)
    masks[6] = jnp.where(row < rows - 1, next_one, 0.0)
    masks[7] = jnp.where(row < rows - 2, next_two, 0.0)
    masks[8] = free_of(bounds, flat + start, pos)
    masks[9] = free_of(bounds, pos + 1, flat + (start + rows))
    masks[10] = jnp.where(row > 0, masks[0], 0.0)
    masks[11] = jnp.where(row > 1, masks[1], 0.0)

    low16 = lane_low(poles)
    my_rate = jnp.concatenate([own_rate[...], own_rate[...]], axis=1)
    my_decay = jnp.exp(-jnp.exp(my_rate))
    block_decay = jnp.exp(-jnp.exp(my_rate) * rows)

    def join_masks(k, c):
        low = jnp.where(low16, k * rows, (ctx - 1 - k) * rows + 1)
        joins[k] = free_of(bounds, low, low + (rows - 1)) * block_decay
        keeps[k] = free_of(bounds, low, low) * my_decay
        return c

    lax.fori_loop(0, ctx, join_masks, 0)

    my_y, my_z = lax.div(me, 2 * NEAR), lax.rem(lax.div(me, 2), NEAR)

    def group_of(s):
        b, t = lax.div(s, NEAR), lax.rem(s, NEAR)
        upper = lax.div(b, 2)
        z_off = (1 - upper) * (b + 2) + upper * (3 - b)
        y = lax.rem(my_y + t + 2, NEAR)
        return y * NEAR + lax.rem(my_z + z_off, NEAR)

    def at(i, third):
        return pl.multiple_of(third * channels + i * LANES, LANES)

    def strided(s, count, stride_rows):
        return pl.ds(lax.div(s, SUBS) * stride_rows + lax.rem(s, SUBS), count, stride=SUBS)

    for load in loads[3:]:
        load.wait()

    def featured(off):
        lanes = pl.ds(off, LANES)
        f = feats[:, lanes].astype(F32)
        one = masks[10] * pltpu.roll(f, 1, 0)
        two = masks[11] * pltpu.roll(f, 2, 0)
        halo_out[:, lanes] = f[rows - 2 :]
        return taps[0:1, lanes] * f + taps[1:2, lanes] * one + taps[2:3, lanes] * two

    def enter(s, c):
        i = group_of(s)
        query, key, value = (featured(at(i, third)) for third in range(3))
        lanes = pl.ds(at(i, 0), LANES)
        up = upstream[:, lanes].astype(F32)
        keys[:, lanes] = key
        values[:, lanes] = value
        queries[:, lanes] = query[:SUBS]
        source[strided(s, rows, half_rows), :] = (key * value).astype(BF16).astype(F32)
        gradient[strided(s, rows, half_rows), :] = (up * query).astype(BF16).astype(F32)
        return c

    lax.fori_loop(0, groups, enter, 0)

    pl.semaphore_wait(barrier, ctx - 1 + dp - 1)

    def remote(src, dst, k, to):
        return pltpu.make_async_remote_copy(
            src_ref=src, dst_ref=dst, send_sem=send_sem.at[k], recv_sem=recv_sem.at[k], device_id=to, device_id_type=MESH
        )

    def send_rates(o, c):
        remote(rate_out, rates.at[me], 1, {"ctx": far_first(o)}).start()
        return c

    lax.fori_loop(0, ctx - 1, send_rates, 0)
    halo_copy = remote(halo_out, halo, 0, {"ctx": peer_of(1)})
    halo_copy.start()

    def send_others(o, c):
        remote(res_out, residues.at[me], 2, {"ctx": far_first(o)}).start()
        remote(skip_out, skips.at[me], 3, {"ctx": far_first(o)}).start()
        return c

    lax.fori_loop(0, ctx - 1, send_others, 0)
    rates[pl.ds(me, 1)] = rate_out[...][None]
    residues[pl.ds(me, 1)] = res_out[...][None]
    skips[pl.ds(me, 1)] = skip_out[...][None]

    halo_copy.wait()
    head = row_iota(SUBS)
    on_first = jnp.where(head == 0, masks[0, :SUBS, :], 0.0)
    both_first = jnp.where(head == 0, masks[1, :SUBS, :], 0.0)
    both_second = jnp.where(head == 1, masks[1, :SUBS, :], 0.0)

    def mend(s, c):
        i = group_of(s)
        here = pl.ds(at(i, 0), LANES)
        parts = []
        for third, buf in enumerate((queries, keys, values)):
            lanes = pl.ds(at(i, third), LANES)
            one, two = taps[1:2, lanes], taps[2:3, lanes]
            h1, h2 = halo[1:2, lanes], halo[0:1, lanes]
            parts.append(buf[:SUBS, here] + (on_first * one + both_second * two) * h1 + (both_first * two) * h2)
        query, key, value = parts
        keys[:SUBS, here] = key
        values[:SUBS, here] = value
        up = upstream[: 2 * SUBS, here].astype(F32)[:SUBS]
        source[strided(s, SUBS, half_rows), :] = (key * value).astype(BF16).astype(F32)
        gradient[strided(s, SUBS, half_rows), :] = (up * query).astype(BF16).astype(F32)
        return c

    lax.fori_loop(0, groups, mend, 0, unroll=True)

    def all_slots(buf, sem, slots):
        pltpu.make_async_copy(buf.at[pl.ds(0, slots)], buf.at[pl.ds(0, slots)], sem).wait()

    def wait_all(buf, k, slots):
        all_slots(buf, recv_sem.at[k], slots)

    wait_all(rates, 1, ctx - 1)

    def spread_rates(s, c):
        i = group_of(s)
        decay[strided(s, poles, pole_rows), :] = jnp.exp(-jnp.exp(unfold(rates[2 * i], rates[2 * i + 1])))
        return c

    lax.fori_loop(0, groups, spread_rates, 0, unroll=True)

    def send_slab(out, into, k, to):
        @pl.when(to != me)
        def _():
            remote(out.at[to], into.at[me], k, {"ctx": to}).start()

        @pl.when(to == me)
        def _():
            into[pl.ds(me, 1)] = out[pl.ds(me, 1)]

    def send_slots(out, into, k, low, high):
        def send(s, c):
            i = group_of(s)
            send_slab(out, into, k, 2 * i)
            send_slab(out, into, k, 2 * i + 1)
            return c

        lax.fori_loop(low, high, send, 0)

    for h in range(halves):
        pole_at = pl.ds(h * pole_rows, pole_rows)
        fac = decay[pole_at, :].reshape(poles, SUBS, LANES)

        def chunk(k, carry):
            s, u = carry
            back = steps - 1 - k
            x = source[pl.ds(pl.multiple_of(h * half_rows + k * 64, 64), 64), :].reshape(SUBS, SUBS, LANES)
            g = gradient[pl.ds(pl.multiple_of(h * half_rows + back * 64, 64), 64), :].reshape(SUBS, SUBS, LANES)
            mx = masks[4, pl.ds(pl.multiple_of(k * SUBS, SUBS), SUBS), :]
            mg = masks[5, pl.ds(pl.multiple_of(back * SUBS, SUBS), SUBS), :]
            for t in range(SUBS):
                r = SUBS - 1 - t
                s = s * fac + (x[t] * mx[t : t + 1])[None]
                u = u * fac + (g[r] * mg[r : r + 1])[None]
            return s, u

        zero = jnp.zeros((poles, SUBS, LANES), F32)
        s, u = lax.fori_loop(0, steps, chunk, (zero, zero))
        state[pole_at, :] = s.reshape(pole_rows, LANES)
        costate[pole_at, :] = u.reshape(pole_rows, LANES)

        def pack_first(s, c):
            i = group_of(s)
            low, high = split_pair(state[strided(s, poles, pole_rows), :], costate[strided(s, poles, pole_rows), :])
            first_out[2 * i] = low.astype(BF16)
            first_out[2 * i + 1] = high.astype(BF16)
            return c

        lax.fori_loop(h * SUBS, (h + 1) * SUBS, pack_first, 0, unroll=True)
        send_slots(first_out, first_in, 4, h * SUBS, (h + 1) * SUBS)

    wait_all(residues, 2, ctx - 1)
    wait_all(skips, 3, ctx - 1)

    def spread_others(s, c):
        i = group_of(s)
        coeff[strided(s, poles, pole_rows), :] = unfold(residues[2 * i], residues[2 * i + 1])
        low_s = jnp.broadcast_to(skips[2 * i], (SUBS, LANES))
        high_s = jnp.broadcast_to(skips[2 * i + 1], (SUBS, LANES))
        gain[pl.ds(s, 1), :] = join_pair(low_s, high_s, True)[0:1]
        return c

    lax.fori_loop(0, groups, spread_others, 0, unroll=True)
    state[...] = jnp.zeros_like(state)
    costate[...] = jnp.zeros_like(costate)
    res_sum[...] = jnp.zeros_like(res_sum)
    skip_sum[...] = jnp.zeros_like(skip_sum)

    def raise_powers(h):
        pole_at = pl.ds(h * pole_rows, pole_rows)
        fac = decay[pole_at, :].reshape(poles, SUBS, LANES)

        def step(k, e):
            for t in range(4):
                e = e * fac
                to = pl.multiple_of((h * rows + k * 4 + t) * pole_rows, pole_rows)
                powers[pl.ds(to, pole_rows), :] = e.reshape(pole_rows, LANES)
            return e

        lax.fori_loop(0, rows // 4, step, coeff[pole_at, :].reshape(poles, SUBS, LANES))

    def half_sweep(h):
        both = pl.ds(h * SUBS, SUBS)
        skip = gain[both, :]

        def chunk(k, c):
            back = steps - 1 - k
            at_x = pl.ds(pl.multiple_of(h * half_rows + k * 64, 64), 64)
            at_g = pl.ds(pl.multiple_of(h * half_rows + back * 64, 64), 64)
            x = source[at_x, :].reshape(SUBS, SUBS, LANES)
            gx = gradient[at_x, :].reshape(SUBS, SUBS, LANES)
            g = gradient[at_g, :].reshape(SUBS, SUBS, LANES)
            keep = masks[0, pl.ds(pl.multiple_of(k * SUBS, SUBS), SUBS), :]
            keep_g = masks[2, pl.ds(pl.multiple_of(back * SUBS, SUBS), SUBS), :]
            out = [skip * x[t] for t in range(SUBS)]
            adj = [skip * g[t] for t in range(SUBS)]
            for p in range(0, poles, GROUP):
                here = pl.ds(h * pole_rows + p * SUBS, GROUP * SUBS)
                shape = (GROUP, SUBS, LANES)
                s = state[here, :].reshape(shape)
                u = costate[here, :].reshape(shape)
                fac = decay[here, :].reshape(shape)
                res = coeff[here, :].reshape(shape)
                acc = res_sum[here, :].reshape(shape)
                for t in range(SUBS):
                    r = SUBS - 1 - t
                    s = s * (fac * keep[t : t + 1][None]) + x[t][None]
                    out[t] = out[t] + jnp.sum(res * s, axis=0)
                    acc = acc + s * gx[t][None]
                    u = u * (fac * keep_g[r : r + 1][None]) + g[r][None]
                    adj[r] = adj[r] + jnp.sum(res * u, axis=0)
                state[here, :] = s.reshape(GROUP * SUBS, LANES)
                costate[here, :] = u.reshape(GROUP * SUBS, LANES)
                res_sum[here, :] = acc.reshape(GROUP * SUBS, LANES)
            output[at_x, :] = jnp.stack(out).reshape(SUBS * SUBS, LANES)
            adjoint[at_g, :] = jnp.stack(adj).reshape(SUBS * SUBS, LANES)
            skip_sum[both, :] = skip_sum[both, :] + jnp.sum(x * gx, axis=0)
            return c

        lax.fori_loop(0, steps, chunk, 0)

    raise_powers(0)
    half_sweep(0)
    raise_powers(1)

    wait_all(first_in, 4, ctx - 1)

    def scan(k, w):
        prefixes[k] = w
        here = jnp.where(low16, first_in[k].astype(F32), first_in[ctx - 1 - k].astype(F32))
        return joins[k] * w + here

    lax.fori_loop(0, ctx, scan, jnp.zeros((poles, LANES), F32), unroll=True)

    def pack_carry(k, c):
        carry_out[k] = jnp.where(low16, prefixes[k], prefixes[ctx - 1 - k]).astype(BF16)
        return c

    lax.fori_loop(0, ctx, pack_carry, 0, unroll=True)
    send_slots(carry_out, carry_in, 5, 0, groups)

    half_sweep(1)

    def pack_res(s, c):
        i = group_of(s)
        a = res_sum[strided(s, poles, pole_rows), :]
        low, high = split_pair(a[:SUBS], a[SUBS:])
        res_part_out[2 * i] = low
        res_part_out[2 * i + 1] = high
        return c

    lax.fori_loop(0, groups, pack_res, 0, unroll=True)
    send_slots(res_part_out, res_part_in, 6, 0, groups)

    def carried_terms(k, acc):
        return acc + keeps[k] * prefixes[k] * swap_halves(first_in[k].astype(F32))

    res_carried = fold(lax.fori_loop(0, ctx, carried_terms, jnp.zeros((poles, LANES), F32)))

    wait_all(carry_in, 5, ctx - 1)

    def unpack_carry(s, c):
        i = group_of(s)
        low, high = carry_in[2 * i].astype(F32), carry_in[2 * i + 1].astype(F32)
        state[strided(s, poles, pole_rows), :] = join_pair(low, high, True)
        costate[strided(s, poles, pole_rows), :] = join_pair(low, high, False)
        return c

    lax.fori_loop(0, groups, unpack_carry, 0, unroll=True)

    for h in range(halves):
        pole_at = pl.ds(h * pole_rows, pole_rows)
        s = state[pole_at, :].reshape(poles, SUBS, LANES)
        u = costate[pole_at, :].reshape(poles, SUBS, LANES)

        def add_carry(k, c):
            for j in range(4):
                t = k * 4 + j
                r = rows - 1 - t
                e = powers[pl.ds(pl.multiple_of((h * rows + t) * pole_rows, pole_rows), pole_rows), :]
                e = e.reshape(poles, SUBS, LANES)
                at_t = pl.ds(pl.multiple_of(h * half_rows + t * SUBS, SUBS), SUBS)
                at_r = pl.ds(pl.multiple_of(h * half_rows + r * SUBS, SUBS), SUBS)
                output[at_t, :] = output[at_t, :] + masks[8, pl.ds(t, 1), :] * jnp.sum(e * s, axis=0)
                adjoint[at_r, :] = adjoint[at_r, :] + masks[9, pl.ds(r, 1), :] * jnp.sum(e * u, axis=0)
            return c

        lax.fori_loop(0, rows // 4, add_carry, 0)

    first_keep, first_both, second_both = masks[0, 0:1, :], masks[1, 0:1, :], masks[1, 1:2, :]

    def leave(s, c):
        i = group_of(s)
        here = pl.ds(at(i, 0), LANES)
        out = output[strided(s, rows, half_rows), :].astype(BF16).astype(F32)
        mixed = adjoint[strided(s, rows, half_rows), :].astype(BF16).astype(F32)
        up = upstream[:, here].astype(F32)
        sums = []
        for third, post in enumerate((up * out, mixed * values[:, here], mixed * keys[:, here])):
            lanes = pl.ds(at(i, third), LANES)
            f = feats[:, lanes].astype(F32)
            one = masks[6] * pltpu.roll(post, rows - 1, 0)
            two = masks[7] * pltpu.roll(post, rows - 2, 0)
            p0, p1 = post[0:1], post[1:2]
            h1, h2 = halo[1:2, lanes], halo[0:1, lanes]
            sums.append(jnp.sum(post * f, axis=0, keepdims=True))
            sums.append(jnp.sum(one * f, axis=0, keepdims=True) + p0 * first_keep * h1)
            sums.append(jnp.sum(two * f, axis=0, keepdims=True) + p0 * first_both * h2 + p1 * second_both * h1)
            edge_out[:, lanes] = post[0:2]
            back = taps[0:1, lanes] * post + taps[1:2, lanes] * one + taps[2:3, lanes] * two
            grad_feats[:, lanes] = back.astype(BF16)
            tail[:, lanes] = back[rows - 16 :]
        top = jnp.concatenate(sums[:SUBS], axis=0)
        rest = jnp.concatenate([sums[SUBS], skip_sum[pl.ds(s, 1), :]] + sums[:6], axis=0)
        low, high = split_pair(top, rest)
        part_out[2 * i] = low
        part_out[2 * i + 1] = high

        @pl.when(s > 0)
        def _():
            j = group_of(s - 1)
            send_slab(part_out, part_in, 9, 2 * j)
            send_slab(part_out, part_in, 9, 2 * j + 1)

        return c

    lax.fori_loop(0, groups, leave, 0)
    edge_copy = remote(edge_out, edge_in, 8, {"ctx": peer_of(ctx - 1)})
    edge_copy.start()
    send_slots(part_out, part_in, 9, groups - 1, groups)

    def sum_slots(buf, count):
        return lax.fori_loop(0, count, lambda k, acc: acc + buf[k], jnp.zeros((SUBS, LANES), F32), unroll=True)

    wait_all(part_in, 9, ctx - 1)
    dp_out[...] = sum_slots(part_in, ctx)

    def send_dp(o, c):
        remote(dp_out, dp_in.at[my_dp], 10, {"dp": dp_peer(o)}).start()
        return c

    lax.fori_loop(1, dp, send_dp, 0)
    dp_in[pl.ds(my_dp, 1)] = dp_out[...][None]
    wait_all(res_part_in, 6, ctx - 1)
    res_dp_out[...] = sum_slots(res_part_in, ctx) + res_carried

    def send_res(o, c):
        remote(res_dp_out, res_dp_in.at[my_dp], 7, {"dp": dp_peer(o)}).start()
        return c

    lax.fori_loop(1, dp, send_res, 0)
    res_dp_in[pl.ds(my_dp, 1)] = res_dp_out[...][None]
    wait_all(dp_in, 10, dp - 1)
    whole = sum_slots(dp_in, dp) * scale
    tap_out[...] = whole

    def send_taps(o, c):
        remote(tap_out, tap_in.at[me], 11, {"ctx": far_first(o)}).start()
        return c

    lax.fori_loop(0, ctx - 1, send_taps, 0)
    tap_in[pl.ds(me, 1)] = whole[None]
    grad_skip[...] = swap_halves(whole)[1:2, : LANES // 2]

    edge_copy.wait()
    last = row_iota(16)
    one16, two16 = masks[2, rows - 16 :, :], masks[3, rows - 16 :, :]
    first_one = jnp.where(last == 15, one16, 0.0)
    first_two = jnp.where(last == 14, two16, 0.0)
    second_two = jnp.where(last == 15, two16, 0.0)

    def finish(i, c):
        lanes = pl.ds(pl.multiple_of(i * LANES, LANES), LANES)
        one, two = taps[1:2, lanes], taps[2:3, lanes]
        e0, e1 = edge_in[0:1, lanes], edge_in[1:2, lanes]
        done = tail[:, lanes] + (first_one * one + first_two * two) * e0 + (second_two * two) * e1
        grad_feats[rows - 16 :, lanes] = done.astype(BF16)
        return c

    lax.fori_loop(0, 3 * groups, finish, 0)
    wait_all(res_dp_in, 7, dp - 1)
    res_whole = sum_slots(res_dp_in, dp) * scale
    grad_res[:SUBS, :] = res_whole[:, : LANES // 2]
    grad_res[SUBS:, :] = swap_halves(res_whole)[:, : LANES // 2]
    for k, buf, slots in [
        (1, rates, ctx),
        (2, residues, ctx),
        (3, skips, ctx),
        (4, first_in, ctx),
        (5, carry_in, ctx),
        (6, res_part_in, ctx),
        (7, res_dp_in, dp),
        (9, part_in, ctx),
        (10, dp_in, dp),
        (11, tap_in, ctx),
    ]:
        all_slots(buf, send_sem.at[k], slots - 1)

    wait_all(tap_in, 11, ctx - 1)

    def place_taps(i, c):
        low, high = tap_in[2 * i], tap_in[2 * i + 1]
        first = join_pair(low, high, True)
        last_row = join_pair(low, high, False)[0:1]
        for third in range(3):
            for j in range(3):
                r = third * 3 + j
                grad_taps[j : j + 1, pl.ds(at(i, third), LANES)] = first[r : r + 1] if r < SUBS else last_row
        return c

    lax.fori_loop(0, groups, place_taps, 0, unroll=True)


def write_out(*refs):
    count = (len(refs) - 1) // 2
    sems = refs[-1]
    copies = [pltpu.make_async_copy(refs[k], refs[count + k], sems.at[k]) for k in range(count)]
    for copy in copies:
        copy.start()
    for copy in copies:
        copy.wait()


def per_device(features, upstream, lengths, conv_taps, residues, log_rate, skip_gain):
    rows, width = features.shape[1:]
    channels = upstream.shape[2]
    poles, owned = residues.shape
    ctx = lax.axis_size("ctx")
    dp = lax.axis_size("dp")
    scale = 1.0 / math.sqrt(rows * ctx * dp)
    groups = channels // LANES
    vmem = pl.BlockSpec(memory_space=pltpu.VMEM)
    smem = pl.BlockSpec(memory_space=pltpu.SMEM)
    hbm = pl.BlockSpec(memory_space=pltpu.HBM)
    slab = (ctx, poles, LANES)
    folded = (ctx, SUBS, LANES)
    wide = pltpu.VMEM((rows * groups, LANES), F32)
    per_pole = pltpu.VMEM((poles * groups, LANES), F32)
    scratch = [
        pltpu.VMEM((rows, width), BF16),
        pltpu.VMEM((rows, channels), BF16),
        pltpu.VMEM((3, width), F32),
        pltpu.VMEM((poles, owned), F32),
        pltpu.VMEM((poles, owned), F32),
        pltpu.VMEM((1, owned), F32),
        pltpu.VMEM((SUBS, LANES), F32),
        pltpu.VMEM((SUBS, LANES), F32),
        pltpu.VMEM((1, LANES), F32),
        pltpu.VMEM(folded, F32),
        pltpu.VMEM(folded, F32),
        pltpu.VMEM((ctx, 1, LANES), F32),
        pltpu.VMEM((2, width), F32),
        pltpu.VMEM((2, width), F32),
        pltpu.VMEM(slab, BF16),
        pltpu.VMEM(slab, BF16),
        pltpu.VMEM(slab, BF16),
        pltpu.VMEM(slab, BF16),
        pltpu.VMEM(slab, F32),
        pltpu.VMEM(slab, F32),
        pltpu.VMEM(slab, F32),
        wide,
        wide,
        wide,
        wide,
        pltpu.VMEM((SUBS, channels), F32),
        pltpu.VMEM((rows, channels), F32),
        pltpu.VMEM((rows, channels), F32),
        per_pole,
        per_pole,
        pltpu.VMEM((rows * poles * groups, LANES), F32),
        pltpu.VMEM((groups, LANES), F32),
        per_pole,
        per_pole,
        per_pole,
        pltpu.VMEM((groups, LANES), F32),
        pltpu.VMEM((12, rows, LANES), F32),
        pltpu.VMEM((2, width), F32),
        pltpu.VMEM((2, width), F32),
        pltpu.VMEM((16, width), F32),
        pltpu.VMEM(folded, F32),
        pltpu.VMEM(folded, F32),
        pltpu.VMEM((SUBS, LANES), F32),
        pltpu.VMEM((dp, SUBS, LANES), F32),
        pltpu.VMEM(folded, F32),
        pltpu.VMEM(folded, F32),
        pltpu.VMEM((SUBS, LANES), F32),
        pltpu.VMEM((dp, SUBS, LANES), F32),
        pltpu.VMEM((SUBS, LANES), F32),
        pltpu.VMEM(folded, F32),
        pltpu.SemaphoreType.DMA((6,)),
        pltpu.SemaphoreType.DMA((12,)),
        pltpu.SemaphoreType.DMA((12,)),
    ]
    results = (
        jax.ShapeDtypeStruct((rows, width), BF16),
        jax.ShapeDtypeStruct((3, width), F32),
        jax.ShapeDtypeStruct((poles, owned), F32),
        jax.ShapeDtypeStruct((1, owned), F32),
    )
    held = pl.pallas_call(
        functools.partial(kernel, ctx, dp, scale),
        out_shape=results,
        in_specs=[smem] + [hbm] * 6,
        out_specs=(vmem,) * 4,
        scratch_shapes=scratch,
        compiler_params=pltpu.CompilerParams(
            collective_id=0, has_side_effects=True, vmem_limit_bytes=44 * 1024 * 1024
        ),
        name="conv_block",
    )(
        *(
            pltpu.with_memory_space_constraint(x, pltpu.HBM)
            for x in (lengths, features[0], upstream[0], conv_taps, residues, log_rate, skip_gain[None])
        )
    )
    grad_feats, grad_taps, grad_res, grad_skip = pl.pallas_call(
        write_out,
        out_shape=results,
        in_specs=[vmem] * 4,
        out_specs=(hbm,) * 4,
        scratch_shapes=[pltpu.SemaphoreType.DMA((4,))],
        compiler_params=pltpu.CompilerParams(vmem_limit_bytes=8 * 1024 * 1024),
        name="write_out",
    )(*held)
    return (grad_feats[None], grad_taps, grad_res, grad_skip[0])


def solution(mesh):
    return jax.shard_map(
        per_device,
        mesh=mesh,
        in_specs=(
            P("dp", "ctx", None),
            P("dp", "ctx", None),
            P("dp", None),
            P(),
            P(None, "ctx"),
            P(None, "ctx"),
            P("ctx"),
        ),
        out_specs=(P("dp", "ctx", None), P(), P(None, "ctx"), P("ctx")),
        check_vma=False,
    )
```

```python
import functools
import math

import jax
import jax.numpy as jnp
from jax import lax
from jax.experimental import pallas as pl
from jax.experimental.pallas import tpu as pltpu
from jax.sharding import PartitionSpec as P

MESH = pl.DeviceIdType.MESH
F32 = jnp.float32
BF16 = jnp.bfloat16
LANES = 128
SUBS = 8
GROUP = 4
NEAR = 4


def row_iota(rows):
    return lax.broadcasted_iota(jnp.int32, (rows, LANES), 0)


def lane_low(rows):
    return lax.broadcasted_iota(jnp.int32, (rows, LANES), 1) < LANES // 2


def swap_halves(x):
    return pltpu.roll(x, LANES // 2, 1)


def join_pair(low, high, first):
    mask = lane_low(low.shape[0])
    if first:
        return jnp.where(mask, low, swap_halves(high))
    return jnp.where(mask, swap_halves(low), high)


def split_pair(a, b):
    mask = lane_low(a.shape[0])
    return jnp.where(mask, a, swap_halves(b)), jnp.where(mask, swap_halves(a), b)


def unfold(low, high):
    return jnp.concatenate([join_pair(low, high, True), join_pair(low, high, False)], axis=0)


def fold(x):
    return jnp.where(lane_low(SUBS), x[:SUBS], swap_halves(x[SUBS:]))


def free_of(bounds, low, high):
    clear = None
    for bound in bounds:
        one = (low > bound) | (high < bound)
        clear = one if clear is None else clear & one
    return jnp.where(clear, 1.0, 0.0).astype(F32)


def kernel(
    ctx,
    dp,
    scale,
    lengths,
    feats_in,
    upstream_in,
    taps_in,
    res_in,
    rate_in,
    skip_in,
    grad_feats,
    grad_taps,
    grad_res,
    grad_skip,
    feats,
    upstream,
    taps,
    own_res,
    own_rate,
    own_skip,
    rate_out,
    res_out,
    skip_out,
    rates,
    residues,
    skips,
    halo_out,
    halo,
    first_out,
    first_in,
    carry_out,
    carry_in,
    prefixes,
    joins,
    keeps,
    source,
    gradient,
    output,
    adjoint,
    queries,
    keys,
    values,
    decay,
    coeff,
    powers,
    gain,
    state,
    costate,
    res_sum,
    skip_sum,
    masks,
    edge_out,
    edge_in,
    posts,
    res_part_out,
    res_part_in,
    res_dp_out,
    res_dp_in,
    part_out,
    part_in,
    column_out,
    column_in,
    tap_out,
    tap_in,
    load_sem,
    send_sem,
    recv_sem,
):
    rows, channels = upstream.shape
    poles = own_res.shape[0]
    groups = channels // LANES
    halves = groups // SUBS
    half_rows = rows * SUBS
    pole_rows = poles * SUBS
    steps = rows // SUBS
    window = rows * ctx
    me = lax.axis_index("ctx")
    my_dp = lax.axis_index("dp")

    def peer_of(o):
        return lax.rem(me + o, ctx)

    def far_first(o):
        k, j = lax.div(o, 4), lax.rem(o, 4)
        z_off = 4 + (1 - 2 * lax.rem(k, 2)) * lax.div(k + 1, 2)
        y_off = 2 + (1 - 2 * lax.rem(j, 2)) * lax.div(j + 1, 2)
        y = lax.rem(lax.div(me, 8) + y_off, 4)
        return y * 8 + lax.rem(lax.rem(me, 8) + z_off, 8)

    def dp_peer(o):
        return lax.rem(my_dp + o, dp)

    my_column, my_row = lax.rem(me, 8), lax.div(me, 8)
    my_member = my_row * dp + my_dp

    def member(j):
        return {"ctx": lax.div(j, dp) * 8 + my_column, "dp": lax.rem(j, dp)}

    def other_member(o):
        return lax.rem(my_member + o, ctx)

    def column_peer(o):
        return {"ctx": my_row * 8 + lax.rem(my_column + o, 8)}

    loads = [
        pltpu.make_async_copy(src, dst, load_sem.at[k])
        for k, (src, dst) in enumerate(
            [
                (rate_in, own_rate),
                (res_in, own_res),
                (skip_in, own_skip),
                (taps_in, taps),
                (feats_in, feats),
                (upstream_in, upstream),
            ]
        )
    ]
    for load in loads:
        load.start()

    barrier = pltpu.get_barrier_semaphore()

    def greet(o, c):
        pl.semaphore_signal(barrier, inc=1, device_id={"ctx": far_first(o)}, device_id_type=MESH)
        return c

    lax.fori_loop(0, ctx - 1, greet, 0)

    def greet_member(o, c):
        pl.semaphore_signal(barrier, inc=1, device_id=member(other_member(o)), device_id_type=MESH)
        return c

    lax.fori_loop(1, ctx, greet_member, 0)

    for load in loads[:3]:
        load.wait()
    rate_out[...] = jnp.concatenate([own_rate[:SUBS, :], own_rate[SUBS:, :]], axis=1)
    res_out[...] = jnp.concatenate([own_res[:SUBS, :], own_res[SUBS:, :]], axis=1)
    skip_out[...] = jnp.concatenate([own_skip[...], own_skip[...]], axis=1)

    bounds = [0]
    total = 0
    for j in range(lengths.shape[1] - 1):
        total = total + lengths[0, j]
        bounds.append(total)
    bounds.append(window)
    start = me * rows
    row = row_iota(rows)
    pos = start + row
    flat = 0 * row
    next_one = free_of(bounds, pos + 1, pos + 1)
    next_two = free_of(bounds, pos + 1, pos + 2)
    masks[0] = free_of(bounds, pos, pos)
    masks[1] = free_of(bounds, pos - 1, pos)
    masks[2] = next_one
    masks[3] = next_two

    masks[4] = free_of(bounds, pos + 1, flat + (start + rows - 1))
    masks[5] = free_of(bounds, flat + (start + 1), pos)
    masks[6] = jnp.where(row < rows - 1, next_one, 0.0)
    masks[7] = jnp.where(row < rows - 2, next_two, 0.0)
    masks[8] = free_of(bounds, flat + start, pos)
    masks[9] = free_of(bounds, pos + 1, flat + (start + rows))
    masks[10] = jnp.where(row > 0, masks[0], 0.0)
    masks[11] = jnp.where(row > 1, masks[1], 0.0)

    low16 = lane_low(poles)
    my_rate = jnp.concatenate([own_rate[...], own_rate[...]], axis=1)
    my_decay = jnp.exp(-jnp.exp(my_rate))
    block_decay = jnp.exp(-jnp.exp(my_rate) * rows)

    def join_masks(k, c):
        low = jnp.where(low16, k * rows, (ctx - 1 - k) * rows + 1)
        joins[k] = free_of(bounds, low, low + (rows - 1)) * block_decay
        keeps[k] = free_of(bounds, low, low) * my_decay
        return c

    lax.fori_loop(0, ctx, join_masks, 0)

    my_y, my_z = lax.div(me, 2 * NEAR), lax.rem(lax.div(me, 2), NEAR)

    def group_of(s):
        b, t = lax.div(s, NEAR), lax.rem(s, NEAR)
        upper = lax.div(b, 2)
        z_off = (1 - upper) * (b + 2) + upper * (3 - b)
        y = lax.rem(my_y + t + 2, NEAR)
        return y * NEAR + lax.rem(my_z + z_off, NEAR)

    def at(i, third):
        return pl.multiple_of(third * channels + i * LANES, LANES)

    def strided(s, count, stride_rows):
        return pl.ds(lax.div(s, SUBS) * stride_rows + lax.rem(s, SUBS), count, stride=SUBS)

    for load in loads[3:]:
        load.wait()

    def featured(off):
        lanes = pl.ds(off, LANES)
        f = feats[:, lanes].astype(F32)
        one = masks[10] * pltpu.roll(f, 1, 0)
        two = masks[11] * pltpu.roll(f, 2, 0)
        halo_out[:, lanes] = f[rows - 2 :]
        return taps[0:1, lanes] * f + taps[1:2, lanes] * one + taps[2:3, lanes] * two

    def enter(s, c):
        i = group_of(s)
        query, key, value = (featured(at(i, third)) for third in range(3))
        lanes = pl.ds(at(i, 0), LANES)
        up = upstream[:, lanes].astype(F32)
        keys[:, lanes] = key
        values[:, lanes] = value
        queries[:, lanes] = query[:SUBS]
        source[strided(s, rows, half_rows), :] = (key * value).astype(BF16).astype(F32)
        gradient[strided(s, rows, half_rows), :] = (up * query).astype(BF16).astype(F32)
        return c

    lax.fori_loop(0, groups, enter, 0)

    pl.semaphore_wait(barrier, 2 * (ctx - 1))

    def remote(src, dst, k, to):
        return pltpu.make_async_remote_copy(
            src_ref=src, dst_ref=dst, send_sem=send_sem.at[k], recv_sem=recv_sem.at[k], device_id=to, device_id_type=MESH
        )

    def send_rates(o, c):
        remote(rate_out, rates.at[me], 1, {"ctx": far_first(o)}).start()
        return c

    lax.fori_loop(0, ctx - 1, send_rates, 0)
    halo_copy = remote(halo_out, halo, 0, {"ctx": peer_of(1)})
    halo_copy.start()

    def send_others(o, c):
        remote(res_out, residues.at[me], 2, {"ctx": far_first(o)}).start()
        remote(skip_out, skips.at[me], 3, {"ctx": far_first(o)}).start()
        return c

    lax.fori_loop(0, ctx - 1, send_others, 0)
    rates[pl.ds(me, 1)] = rate_out[...][None]
    residues[pl.ds(me, 1)] = res_out[...][None]
    skips[pl.ds(me, 1)] = skip_out[...][None]

    halo_copy.wait()
    head = row_iota(SUBS)
    on_first = jnp.where(head == 0, masks[0, :SUBS, :], 0.0)
    both_first = jnp.where(head == 0, masks[1, :SUBS, :], 0.0)
    both_second = jnp.where(head == 1, masks[1, :SUBS, :], 0.0)

    def mend(s, c):
        i = group_of(s)
        here = pl.ds(at(i, 0), LANES)
        parts = []
        for third, buf in enumerate((queries, keys, values)):
            lanes = pl.ds(at(i, third), LANES)
            one, two = taps[1:2, lanes], taps[2:3, lanes]
            h1, h2 = halo[1:2, lanes], halo[0:1, lanes]
            parts.append(buf[:SUBS, here] + (on_first * one + both_second * two) * h1 + (both_first * two) * h2)
        query, key, value = parts
        keys[:SUBS, here] = key
        values[:SUBS, here] = value
        up = upstream[: 2 * SUBS, here].astype(F32)[:SUBS]
        source[strided(s, SUBS, half_rows), :] = (key * value).astype(BF16).astype(F32)
        gradient[strided(s, SUBS, half_rows), :] = (up * query).astype(BF16).astype(F32)
        return c

    lax.fori_loop(0, groups, mend, 0, unroll=True)

    def all_slots(buf, sem, slots):
        pltpu.make_async_copy(buf.at[pl.ds(0, slots)], buf.at[pl.ds(0, slots)], sem).wait()

    def wait_all(buf, k, slots):
        all_slots(buf, recv_sem.at[k], slots)

    wait_all(rates, 1, ctx - 1)

    def spread_rates(s, c):
        i = group_of(s)
        decay[strided(s, poles, pole_rows), :] = jnp.exp(-jnp.exp(unfold(rates[2 * i], rates[2 * i + 1])))
        return c

    lax.fori_loop(0, groups, spread_rates, 0, unroll=True)

    def send_slab(out, into, k, to):
        @pl.when(to != me)
        def _():
            remote(out.at[to], into.at[me], k, {"ctx": to}).start()

        @pl.when(to == me)
        def _():
            into[pl.ds(me, 1)] = out[pl.ds(me, 1)]

    def send_slots(out, into, k, low, high):
        def send(s, c):
            i = group_of(s)
            send_slab(out, into, k, 2 * i)
            send_slab(out, into, k, 2 * i + 1)
            return c

        lax.fori_loop(low, high, send, 0)

    for h in range(halves):
        pole_at = pl.ds(h * pole_rows, pole_rows)
        fac = decay[pole_at, :].reshape(poles, SUBS, LANES)

        def chunk(k, carry):
            s, u = carry
            back = steps - 1 - k
            x = source[pl.ds(pl.multiple_of(h * half_rows + k * 64, 64), 64), :].reshape(SUBS, SUBS, LANES)
            g = gradient[pl.ds(pl.multiple_of(h * half_rows + back * 64, 64), 64), :].reshape(SUBS, SUBS, LANES)
            mx = masks[4, pl.ds(pl.multiple_of(k * SUBS, SUBS), SUBS), :]
            mg = masks[5, pl.ds(pl.multiple_of(back * SUBS, SUBS), SUBS), :]
            for t in range(SUBS):
                r = SUBS - 1 - t
                s = s * fac + (x[t] * mx[t : t + 1])[None]
                u = u * fac + (g[r] * mg[r : r + 1])[None]
            return s, u

        zero = jnp.zeros((poles, SUBS, LANES), F32)
        s, u = lax.fori_loop(0, steps, chunk, (zero, zero))
        state[pole_at, :] = s.reshape(pole_rows, LANES)
        costate[pole_at, :] = u.reshape(pole_rows, LANES)

        def pack_first(s, c):
            i = group_of(s)
            low, high = split_pair(state[strided(s, poles, pole_rows), :], costate[strided(s, poles, pole_rows), :])
            first_out[2 * i] = low.astype(BF16)
            first_out[2 * i + 1] = high.astype(BF16)
            return c

        lax.fori_loop(h * SUBS, (h + 1) * SUBS, pack_first, 0, unroll=True)
        send_slots(first_out, first_in, 4, h * SUBS, (h + 1) * SUBS)

    wait_all(residues, 2, ctx - 1)
    wait_all(skips, 3, ctx - 1)

    def spread_others(s, c):
        i = group_of(s)
        coeff[strided(s, poles, pole_rows), :] = unfold(residues[2 * i], residues[2 * i + 1])
        low_s = jnp.broadcast_to(skips[2 * i], (SUBS, LANES))
        high_s = jnp.broadcast_to(skips[2 * i + 1], (SUBS, LANES))
        gain[pl.ds(s, 1), :] = join_pair(low_s, high_s, True)[0:1]
        return c

    lax.fori_loop(0, groups, spread_others, 0, unroll=True)
    state[...] = jnp.zeros_like(state)
    costate[...] = jnp.zeros_like(costate)
    res_sum[...] = jnp.zeros_like(res_sum)
    skip_sum[...] = jnp.zeros_like(skip_sum)

    def raise_powers(h):
        pole_at = pl.ds(h * pole_rows, pole_rows)
        fac = decay[pole_at, :].reshape(poles, SUBS, LANES)

        def step(k, e):
            for t in range(4):
                e = e * fac
                to = pl.multiple_of((h * rows + k * 4 + t) * pole_rows, pole_rows)
                powers[pl.ds(to, pole_rows), :] = e.reshape(pole_rows, LANES)
            return e

        lax.fori_loop(0, rows // 4, step, coeff[pole_at, :].reshape(poles, SUBS, LANES))

    def half_sweep(h):
        both = pl.ds(h * SUBS, SUBS)
        skip = gain[both, :]

        def chunk(k, c):
            back = steps - 1 - k
            at_x = pl.ds(pl.multiple_of(h * half_rows + k * 64, 64), 64)
            at_g = pl.ds(pl.multiple_of(h * half_rows + back * 64, 64), 64)
            x = source[at_x, :].reshape(SUBS, SUBS, LANES)
            gx = gradient[at_x, :].reshape(SUBS, SUBS, LANES)
            g = gradient[at_g, :].reshape(SUBS, SUBS, LANES)
            keep = masks[0, pl.ds(pl.multiple_of(k * SUBS, SUBS), SUBS), :]
            keep_g = masks[2, pl.ds(pl.multiple_of(back * SUBS, SUBS), SUBS), :]
            out = [skip * x[t] for t in range(SUBS)]
            adj = [skip * g[t] for t in range(SUBS)]
            for p in range(0, poles, GROUP):
                here = pl.ds(h * pole_rows + p * SUBS, GROUP * SUBS)
                shape = (GROUP, SUBS, LANES)
                s = state[here, :].reshape(shape)
                u = costate[here, :].reshape(shape)
                fac = decay[here, :].reshape(shape)
                res = coeff[here, :].reshape(shape)
                acc = res_sum[here, :].reshape(shape)
                for t in range(SUBS):
                    r = SUBS - 1 - t
                    s = s * (fac * keep[t : t + 1][None]) + x[t][None]
                    out[t] = out[t] + jnp.sum(res * s, axis=0)
                    acc = acc + s * gx[t][None]
                    u = u * (fac * keep_g[r : r + 1][None]) + g[r][None]
                    adj[r] = adj[r] + jnp.sum(res * u, axis=0)
                state[here, :] = s.reshape(GROUP * SUBS, LANES)
                costate[here, :] = u.reshape(GROUP * SUBS, LANES)
                res_sum[here, :] = acc.reshape(GROUP * SUBS, LANES)
            output[at_x, :] = jnp.stack(out).reshape(SUBS * SUBS, LANES)
            adjoint[at_g, :] = jnp.stack(adj).reshape(SUBS * SUBS, LANES)
            skip_sum[both, :] = skip_sum[both, :] + jnp.sum(x * gx, axis=0)
            return c

        lax.fori_loop(0, steps, chunk, 0)

    raise_powers(0)
    half_sweep(0)
    raise_powers(1)

    wait_all(first_in, 4, ctx - 1)

    def scan(k, w):
        prefixes[k] = w
        here = jnp.where(low16, first_in[k].astype(F32), first_in[ctx - 1 - k].astype(F32))
        return joins[k] * w + here

    lax.fori_loop(0, ctx, scan, jnp.zeros((poles, LANES), F32), unroll=True)

    def pack_carry(k, c):
        carry_out[k] = jnp.where(low16, prefixes[k], prefixes[ctx - 1 - k]).astype(BF16)
        return c

    lax.fori_loop(0, ctx, pack_carry, 0, unroll=True)
    send_slots(carry_out, carry_in, 5, 0, groups)

    half_sweep(1)

    def pack_res(s, c):
        i = group_of(s)
        a = res_sum[strided(s, poles, pole_rows), :]
        low, high = split_pair(a[:SUBS], a[SUBS:])
        res_part_out[2 * i] = low
        res_part_out[2 * i + 1] = high
        return c

    lax.fori_loop(0, groups, pack_res, 0, unroll=True)
    send_slots(res_part_out, res_part_in, 6, 0, groups)

    def carried_terms(k, acc):
        return acc + keeps[k] * prefixes[k] * swap_halves(first_in[k].astype(F32))

    res_carried = fold(lax.fori_loop(0, ctx, carried_terms, jnp.zeros((poles, LANES), F32)))

    wait_all(carry_in, 5, ctx - 1)

    def unpack_carry(s, c):
        i = group_of(s)
        low, high = carry_in[2 * i].astype(F32), carry_in[2 * i + 1].astype(F32)
        state[strided(s, poles, pole_rows), :] = join_pair(low, high, True)
        costate[strided(s, poles, pole_rows), :] = join_pair(low, high, False)
        return c

    lax.fori_loop(0, groups, unpack_carry, 0, unroll=True)

    for h in range(halves):
        pole_at = pl.ds(h * pole_rows, pole_rows)
        s = state[pole_at, :].reshape(poles, SUBS, LANES)
        u = costate[pole_at, :].reshape(poles, SUBS, LANES)

        def add_carry(k, c):
            for j in range(4):
                t = k * 4 + j
                r = rows - 1 - t
                e = powers[pl.ds(pl.multiple_of((h * rows + t) * pole_rows, pole_rows), pole_rows), :]
                e = e.reshape(poles, SUBS, LANES)
                at_t = pl.ds(pl.multiple_of(h * half_rows + t * SUBS, SUBS), SUBS)
                at_r = pl.ds(pl.multiple_of(h * half_rows + r * SUBS, SUBS), SUBS)
                output[at_t, :] = output[at_t, :] + masks[8, pl.ds(t, 1), :] * jnp.sum(e * s, axis=0)
                adjoint[at_r, :] = adjoint[at_r, :] + masks[9, pl.ds(r, 1), :] * jnp.sum(e * u, axis=0)
            return c

        lax.fori_loop(0, rows // 4, add_carry, 0)

    first_keep, first_both, second_both = masks[0, 0:1, :], masks[1, 0:1, :], masks[1, 1:2, :]
    my_x = lax.div(my_dp, 2)

    def team_group(o):
        k, j = lax.div(o, NEAR), lax.rem(o, NEAR)
        x_off = 2 + (1 - 2 * lax.rem(k, 2)) * lax.div(k + 1, 2)
        y_off = 2 + (1 - 2 * lax.rem(j, 2)) * lax.div(j + 1, 2)
        return lax.rem(my_row + y_off, NEAR) * NEAR + lax.rem(my_x + x_off, NEAR)

    def slot_of(i):
        t = lax.rem(lax.div(i, NEAR) + NEAR - my_y + 2, NEAR)
        z_off = lax.rem(lax.rem(i, NEAR) + NEAR - my_z, NEAR)
        upper = lax.div(z_off, 2)
        return ((1 - upper) * (3 - z_off) + upper * (z_off - 2)) * NEAR + t

    def send_part(j):
        remote(part_out.at[j], part_in.at[my_member], 9, member(j)).start()

    def leave(o, c):
        i = team_group(o)
        s = slot_of(i)
        here = pl.ds(at(i, 0), LANES)
        out = output[strided(s, rows, half_rows), :].astype(BF16).astype(F32)
        mixed = adjoint[strided(s, rows, half_rows), :].astype(BF16).astype(F32)
        up = upstream[:, here].astype(F32)
        sums = []
        for third, post in enumerate((up * out, mixed * values[:, here], mixed * keys[:, here])):
            lanes = pl.ds(at(i, third), LANES)
            f = feats[:, lanes].astype(F32)
            posts[:, lanes] = post
            edge_out[:, lanes] = post[0:2]
            one = masks[6] * pltpu.roll(post, rows - 1, 0)
            two = masks[7] * pltpu.roll(post, rows - 2, 0)
            p0, p1 = post[0:1], post[1:2]
            h1, h2 = halo[1:2, lanes], halo[0:1, lanes]
            sums.append(jnp.sum(post * f, axis=0, keepdims=True))
            sums.append(jnp.sum(one * f, axis=0, keepdims=True) + p0 * first_keep * h1)
            sums.append(jnp.sum(two * f, axis=0, keepdims=True) + p0 * first_both * h2 + p1 * second_both * h1)
        top = jnp.concatenate(sums[:SUBS], axis=0)
        rest = jnp.concatenate([sums[SUBS], skip_sum[pl.ds(s, 1), :]] + sums[:6], axis=0)
        low, high = split_pair(top, rest)
        part_out[2 * i] = low
        part_out[2 * i + 1] = high

        @pl.when(o > 0)
        def _():
            j = team_group(o - 1)
            send_part(2 * j)
            send_part(2 * j + 1)

        return c

    lax.fori_loop(0, groups, leave, 0)
    mate = my_member + 1 - 2 * lax.rem(my_member, 2)
    send_part(mate)
    part_in[pl.ds(my_member, 1)] = part_out[pl.ds(my_member, 1)]
    edge_copy = remote(edge_out, edge_in, 8, {"ctx": peer_of(ctx - 1)})
    edge_copy.start()

    def sum_slots(buf, count):
        return lax.fori_loop(0, count, lambda k, acc: acc + buf[k], jnp.zeros((SUBS, LANES), F32), unroll=True)

    wait_all(part_in, 9, ctx - 1)
    column_out[...] = sum_slots(part_in, ctx)

    def send_column(o, c):
        remote(column_out, column_in.at[my_column], 10, column_peer(o)).start()
        return c

    lax.fori_loop(1, 8, send_column, 0)
    column_in[pl.ds(my_column, 1)] = column_out[...][None]
    wait_all(column_in, 10, 7)
    whole = sum_slots(column_in, 8) * scale
    tap_out[...] = whole

    def send_taps(o, c):
        remote(tap_out, tap_in.at[my_member], 11, member(other_member(o))).start()
        return c

    lax.fori_loop(1, ctx, send_taps, 0)
    tap_in[pl.ds(my_member, 1)] = whole[None]

    wait_all(res_part_in, 6, ctx - 1)
    res_dp_out[...] = sum_slots(res_part_in, ctx) + res_carried

    def send_res(o, c):
        remote(res_dp_out, res_dp_in.at[my_dp], 7, {"dp": dp_peer(o)}).start()
        return c

    lax.fori_loop(1, dp, send_res, 0)
    res_dp_in[pl.ds(my_dp, 1)] = res_dp_out[...][None]
    edge_copy.wait()

    def finish(i, c):
        lanes = pl.ds(pl.multiple_of(i * LANES, LANES), LANES)
        post = posts[:, lanes]
        after = jnp.where(head == 0, edge_in[0:1, lanes], edge_in[1:2, lanes])
        ext = jnp.concatenate([post, after], axis=0)
        one = masks[2] * pltpu.roll(ext, rows + SUBS - 1, 0)[:rows]
        two = masks[3] * pltpu.roll(ext, rows + SUBS - 2, 0)[:rows]
        back = taps[0:1, lanes] * post + taps[1:2, lanes] * one + taps[2:3, lanes] * two
        grad_feats[:, lanes] = back.astype(BF16)
        return c

    lax.fori_loop(0, 3 * groups, finish, 0)
    wait_all(res_dp_in, 7, dp - 1)
    res_whole = sum_slots(res_dp_in, dp) * scale
    grad_res[:SUBS, :] = res_whole[:, : LANES // 2]
    grad_res[SUBS:, :] = swap_halves(res_whole)[:, : LANES // 2]
    for k, buf, slots in [
        (1, rates, ctx),
        (2, residues, ctx),
        (3, skips, ctx),
        (4, first_in, ctx),
        (5, carry_in, ctx),
        (6, res_part_in, ctx),
        (7, res_dp_in, dp),
        (9, part_in, ctx),
        (10, column_in, 8),
        (11, tap_in, ctx),
    ]:
        all_slots(buf, send_sem.at[k], slots - 1)

    wait_all(tap_in, 11, ctx - 1)
    grad_skip[...] = swap_halves(tap_in[me])[1:2, : LANES // 2]

    def place_taps(i, c):
        low, high = tap_in[2 * i], tap_in[2 * i + 1]
        first = join_pair(low, high, True)
        last_row = join_pair(low, high, False)[0:1]
        for third in range(3):
            for j in range(3):
                r = third * 3 + j
                grad_taps[j : j + 1, pl.ds(at(i, third), LANES)] = first[r : r + 1] if r < SUBS else last_row
        return c

    lax.fori_loop(0, groups, place_taps, 0, unroll=True)


def write_out(*refs):
    count = (len(refs) - 1) // 2
    sems = refs[-1]
    copies = [pltpu.make_async_copy(refs[k], refs[count + k], sems.at[k]) for k in range(count)]
    for copy in copies:
        copy.start()
    for copy in copies:
        copy.wait()


def per_device(features, upstream, lengths, conv_taps, residues, log_rate, skip_gain):
    rows, width = features.shape[1:]
    channels = upstream.shape[2]
    poles, owned = residues.shape
    ctx = lax.axis_size("ctx")
    dp = lax.axis_size("dp")
    scale = 1.0 / math.sqrt(rows * ctx * dp)
    groups = channels // LANES
    vmem = pl.BlockSpec(memory_space=pltpu.VMEM)
    smem = pl.BlockSpec(memory_space=pltpu.SMEM)
    hbm = pl.BlockSpec(memory_space=pltpu.HBM)
    slab = (ctx, poles, LANES)
    folded = (ctx, SUBS, LANES)
    wide = pltpu.VMEM((rows * groups, LANES), F32)
    per_pole = pltpu.VMEM((poles * groups, LANES), F32)
    scratch = [
        pltpu.VMEM((rows, width), BF16),
        pltpu.VMEM((rows, channels), BF16),
        pltpu.VMEM((3, width), F32),
        pltpu.VMEM((poles, owned), F32),
        pltpu.VMEM((poles, owned), F32),
        pltpu.VMEM((1, owned), F32),
        pltpu.VMEM((SUBS, LANES), F32),
        pltpu.VMEM((SUBS, LANES), F32),
        pltpu.VMEM((1, LANES), F32),
        pltpu.VMEM(folded, F32),
        pltpu.VMEM(folded, F32),
        pltpu.VMEM((ctx, 1, LANES), F32),
        pltpu.VMEM((2, width), F32),
        pltpu.VMEM((2, width), F32),
        pltpu.VMEM(slab, BF16),
        pltpu.VMEM(slab, BF16),
        pltpu.VMEM(slab, BF16),
        pltpu.VMEM(slab, BF16),
        pltpu.VMEM(slab, F32),
        pltpu.VMEM(slab, F32),
        pltpu.VMEM(slab, F32),
        wide,
        wide,
        wide,
        wide,
        pltpu.VMEM((SUBS, channels), F32),
        pltpu.VMEM((rows, channels), F32),
        pltpu.VMEM((rows, channels), F32),
        per_pole,
        per_pole,
        pltpu.VMEM((rows * poles * groups, LANES), F32),
        pltpu.VMEM((groups, LANES), F32),
        per_pole,
        per_pole,
        per_pole,
        pltpu.VMEM((groups, LANES), F32),
        pltpu.VMEM((12, rows, LANES), F32),
        pltpu.VMEM((2, width), F32),
        pltpu.VMEM((2, width), F32),
        pltpu.VMEM((rows, width), F32),
        pltpu.VMEM(folded, F32),
        pltpu.VMEM(folded, F32),
        pltpu.VMEM((SUBS, LANES), F32),
        pltpu.VMEM((dp, SUBS, LANES), F32),
        pltpu.VMEM(folded, F32),
        pltpu.VMEM(folded, F32),
        pltpu.VMEM((SUBS, LANES), F32),
        pltpu.VMEM((8, SUBS, LANES), F32),
        pltpu.VMEM((SUBS, LANES), F32),
        pltpu.VMEM(folded, F32),
        pltpu.SemaphoreType.DMA((6,)),
        pltpu.SemaphoreType.DMA((12,)),
        pltpu.SemaphoreType.DMA((12,)),
    ]
    results = (
        jax.ShapeDtypeStruct((rows, width), BF16),
        jax.ShapeDtypeStruct((3, width), F32),
        jax.ShapeDtypeStruct((poles, owned), F32),
        jax.ShapeDtypeStruct((1, owned), F32),
    )
    held = pl.pallas_call(
        functools.partial(kernel, ctx, dp, scale),
        out_shape=results,
        in_specs=[smem] + [hbm] * 6,
        out_specs=(vmem,) * 4,
        scratch_shapes=scratch,
        compiler_params=pltpu.CompilerParams(
            collective_id=0, has_side_effects=True, vmem_limit_bytes=44 * 1024 * 1024
        ),
        name="conv_block",
    )(
        *(
            pltpu.with_memory_space_constraint(x, pltpu.HBM)
            for x in (lengths, features[0], upstream[0], conv_taps, residues, log_rate, skip_gain[None])
        )
    )
    grad_feats, grad_taps, grad_res, grad_skip = pl.pallas_call(
        write_out,
        out_shape=results,
        in_specs=[vmem] * 4,
        out_specs=(hbm,) * 4,
        scratch_shapes=[pltpu.SemaphoreType.DMA((4,))],
        compiler_params=pltpu.CompilerParams(vmem_limit_bytes=8 * 1024 * 1024),
        name="write_out",
    )(*held)
    return (grad_feats[None], grad_taps, grad_res, grad_skip[0])


def solution(mesh):
    return jax.shard_map(
        per_device,
        mesh=mesh,
        in_specs=(
            P("dp", "ctx", None),
            P("dp", "ctx", None),
            P("dp", None),
            P(),
            P(None, "ctx"),
            P(None, "ctx"),
            P("ctx"),
        ),
        out_specs=(P("dp", "ctx", None), P(), P(None, "ctx"), P("ctx")),
        check_vma=False,
    )
```

```python
import functools
import math

import jax
import jax.numpy as jnp
from jax import lax
from jax.experimental import pallas as pl
from jax.experimental.pallas import tpu as pltpu
from jax.sharding import PartitionSpec as P

MESH = pl.DeviceIdType.MESH
F32 = jnp.float32
BF16 = jnp.bfloat16
LANES = 128
SUBS = 8
GROUP = 4
NEAR = 4


def row_iota(rows):
    return lax.broadcasted_iota(jnp.int32, (rows, LANES), 0)


def lane_low(rows):
    return lax.broadcasted_iota(jnp.int32, (rows, LANES), 1) < LANES // 2


def swap_halves(x):
    return pltpu.roll(x, LANES // 2, 1)


def join_pair(low, high, first):
    mask = lane_low(low.shape[0])
    if first:
        return jnp.where(mask, low, swap_halves(high))
    return jnp.where(mask, swap_halves(low), high)


def split_pair(a, b):
    mask = lane_low(a.shape[0])
    return jnp.where(mask, a, swap_halves(b)), jnp.where(mask, swap_halves(a), b)


def unfold(low, high):
    return jnp.concatenate([join_pair(low, high, True), join_pair(low, high, False)], axis=0)


def fold(x):
    return jnp.where(lane_low(SUBS), x[:SUBS], swap_halves(x[SUBS:]))


def free_of(bounds, low, high):
    clear = None
    for bound in bounds:
        one = (low > bound) | (high < bound)
        clear = one if clear is None else clear & one
    return jnp.where(clear, 1.0, 0.0).astype(F32)


def kernel(
    ctx,
    dp,
    scale,
    lengths,
    feats_in,
    upstream_in,
    taps_in,
    res_in,
    rate_in,
    skip_in,
    grad_feats,
    grad_taps,
    grad_res,
    grad_skip,
    feats,
    upstream,
    taps,
    own_res,
    own_rate,
    own_skip,
    rate_out,
    res_out,
    skip_out,
    rates,
    residues,
    skips,
    halo_out,
    halo,
    first_out,
    first_in,
    carry_out,
    carry_in,
    prefixes,
    joins,
    keeps,
    source,
    gradient,
    output,
    adjoint,
    queries,
    keys,
    values,
    decay,
    coeff,
    powers,
    gain,
    state,
    costate,
    res_sum,
    skip_sum,
    masks,
    edge_out,
    edge_in,
    posts,
    res_part_out,
    res_part_in,
    res_dp_out,
    res_dp_in,
    part_out,
    part_in,
    column_out,
    column_in,
    tap_out,
    tap_in,
    load_sem,
    send_sem,
    recv_sem,
):
    rows, channels = upstream.shape
    poles = own_res.shape[0]
    groups = channels // LANES
    halves = groups // SUBS
    half_rows = rows * SUBS
    pole_rows = poles * SUBS
    steps = rows // SUBS
    window = rows * ctx
    me = lax.axis_index("ctx")
    my_dp = lax.axis_index("dp")

    def peer_of(o):
        return lax.rem(me + o, ctx)

    def far_first(o):
        k, j = lax.div(o, 4), lax.rem(o, 4)
        z_off = 4 + (1 - 2 * lax.rem(k, 2)) * lax.div(k + 1, 2)
        y_off = 2 + (1 - 2 * lax.rem(j, 2)) * lax.div(j + 1, 2)
        y = lax.rem(lax.div(me, 8) + y_off, 4)
        return y * 8 + lax.rem(lax.rem(me, 8) + z_off, 8)

    def dp_peer(o):
        return lax.rem(my_dp + o, dp)

    my_column, my_row = lax.rem(me, 8), lax.div(me, 8)
    my_member = my_row * dp + my_dp

    def member(j):
        return {"ctx": lax.div(j, dp) * 8 + my_column, "dp": lax.rem(j, dp)}

    def other_member(o):
        return lax.rem(my_member + o, ctx)

    def column_peer(o):
        return {"ctx": my_row * 8 + lax.rem(my_column + o, 8)}

    loads = [
        pltpu.make_async_copy(src, dst, load_sem.at[k])
        for k, (src, dst) in enumerate(
            [
                (rate_in, own_rate),
                (res_in, own_res),
                (skip_in, own_skip),
                (taps_in, taps),
                (feats_in, feats),
                (upstream_in, upstream),
            ]
        )
    ]
    for load in loads:
        load.start()

    barrier = pltpu.get_barrier_semaphore()

    def greet(o, c):
        pl.semaphore_signal(barrier, inc=1, device_id={"ctx": far_first(o)}, device_id_type=MESH)
        return c

    lax.fori_loop(0, ctx - 1, greet, 0)

    def greet_member(o, c):
        pl.semaphore_signal(barrier, inc=1, device_id=member(other_member(o)), device_id_type=MESH)
        return c

    lax.fori_loop(1, ctx, greet_member, 0)

    for load in loads[:3]:
        load.wait()
    rate_out[...] = jnp.concatenate([own_rate[:SUBS, :], own_rate[SUBS:, :]], axis=1)
    res_out[...] = jnp.concatenate([own_res[:SUBS, :], own_res[SUBS:, :]], axis=1)
    skip_out[...] = jnp.concatenate([own_skip[...], own_skip[...]], axis=1)

    bounds = [0]
    total = 0
    for j in range(lengths.shape[1] - 1):
        total = total + lengths[0, j]
        bounds.append(total)
    bounds.append(window)
    start = me * rows
    row = row_iota(rows)
    pos = start + row
    flat = 0 * row
    next_one = free_of(bounds, pos + 1, pos + 1)
    next_two = free_of(bounds, pos + 1, pos + 2)
    masks[0] = free_of(bounds, pos, pos)
    masks[1] = free_of(bounds, pos - 1, pos)
    masks[2] = next_one
    masks[3] = next_two

    masks[4] = free_of(bounds, pos + 1, flat + (start + rows - 1))
    masks[5] = free_of(bounds, flat + (start + 1), pos)
    masks[6] = jnp.where(row < rows - 1, next_one, 0.0)
    masks[7] = jnp.where(row < rows - 2, next_two, 0.0)
    masks[8] = free_of(bounds, flat + start, pos)
    masks[9] = free_of(bounds, pos + 1, flat + (start + rows))
    masks[10] = jnp.where(row > 0, masks[0], 0.0)
    masks[11] = jnp.where(row > 1, masks[1], 0.0)

    low16 = lane_low(poles)
    my_rate = jnp.concatenate([own_rate[...], own_rate[...]], axis=1)
    my_decay = jnp.exp(-jnp.exp(my_rate))
    block_decay = jnp.exp(-jnp.exp(my_rate) * rows)

    def join_masks(k, c):
        low = jnp.where(low16, k * rows, (ctx - 1 - k) * rows + 1)
        joins[k] = free_of(bounds, low, low + (rows - 1)) * block_decay
        keeps[k] = free_of(bounds, low, low) * my_decay
        return c

    lax.fori_loop(0, ctx, join_masks, 0)

    my_y, my_z = lax.div(me, 2 * NEAR), lax.rem(lax.div(me, 2), NEAR)

    def group_of(s):
        b, t = lax.div(s, NEAR), lax.rem(s, NEAR)
        upper = lax.div(b, 2)
        z_off = (1 - upper) * (b + 2) + upper * (3 - b)
        y = lax.rem(my_y + t + 2, NEAR)
        return y * NEAR + lax.rem(my_z + z_off, NEAR)

    def at(i, third):
        return pl.multiple_of(third * channels + i * LANES, LANES)

    def strided(s, count, stride_rows):
        return pl.ds(lax.div(s, SUBS) * stride_rows + lax.rem(s, SUBS), count, stride=SUBS)

    for load in loads[3:]:
        load.wait()

    def featured(off):
        lanes = pl.ds(off, LANES)
        f = feats[:, lanes].astype(F32)
        one = masks[10] * pltpu.roll(f, 1, 0)
        two = masks[11] * pltpu.roll(f, 2, 0)
        halo_out[:, lanes] = f[rows - 2 :]
        return taps[0:1, lanes] * f + taps[1:2, lanes] * one + taps[2:3, lanes] * two

    def enter(s, c):
        i = group_of(s)
        query, key, value = (featured(at(i, third)) for third in range(3))
        lanes = pl.ds(at(i, 0), LANES)
        up = upstream[:, lanes].astype(F32)
        keys[:, lanes] = key
        values[:, lanes] = value
        queries[:, lanes] = query[:SUBS]
        source[strided(s, rows, half_rows), :] = (key * value).astype(BF16).astype(F32)
        gradient[strided(s, rows, half_rows), :] = (up * query).astype(BF16).astype(F32)
        return c

    lax.fori_loop(0, groups, enter, 0)

    pl.semaphore_wait(barrier, 2 * (ctx - 1))

    def remote(src, dst, k, to):
        return pltpu.make_async_remote_copy(
            src_ref=src, dst_ref=dst, send_sem=send_sem.at[k], recv_sem=recv_sem.at[k], device_id=to, device_id_type=MESH
        )

    def send_rates(o, c):
        remote(rate_out, rates.at[me], 1, {"ctx": far_first(o)}).start()
        return c

    lax.fori_loop(0, ctx - 1, send_rates, 0)
    halo_copy = remote(halo_out, halo, 0, {"ctx": peer_of(1)})
    halo_copy.start()

    def send_others(o, c):
        remote(res_out, residues.at[me], 2, {"ctx": far_first(o)}).start()
        remote(skip_out, skips.at[me], 3, {"ctx": far_first(o)}).start()
        return c

    lax.fori_loop(0, ctx - 1, send_others, 0)
    rates[pl.ds(me, 1)] = rate_out[...][None]
    residues[pl.ds(me, 1)] = res_out[...][None]
    skips[pl.ds(me, 1)] = skip_out[...][None]

    halo_copy.wait()
    head = row_iota(SUBS)
    on_first = jnp.where(head == 0, masks[0, :SUBS, :], 0.0)
    both_first = jnp.where(head == 0, masks[1, :SUBS, :], 0.0)
    both_second = jnp.where(head == 1, masks[1, :SUBS, :], 0.0)

    def mend(s, c):
        i = group_of(s)
        here = pl.ds(at(i, 0), LANES)
        parts = []
        for third, buf in enumerate((queries, keys, values)):
            lanes = pl.ds(at(i, third), LANES)
            one, two = taps[1:2, lanes], taps[2:3, lanes]
            h1, h2 = halo[1:2, lanes], halo[0:1, lanes]
            parts.append(buf[:SUBS, here] + (on_first * one + both_second * two) * h1 + (both_first * two) * h2)
        query, key, value = parts
        keys[:SUBS, here] = key
        values[:SUBS, here] = value
        up = upstream[: 2 * SUBS, here].astype(F32)[:SUBS]
        source[strided(s, SUBS, half_rows), :] = (key * value).astype(BF16).astype(F32)
        gradient[strided(s, SUBS, half_rows), :] = (up * query).astype(BF16).astype(F32)
        return c

    lax.fori_loop(0, groups, mend, 0, unroll=True)

    def all_slots(buf, sem, slots):
        pltpu.make_async_copy(buf.at[pl.ds(0, slots)], buf.at[pl.ds(0, slots)], sem).wait()

    def wait_all(buf, k, slots):
        all_slots(buf, recv_sem.at[k], slots)

    wait_all(rates, 1, ctx - 1)

    def spread_rates(s, c):
        i = group_of(s)
        decay[strided(s, poles, pole_rows), :] = jnp.exp(-jnp.exp(unfold(rates[2 * i], rates[2 * i + 1])))
        return c

    lax.fori_loop(0, groups, spread_rates, 0, unroll=True)

    def send_slab(out, into, k, to):
        @pl.when(to != me)
        def _():
            remote(out.at[to], into.at[me], k, {"ctx": to}).start()

        @pl.when(to == me)
        def _():
            into[pl.ds(me, 1)] = out[pl.ds(me, 1)]

    def send_slots(out, into, k, low, high):
        def send(s, c):
            i = group_of(s)
            send_slab(out, into, k, 2 * i)
            send_slab(out, into, k, 2 * i + 1)
            return c

        lax.fori_loop(low, high, send, 0)

    for h in range(halves):
        pole_at = pl.ds(h * pole_rows, pole_rows)
        fac = decay[pole_at, :].reshape(poles, SUBS, LANES)

        def chunk(k, carry):
            s, u = carry
            back = steps - 1 - k
            x = source[pl.ds(pl.multiple_of(h * half_rows + k * 64, 64), 64), :].reshape(SUBS, SUBS, LANES)
            g = gradient[pl.ds(pl.multiple_of(h * half_rows + back * 64, 64), 64), :].reshape(SUBS, SUBS, LANES)
            mx = masks[4, pl.ds(pl.multiple_of(k * SUBS, SUBS), SUBS), :]
            mg = masks[5, pl.ds(pl.multiple_of(back * SUBS, SUBS), SUBS), :]
            for t in range(SUBS):
                r = SUBS - 1 - t
                s = s * fac + (x[t] * mx[t : t + 1])[None]
                u = u * fac + (g[r] * mg[r : r + 1])[None]
            return s, u

        zero = jnp.zeros((poles, SUBS, LANES), F32)
        s, u = lax.fori_loop(0, steps, chunk, (zero, zero))
        state[pole_at, :] = s.reshape(pole_rows, LANES)
        costate[pole_at, :] = u.reshape(pole_rows, LANES)

        def pack_first(s, c):
            i = group_of(s)
            low, high = split_pair(state[strided(s, poles, pole_rows), :], costate[strided(s, poles, pole_rows), :])
            first_out[2 * i] = low.astype(BF16)
            first_out[2 * i + 1] = high.astype(BF16)
            return c

        lax.fori_loop(h * SUBS, (h + 1) * SUBS, pack_first, 0, unroll=True)
        send_slots(first_out, first_in, 4, h * SUBS, (h + 1) * SUBS)

    wait_all(residues, 2, ctx - 1)
    wait_all(skips, 3, ctx - 1)

    def spread_others(s, c):
        i = group_of(s)
        coeff[strided(s, poles, pole_rows), :] = unfold(residues[2 * i], residues[2 * i + 1])
        low_s = jnp.broadcast_to(skips[2 * i], (SUBS, LANES))
        high_s = jnp.broadcast_to(skips[2 * i + 1], (SUBS, LANES))
        gain[pl.ds(s, 1), :] = join_pair(low_s, high_s, True)[0:1]
        return c

    lax.fori_loop(0, groups, spread_others, 0, unroll=True)
    state[...] = jnp.zeros_like(state)
    costate[...] = jnp.zeros_like(costate)
    res_sum[...] = jnp.zeros_like(res_sum)
    skip_sum[...] = jnp.zeros_like(skip_sum)

    def raise_powers(h):
        pole_at = pl.ds(h * pole_rows, pole_rows)
        fac = decay[pole_at, :].reshape(poles, SUBS, LANES)

        def step(k, e):
            for t in range(4):
                e = e * fac
                to = pl.multiple_of((h * rows + k * 4 + t) * pole_rows, pole_rows)
                powers[pl.ds(to, pole_rows), :] = e.reshape(pole_rows, LANES)
            return e

        lax.fori_loop(0, rows // 4, step, coeff[pole_at, :].reshape(poles, SUBS, LANES))

    def half_sweep(h):
        both = pl.ds(h * SUBS, SUBS)
        skip = gain[both, :]

        def chunk(k, c):
            back = steps - 1 - k
            at_x = pl.ds(pl.multiple_of(h * half_rows + k * 64, 64), 64)
            at_g = pl.ds(pl.multiple_of(h * half_rows + back * 64, 64), 64)
            x = source[at_x, :].reshape(SUBS, SUBS, LANES)
            gx = gradient[at_x, :].reshape(SUBS, SUBS, LANES)
            g = gradient[at_g, :].reshape(SUBS, SUBS, LANES)
            keep = masks[0, pl.ds(pl.multiple_of(k * SUBS, SUBS), SUBS), :]
            keep_g = masks[2, pl.ds(pl.multiple_of(back * SUBS, SUBS), SUBS), :]
            out = [skip * x[t] for t in range(SUBS)]
            adj = [skip * g[t] for t in range(SUBS)]
            for p in range(0, poles, GROUP):
                here = pl.ds(h * pole_rows + p * SUBS, GROUP * SUBS)
                shape = (GROUP, SUBS, LANES)
                s = state[here, :].reshape(shape)
                u = costate[here, :].reshape(shape)
                fac = decay[here, :].reshape(shape)
                res = coeff[here, :].reshape(shape)
                acc = res_sum[here, :].reshape(shape)
                for t in range(SUBS):
                    r = SUBS - 1 - t
                    s = s * (fac * keep[t : t + 1][None]) + x[t][None]
                    out[t] = out[t] + jnp.sum(res * s, axis=0)
                    acc = acc + s * gx[t][None]
                    u = u * (fac * keep_g[r : r + 1][None]) + g[r][None]
                    adj[r] = adj[r] + jnp.sum(res * u, axis=0)
                state[here, :] = s.reshape(GROUP * SUBS, LANES)
                costate[here, :] = u.reshape(GROUP * SUBS, LANES)
                res_sum[here, :] = acc.reshape(GROUP * SUBS, LANES)
            output[at_x, :] = jnp.stack(out).reshape(SUBS * SUBS, LANES)
            adjoint[at_g, :] = jnp.stack(adj).reshape(SUBS * SUBS, LANES)
            skip_sum[both, :] = skip_sum[both, :] + jnp.sum(x * gx, axis=0)
            return c

        lax.fori_loop(0, steps, chunk, 0)

    raise_powers(0)
    half_sweep(0)
    raise_powers(1)

    wait_all(first_in, 4, ctx - 1)

    def scan(k, w):
        prefixes[k] = w
        here = jnp.where(low16, first_in[k].astype(F32), first_in[ctx - 1 - k].astype(F32))
        return joins[k] * w + here

    lax.fori_loop(0, ctx, scan, jnp.zeros((poles, LANES), F32), unroll=True)

    def pack_carry(k, c):
        carry_out[k] = jnp.where(low16, prefixes[k], prefixes[ctx - 1 - k]).astype(BF16)
        return c

    lax.fori_loop(0, ctx, pack_carry, 0, unroll=True)
    send_slots(carry_out, carry_in, 5, 0, groups)

    half_sweep(1)

    def pack_res(s, c):
        i = group_of(s)
        a = res_sum[strided(s, poles, pole_rows), :]
        low, high = split_pair(a[:SUBS], a[SUBS:])
        res_part_out[2 * i] = low
        res_part_out[2 * i + 1] = high
        return c

    lax.fori_loop(0, groups, pack_res, 0, unroll=True)
    send_slots(res_part_out, res_part_in, 6, 0, groups)

    def carried_terms(k, acc):
        return acc + keeps[k] * prefixes[k] * swap_halves(first_in[k].astype(F32))

    res_carried = fold(lax.fori_loop(0, ctx, carried_terms, jnp.zeros((poles, LANES), F32)))

    wait_all(carry_in, 5, ctx - 1)

    def unpack_carry(s, c):
        i = group_of(s)
        low, high = carry_in[2 * i].astype(F32), carry_in[2 * i + 1].astype(F32)
        state[strided(s, poles, pole_rows), :] = join_pair(low, high, True)
        costate[strided(s, poles, pole_rows), :] = join_pair(low, high, False)
        return c

    lax.fori_loop(0, groups, unpack_carry, 0, unroll=True)

    for h in range(halves):
        pole_at = pl.ds(h * pole_rows, pole_rows)
        s = state[pole_at, :].reshape(poles, SUBS, LANES)
        u = costate[pole_at, :].reshape(poles, SUBS, LANES)

        def add_carry(k, c):
            for j in range(4):
                t = k * 4 + j
                r = rows - 1 - t
                e = powers[pl.ds(pl.multiple_of((h * rows + t) * pole_rows, pole_rows), pole_rows), :]
                e = e.reshape(poles, SUBS, LANES)
                at_t = pl.ds(pl.multiple_of(h * half_rows + t * SUBS, SUBS), SUBS)
                at_r = pl.ds(pl.multiple_of(h * half_rows + r * SUBS, SUBS), SUBS)
                output[at_t, :] = output[at_t, :] + masks[8, pl.ds(t, 1), :] * jnp.sum(e * s, axis=0)
                adjoint[at_r, :] = adjoint[at_r, :] + masks[9, pl.ds(r, 1), :] * jnp.sum(e * u, axis=0)
            return c

        lax.fori_loop(0, rows // 4, add_carry, 0)

    first_keep, first_both, second_both = masks[0, 0:1, :], masks[1, 0:1, :], masks[1, 1:2, :]
    my_x = lax.div(my_dp, 2)

    def team_group(o):
        k, j = lax.div(o, NEAR), lax.rem(o, NEAR)
        x_off = 2 + (1 - 2 * lax.rem(k, 2)) * lax.div(k + 1, 2)
        y_off = 2 + (1 - 2 * lax.rem(j, 2)) * lax.div(j + 1, 2)
        return lax.rem(my_row + y_off, NEAR) * NEAR + lax.rem(my_x + x_off, NEAR)

    def slot_of(i):
        t = lax.rem(lax.div(i, NEAR) + NEAR - my_y + 2, NEAR)
        z_off = lax.rem(lax.rem(i, NEAR) + NEAR - my_z, NEAR)
        upper = lax.div(z_off, 2)
        return ((1 - upper) * (3 - z_off) + upper * (z_off - 2)) * NEAR + t

    def send_part(j):
        remote(part_out.at[j], part_in.at[my_member], 9, member(j)).start()

    first_row, second_row = head == 0, head == 1
    last_row, last_two = head == SUBS - 1, head >= SUBS - 2

    def above(x, after, by):
        edge = last_row if by == 1 else last_two
        return jnp.where(edge, pltpu.roll(after, SUBS - by, 0), pltpu.roll(x, SUBS - by, 0))

    def leave(o):
        i = team_group(o)
        s = slot_of(i)
        here = pl.ds(at(i, 0), LANES)
        thirds = [pl.ds(at(i, third), LANES) for third in range(3)]
        base = lax.div(s, SUBS) * half_rows + lax.rem(s, SUBS)
        sums = [jnp.zeros((SUBS, LANES), F32)] * 9
        after = [jnp.zeros((SUBS, LANES), F32)] * 3
        for pair in reversed(range(rows // 16)):
            rows16 = pl.ds(pair * 16, 16)
            up16 = upstream[rows16, here].astype(F32)
            f16 = [feats[rows16, lanes].astype(F32) for lanes in thirds]
            for half in (1, 0):
                r = pair * 16 + half * SUBS
                tile = pl.ds(r, SUBS)
                picked = pl.ds(base + r * SUBS, SUBS, stride=SUBS)
                out = output[picked, :].astype(BF16).astype(F32)
                mixed = adjoint[picked, :].astype(BF16).astype(F32)
                part = slice(half * SUBS, (half + 1) * SUBS)
                post = [up16[part] * out, mixed * values[tile, here], mixed * keys[tile, here]]
                next_one, next_two = masks[6, tile, :], masks[7, tile, :]
                for third in range(3):
                    f = f16[third][part]
                    posts[tile, thirds[third]] = post[third]
                    sums[3 * third] = sums[3 * third] + post[third] * f
                    sums[3 * third + 1] = sums[3 * third + 1] + next_one * above(post[third], after[third], 1) * f
                    sums[3 * third + 2] = sums[3 * third + 2] + next_two * above(post[third], after[third], 2) * f
                after = post
        for third, lanes in enumerate(thirds):
            edge_out[:, lanes] = after[third][0:2]
            h1, h2 = halo[1:2, lanes], halo[0:1, lanes]
            sums[3 * third + 1] = sums[3 * third + 1] + jnp.where(first_row, after[third] * first_keep * h1, 0.0)
            sums[3 * third + 2] = (
                sums[3 * third + 2]
                + jnp.where(first_row, after[third] * first_both * h2, 0.0)
                + jnp.where(second_row, after[third] * second_both * h1, 0.0)
            )
        sums = [jnp.sum(x, axis=0, keepdims=True) for x in sums]
        top = jnp.concatenate(sums[:SUBS], axis=0)
        rest = jnp.concatenate([sums[SUBS], skip_sum[pl.ds(s, 1), :]] + sums[:6], axis=0)
        low, high = split_pair(top, rest)
        part_out[2 * i] = low
        part_out[2 * i + 1] = high

    def leave_and_send(o, c):
        leave(o)
        j = team_group(o - 1)
        send_part(2 * j)
        send_part(2 * j + 1)
        return c

    leave(0)
    lax.fori_loop(1, groups, leave_and_send, 0)
    mate = my_member + 1 - 2 * lax.rem(my_member, 2)
    send_part(mate)
    part_in[pl.ds(my_member, 1)] = part_out[pl.ds(my_member, 1)]
    edge_copy = remote(edge_out, edge_in, 8, {"ctx": peer_of(ctx - 1)})
    edge_copy.start()

    def sum_slots(buf, count):
        return lax.fori_loop(0, count, lambda k, acc: acc + buf[k], jnp.zeros((SUBS, LANES), F32), unroll=True)

    wait_all(res_part_in, 6, ctx - 1)
    res_dp_out[...] = sum_slots(res_part_in, ctx) + res_carried

    def send_res(o, c):
        remote(res_dp_out, res_dp_in.at[my_dp], 7, {"dp": dp_peer(o)}).start()
        return c

    lax.fori_loop(1, dp, send_res, 0)
    res_dp_in[pl.ds(my_dp, 1)] = res_dp_out[...][None]

    wait_all(part_in, 9, ctx - 1)
    column_out[...] = sum_slots(part_in, ctx)

    def send_column(o, c):
        remote(column_out, column_in.at[my_column], 10, column_peer(o)).start()
        return c

    lax.fori_loop(1, 8, send_column, 0)
    column_in[pl.ds(my_column, 1)] = column_out[...][None]
    wait_all(column_in, 10, 7)
    whole = sum_slots(column_in, 8) * scale
    tap_out[...] = whole

    def send_taps(o, c):
        i = team_group(o)
        for j in (2 * i, 2 * i + 1):
            remote(tap_out, tap_in.at[my_member], 11, member(j)).start()
        return c

    lax.fori_loop(0, groups - 1, send_taps, 0)
    remote(tap_out, tap_in.at[my_member], 11, member(mate)).start()
    tap_in[pl.ds(my_member, 1)] = whole[None]

    edge_copy.wait()

    def finish(i, c):
        thirds = [pl.ds(at(i, third), LANES) for third in range(3)]
        after = [jnp.where(first_row, edge_in[0:1, lanes], edge_in[1:2, lanes]) for lanes in thirds]
        for pair in reversed(range(rows // 16)):
            done = [[], [], []]
            for half in (1, 0):
                tile = pl.ds(pair * 16 + half * SUBS, SUBS)
                one, two = masks[2, tile, :], masks[3, tile, :]
                for third, lanes in enumerate(thirds):
                    post = posts[tile, lanes]
                    back = (
                        taps[0:1, lanes] * post
                        + taps[1:2, lanes] * (one * above(post, after[third], 1))
                        + taps[2:3, lanes] * (two * above(post, after[third], 2))
                    )
                    done[third].insert(0, back)
                    after[third] = post
            for third, lanes in enumerate(thirds):
                grad_feats[pl.ds(pair * 16, 16), lanes] = jnp.concatenate(done[third], axis=0).astype(BF16)
        return c

    lax.fori_loop(0, groups, finish, 0)
    wait_all(res_dp_in, 7, dp - 1)
    res_whole = sum_slots(res_dp_in, dp) * scale
    grad_res[:SUBS, :] = res_whole[:, : LANES // 2]
    grad_res[SUBS:, :] = swap_halves(res_whole)[:, : LANES // 2]
    for k, buf, slots in [
        (1, rates, ctx),
        (2, residues, ctx),
        (3, skips, ctx),
        (4, first_in, ctx),
        (5, carry_in, ctx),
        (6, res_part_in, ctx),
        (7, res_dp_in, dp),
        (9, part_in, ctx),
        (10, column_in, 8),
        (11, tap_in, ctx),
    ]:
        all_slots(buf, send_sem.at[k], slots - 1)

    wait_all(tap_in, 11, ctx - 1)
    grad_skip[...] = swap_halves(tap_in[me])[1:2, : LANES // 2]

    def place_taps(i, c):
        low, high = tap_in[2 * i], tap_in[2 * i + 1]
        first = join_pair(low, high, True)
        last_row = join_pair(low, high, False)[0:1]
        for third in range(3):
            for j in range(3):
                r = third * 3 + j
                grad_taps[j : j + 1, pl.ds(at(i, third), LANES)] = first[r : r + 1] if r < SUBS else last_row
        return c

    lax.fori_loop(0, groups, place_taps, 0, unroll=True)


def write_out(*refs):
    count = (len(refs) - 1) // 2
    sems = refs[-1]
    copies = [pltpu.make_async_copy(refs[k], refs[count + k], sems.at[k]) for k in range(count)]
    for copy in copies:
        copy.start()
    for copy in copies:
        copy.wait()


def per_device(features, upstream, lengths, conv_taps, residues, log_rate, skip_gain):
    rows, width = features.shape[1:]
    channels = upstream.shape[2]
    poles, owned = residues.shape
    ctx = lax.axis_size("ctx")
    dp = lax.axis_size("dp")
    scale = 1.0 / math.sqrt(rows * ctx * dp)
    groups = channels // LANES
    vmem = pl.BlockSpec(memory_space=pltpu.VMEM)
    smem = pl.BlockSpec(memory_space=pltpu.SMEM)
    hbm = pl.BlockSpec(memory_space=pltpu.HBM)
    slab = (ctx, poles, LANES)
    folded = (ctx, SUBS, LANES)
    wide = pltpu.VMEM((rows * groups, LANES), F32)
    per_pole = pltpu.VMEM((poles * groups, LANES), F32)
    scratch = [
        pltpu.VMEM((rows, width), BF16),
        pltpu.VMEM((rows, channels), BF16),
        pltpu.VMEM((3, width), F32),
        pltpu.VMEM((poles, owned), F32),
        pltpu.VMEM((poles, owned), F32),
        pltpu.VMEM((1, owned), F32),
        pltpu.VMEM((SUBS, LANES), F32),
        pltpu.VMEM((SUBS, LANES), F32),
        pltpu.VMEM((1, LANES), F32),
        pltpu.VMEM(folded, F32),
        pltpu.VMEM(folded, F32),
        pltpu.VMEM((ctx, 1, LANES), F32),
        pltpu.VMEM((2, width), F32),
        pltpu.VMEM((2, width), F32),
        pltpu.VMEM(slab, BF16),
        pltpu.VMEM(slab, BF16),
        pltpu.VMEM(slab, BF16),
        pltpu.VMEM(slab, BF16),
        pltpu.VMEM(slab, F32),
        pltpu.VMEM(slab, F32),
        pltpu.VMEM(slab, F32),
        wide,
        wide,
        wide,
        wide,
        pltpu.VMEM((SUBS, channels), F32),
        pltpu.VMEM((rows, channels), F32),
        pltpu.VMEM((rows, channels), F32),
        per_pole,
        per_pole,
        pltpu.VMEM((rows * poles * groups, LANES), F32),
        pltpu.VMEM((groups, LANES), F32),
        per_pole,
        per_pole,
        per_pole,
        pltpu.VMEM((groups, LANES), F32),
        pltpu.VMEM((12, rows, LANES), F32),
        pltpu.VMEM((2, width), F32),
        pltpu.VMEM((2, width), F32),
        pltpu.VMEM((rows, width), F32),
        pltpu.VMEM(folded, F32),
        pltpu.VMEM(folded, F32),
        pltpu.VMEM((SUBS, LANES), F32),
        pltpu.VMEM((dp, SUBS, LANES), F32),
        pltpu.VMEM(folded, F32),
        pltpu.VMEM(folded, F32),
        pltpu.VMEM((SUBS, LANES), F32),
        pltpu.VMEM((8, SUBS, LANES), F32),
        pltpu.VMEM((SUBS, LANES), F32),
        pltpu.VMEM(folded, F32),
        pltpu.SemaphoreType.DMA((6,)),
        pltpu.SemaphoreType.DMA((12,)),
        pltpu.SemaphoreType.DMA((12,)),
    ]
    results = (
        jax.ShapeDtypeStruct((rows, width), BF16),
        jax.ShapeDtypeStruct((3, width), F32),
        jax.ShapeDtypeStruct((poles, owned), F32),
        jax.ShapeDtypeStruct((1, owned), F32),
    )
    held = pl.pallas_call(
        functools.partial(kernel, ctx, dp, scale),
        out_shape=results,
        in_specs=[smem] + [hbm] * 6,
        out_specs=(vmem,) * 4,
        scratch_shapes=scratch,
        compiler_params=pltpu.CompilerParams(
            collective_id=0, has_side_effects=True, vmem_limit_bytes=44 * 1024 * 1024
        ),
        name="conv_block",
    )(
        *(
            pltpu.with_memory_space_constraint(x, pltpu.HBM)
            for x in (lengths, features[0], upstream[0], conv_taps, residues, log_rate, skip_gain[None])
        )
    )
    grad_feats, grad_taps, grad_res, grad_skip = pl.pallas_call(
        write_out,
        out_shape=results,
        in_specs=[vmem] * 4,
        out_specs=(hbm,) * 4,
        scratch_shapes=[pltpu.SemaphoreType.DMA((4,))],
        compiler_params=pltpu.CompilerParams(vmem_limit_bytes=8 * 1024 * 1024),
        name="write_out",
    )(*held)
    return (grad_feats[None], grad_taps, grad_res, grad_skip[0])


def solution(mesh):
    return jax.shard_map(
        per_device,
        mesh=mesh,
        in_specs=(
            P("dp", "ctx", None),
            P("dp", "ctx", None),
            P("dp", None),
            P(),
            P(None, "ctx"),
            P(None, "ctx"),
            P("ctx"),
        ),
        out_specs=(P("dp", "ctx", None), P(), P(None, "ctx"), P("ctx")),
        check_vma=False,
    )
```

```python
import functools
import math

import jax
import jax.numpy as jnp
from jax import lax
from jax.experimental import pallas as pl
from jax.experimental.pallas import tpu as pltpu
from jax.sharding import PartitionSpec as P

MESH = pl.DeviceIdType.MESH
F32 = jnp.float32
BF16 = jnp.bfloat16
LANES = 128
SUBS = 8
GROUP = 4
NEAR = 4


def row_iota(rows):
    return lax.broadcasted_iota(jnp.int32, (rows, LANES), 0)


def lane_low(rows):
    return lax.broadcasted_iota(jnp.int32, (rows, LANES), 1) < LANES // 2


def swap_halves(x):
    return pltpu.roll(x, LANES // 2, 1)


def join_pair(low, high, first):
    mask = lane_low(low.shape[0])
    if first:
        return jnp.where(mask, low, swap_halves(high))
    return jnp.where(mask, swap_halves(low), high)


def split_pair(a, b):
    mask = lane_low(a.shape[0])
    return jnp.where(mask, a, swap_halves(b)), jnp.where(mask, swap_halves(a), b)


def unfold(low, high):
    return jnp.concatenate([join_pair(low, high, True), join_pair(low, high, False)], axis=0)


def fold(x):
    return jnp.where(lane_low(SUBS), x[:SUBS], swap_halves(x[SUBS:]))


FAR_Z = (4, 3, 5, 2, 6, 1, 7, 0)
FAR = (2, 1, 3, 0)


def free_of(bounds, low, high):
    clear = None
    for bound in bounds:
        one = (low > bound) | (high < bound)
        clear = one if clear is None else clear & one
    return jnp.where(clear, 1.0, 0.0).astype(F32)


def kernel(
    ctx,
    dp,
    scale,
    lengths,
    feats_in,
    upstream_in,
    taps_in,
    res_in,
    rate_in,
    skip_in,
    grad_feats,
    grad_taps,
    grad_res,
    grad_skip,
    feats,
    upstream,
    taps,
    own_res,
    own_rate,
    own_skip,
    rate_out,
    res_out,
    skip_out,
    rates,
    residues,
    skips,
    halo_out,
    halo,
    first_out,
    first_in,
    carry_out,
    carry_in,
    prefixes,
    joins,
    keeps,
    source,
    gradient,
    output,
    adjoint,
    queries,
    keys,
    values,
    decay,
    coeff,
    powers,
    gain,
    state,
    costate,
    res_sum,
    skip_sum,
    masks,
    edge_out,
    edge_in,
    posts,
    res_part_out,
    res_part_in,
    res_dp_out,
    res_dp_in,
    part_out,
    part_in,
    column_out,
    column_in,
    tap_out,
    tap_in,
    load_sem,
    send_sem,
    recv_sem,
):
    rows, channels = upstream.shape
    poles = own_res.shape[0]
    groups = channels // LANES
    halves = groups // SUBS
    half_rows = rows * SUBS
    pole_rows = poles * SUBS
    steps = rows // SUBS
    window = rows * ctx
    me = lax.axis_index("ctx")
    my_dp = lax.axis_index("dp")

    def peer_of(o):
        return lax.rem(me + o, ctx)

    def far_first(o):
        k, j = lax.div(o, 4), lax.rem(o, 4)
        z_off = 4 + (1 - 2 * lax.rem(k, 2)) * lax.div(k + 1, 2)
        y_off = 2 + (1 - 2 * lax.rem(j, 2)) * lax.div(j + 1, 2)
        y = lax.rem(lax.div(me, 8) + y_off, 4)
        return y * 8 + lax.rem(lax.rem(me, 8) + z_off, 8)

    def dp_peer(o):
        return lax.rem(my_dp + o, dp)

    my_column, my_row = lax.rem(me, 8), lax.div(me, 8)
    my_member = my_row * dp + my_dp
    my_x, my_core = lax.div(my_dp, 2), lax.rem(my_dp, 2)
    row_at = [lax.rem(my_row + k, 4) for k in range(4)]
    column_at = [lax.rem(my_column + k, 8) for k in range(8)]
    x_at = [lax.rem(my_x + k, 4) * 2 for k in range(4)]
    core_at = [my_core, 1 - my_core]
    far_ctx = [{"ctx": row_at[y] * 8 + column_at[z]} for z in FAR_Z for y in FAR if y or z]
    far_team = [
        {"ctx": row_at[y] * 8 + my_column, "dp": x_at[x] + core_at[c]}
        for x in FAR
        for y in FAR
        for c in (1, 0)
        if x or y or c
    ]

    def member(j):
        return {"ctx": lax.div(j, dp) * 8 + my_column, "dp": lax.rem(j, dp)}

    def column_peer(o):
        return {"ctx": my_row * 8 + lax.rem(my_column + o, 8)}

    loads = [
        pltpu.make_async_copy(src, dst, load_sem.at[k])
        for k, (src, dst) in enumerate(
            [
                (rate_in, own_rate),
                (res_in, own_res),
                (skip_in, own_skip),
                (taps_in, taps),
                (feats_in, feats),
                (upstream_in, upstream),
            ]
        )
    ]
    for load in loads:
        load.start()

    barrier = pltpu.get_barrier_semaphore()

    for to in far_ctx + far_team:
        pl.semaphore_signal(barrier, inc=1, device_id=to, device_id_type=MESH)

    for load in loads[:3]:
        load.wait()
    rate_out[...] = jnp.concatenate([own_rate[:SUBS, :], own_rate[SUBS:, :]], axis=1)
    res_out[...] = jnp.concatenate([own_res[:SUBS, :], own_res[SUBS:, :]], axis=1)
    skip_out[...] = jnp.concatenate([own_skip[...], own_skip[...]], axis=1)

    bounds = [0]
    total = 0
    for j in range(lengths.shape[1] - 1):
        total = total + lengths[0, j]
        bounds.append(total)
    bounds.append(window)
    start = me * rows
    row = row_iota(rows)
    pos = start + row
    flat = 0 * row
    next_one = free_of(bounds, pos + 1, pos + 1)
    next_two = free_of(bounds, pos + 1, pos + 2)
    masks[0] = free_of(bounds, pos, pos)
    masks[1] = free_of(bounds, pos - 1, pos)
    masks[2] = next_one
    masks[3] = next_two

    masks[4] = free_of(bounds, pos + 1, flat + (start + rows - 1))
    masks[5] = free_of(bounds, flat + (start + 1), pos)
    masks[6] = jnp.where(row < rows - 1, next_one, 0.0)
    masks[7] = jnp.where(row < rows - 2, next_two, 0.0)
    masks[8] = free_of(bounds, flat + start, pos)
    masks[9] = free_of(bounds, pos + 1, flat + (start + rows))
    masks[10] = jnp.where(row > 0, masks[0], 0.0)
    masks[11] = jnp.where(row > 1, masks[1], 0.0)

    low16 = lane_low(poles)
    my_rate = jnp.concatenate([own_rate[...], own_rate[...]], axis=1)
    my_decay = jnp.exp(-jnp.exp(my_rate))
    block_decay = jnp.exp(-jnp.exp(my_rate) * rows)

    def join_masks(k, c):
        low = jnp.where(low16, k * rows, (ctx - 1 - k) * rows + 1)
        joins[k] = free_of(bounds, low, low + (rows - 1)) * block_decay
        keeps[k] = free_of(bounds, low, low) * my_decay
        return c

    lax.fori_loop(0, ctx, join_masks, 0)

    my_y, my_z = lax.div(me, 2 * NEAR), lax.rem(lax.div(me, 2), NEAR)

    def group_of(s):
        b, t = lax.div(s, NEAR), lax.rem(s, NEAR)
        upper = lax.div(b, 2)
        z_off = (1 - upper) * (b + 2) + upper * (3 - b)
        y = lax.rem(my_y + t + 2, NEAR)
        return y * NEAR + lax.rem(my_z + z_off, NEAR)

    def at(i, third):
        return pl.multiple_of(third * channels + i * LANES, LANES)

    def strided(s, count, stride_rows):
        return pl.ds(lax.div(s, SUBS) * stride_rows + lax.rem(s, SUBS), count, stride=SUBS)

    for load in loads[3:]:
        load.wait()

    def featured(off):
        lanes = pl.ds(off, LANES)
        f = feats[:, lanes].astype(F32)
        one = masks[10] * pltpu.roll(f, 1, 0)
        two = masks[11] * pltpu.roll(f, 2, 0)
        halo_out[:, lanes] = f[rows - 2 :]
        return taps[0:1, lanes] * f + taps[1:2, lanes] * one + taps[2:3, lanes] * two

    def enter(s, c):
        i = group_of(s)
        query, key, value = (featured(at(i, third)) for third in range(3))
        lanes = pl.ds(at(i, 0), LANES)
        up = upstream[:, lanes].astype(F32)
        keys[:, lanes] = key
        values[:, lanes] = value
        queries[:, lanes] = query[:SUBS]
        source[strided(s, rows, half_rows), :] = (key * value).astype(BF16).astype(F32)
        gradient[strided(s, rows, half_rows), :] = (up * query).astype(BF16).astype(F32)
        return c

    lax.fori_loop(0, groups, enter, 0)

    pl.semaphore_wait(barrier, 2 * (ctx - 1))

    def remote(src, dst, k, to):
        return pltpu.make_async_remote_copy(
            src_ref=src, dst_ref=dst, send_sem=send_sem.at[k], recv_sem=recv_sem.at[k], device_id=to, device_id_type=MESH
        )

    for to in far_ctx:
        remote(rate_out, rates.at[me], 1, to).start()
    halo_copy = remote(halo_out, halo, 0, {"ctx": peer_of(1)})
    halo_copy.start()

    def send_others(o, c):
        remote(res_out, residues.at[me], 2, {"ctx": far_first(o)}).start()
        remote(skip_out, skips.at[me], 3, {"ctx": far_first(o)}).start()
        return c

    lax.fori_loop(0, ctx - 1, send_others, 0)
    rates[pl.ds(me, 1)] = rate_out[...][None]
    residues[pl.ds(me, 1)] = res_out[...][None]
    skips[pl.ds(me, 1)] = skip_out[...][None]

    halo_copy.wait()
    head = row_iota(SUBS)
    on_first = jnp.where(head == 0, masks[0, :SUBS, :], 0.0)
    both_first = jnp.where(head == 0, masks[1, :SUBS, :], 0.0)
    both_second = jnp.where(head == 1, masks[1, :SUBS, :], 0.0)

    def mend(s, c):
        i = group_of(s)
        here = pl.ds(at(i, 0), LANES)
        parts = []
        for third, buf in enumerate((queries, keys, values)):
            lanes = pl.ds(at(i, third), LANES)
            one, two = taps[1:2, lanes], taps[2:3, lanes]
            h1, h2 = halo[1:2, lanes], halo[0:1, lanes]
            parts.append(buf[:SUBS, here] + (on_first * one + both_second * two) * h1 + (both_first * two) * h2)
        query, key, value = parts
        keys[:SUBS, here] = key
        values[:SUBS, here] = value
        up = upstream[: 2 * SUBS, here].astype(F32)[:SUBS]
        source[strided(s, SUBS, half_rows), :] = (key * value).astype(BF16).astype(F32)
        gradient[strided(s, SUBS, half_rows), :] = (up * query).astype(BF16).astype(F32)
        return c

    lax.fori_loop(0, groups, mend, 0, unroll=True)

    def all_slots(buf, sem, slots):
        pltpu.make_async_copy(buf.at[pl.ds(0, slots)], buf.at[pl.ds(0, slots)], sem).wait()

    def wait_all(buf, k, slots):
        all_slots(buf, recv_sem.at[k], slots)

    wait_all(rates, 1, ctx - 1)

    def spread_rates(s, c):
        i = group_of(s)
        decay[strided(s, poles, pole_rows), :] = jnp.exp(-jnp.exp(unfold(rates[2 * i], rates[2 * i + 1])))
        return c

    lax.fori_loop(0, groups, spread_rates, 0, unroll=True)

    def send_slab(out, into, k, to):
        @pl.when(to != me)
        def _():
            remote(out.at[to], into.at[me], k, {"ctx": to}).start()

        @pl.when(to == me)
        def _():
            into[pl.ds(me, 1)] = out[pl.ds(me, 1)]

    def send_slots(out, into, k, low, high):
        def send(s, c):
            i = group_of(s)
            send_slab(out, into, k, 2 * i)
            send_slab(out, into, k, 2 * i + 1)
            return c

        lax.fori_loop(low, high, send, 0)

    for h in range(halves):
        pole_at = pl.ds(h * pole_rows, pole_rows)
        fac = decay[pole_at, :].reshape(poles, SUBS, LANES)

        def chunk(k, carry):
            s, u = carry
            back = steps - 1 - k
            x = source[pl.ds(pl.multiple_of(h * half_rows + k * 64, 64), 64), :].reshape(SUBS, SUBS, LANES)
            g = gradient[pl.ds(pl.multiple_of(h * half_rows + back * 64, 64), 64), :].reshape(SUBS, SUBS, LANES)
            mx = masks[4, pl.ds(pl.multiple_of(k * SUBS, SUBS), SUBS), :]
            mg = masks[5, pl.ds(pl.multiple_of(back * SUBS, SUBS), SUBS), :]
            for t in range(SUBS):
                r = SUBS - 1 - t
                s = s * fac + (x[t] * mx[t : t + 1])[None]
                u = u * fac + (g[r] * mg[r : r + 1])[None]
            return s, u

        zero = jnp.zeros((poles, SUBS, LANES), F32)
        s, u = lax.fori_loop(0, steps, chunk, (zero, zero))
        state[pole_at, :] = s.reshape(pole_rows, LANES)
        costate[pole_at, :] = u.reshape(pole_rows, LANES)

        def pack_first(s, c):
            i = group_of(s)
            low, high = split_pair(state[strided(s, poles, pole_rows), :], costate[strided(s, poles, pole_rows), :])
            first_out[2 * i] = low.astype(BF16)
            first_out[2 * i + 1] = high.astype(BF16)
            return c

        lax.fori_loop(h * SUBS, (h + 1) * SUBS, pack_first, 0, unroll=True)
        send_slots(first_out, first_in, 4, h * SUBS, (h + 1) * SUBS)

    wait_all(residues, 2, ctx - 1)
    wait_all(skips, 3, ctx - 1)

    def spread_others(s, c):
        i = group_of(s)
        coeff[strided(s, poles, pole_rows), :] = unfold(residues[2 * i], residues[2 * i + 1])
        low_s = jnp.broadcast_to(skips[2 * i], (SUBS, LANES))
        high_s = jnp.broadcast_to(skips[2 * i + 1], (SUBS, LANES))
        gain[pl.ds(s, 1), :] = join_pair(low_s, high_s, True)[0:1]
        return c

    lax.fori_loop(0, groups, spread_others, 0, unroll=True)
    state[...] = jnp.zeros_like(state)
    costate[...] = jnp.zeros_like(costate)
    res_sum[...] = jnp.zeros_like(res_sum)
    skip_sum[...] = jnp.zeros_like(skip_sum)

    def raise_powers(h):
        pole_at = pl.ds(h * pole_rows, pole_rows)
        fac = decay[pole_at, :].reshape(poles, SUBS, LANES)
        twice = fac * fac

        def step(k, e):
            for t in range(4):
                to = pl.multiple_of((h * (rows // 2) + k * 4 + t) * pole_rows, pole_rows)
                powers[pl.ds(to, pole_rows), :] = e.reshape(pole_rows, LANES)
                e = e * twice
            return e

        lax.fori_loop(0, rows // 8, step, coeff[pole_at, :].reshape(poles, SUBS, LANES) * fac)

    def half_sweep(h):
        both = pl.ds(h * SUBS, SUBS)
        skip = gain[both, :]

        def chunk(k, c):
            back = steps - 1 - k
            at_x = pl.ds(pl.multiple_of(h * half_rows + k * 64, 64), 64)
            at_g = pl.ds(pl.multiple_of(h * half_rows + back * 64, 64), 64)
            x = source[at_x, :].reshape(SUBS, SUBS, LANES)
            gx = gradient[at_x, :].reshape(SUBS, SUBS, LANES)
            g = gradient[at_g, :].reshape(SUBS, SUBS, LANES)
            keep = masks[0, pl.ds(pl.multiple_of(k * SUBS, SUBS), SUBS), :]
            keep_g = masks[2, pl.ds(pl.multiple_of(back * SUBS, SUBS), SUBS), :]
            out = [skip * x[t] for t in range(SUBS)]
            adj = [skip * g[t] for t in range(SUBS)]
            for p in range(0, poles, GROUP):
                here = pl.ds(h * pole_rows + p * SUBS, GROUP * SUBS)
                shape = (GROUP, SUBS, LANES)
                s = state[here, :].reshape(shape)
                u = costate[here, :].reshape(shape)
                fac = decay[here, :].reshape(shape)
                res = coeff[here, :].reshape(shape)
                acc = res_sum[here, :].reshape(shape)
                for t in range(SUBS):
                    r = SUBS - 1 - t
                    s = s * (fac * keep[t : t + 1][None]) + x[t][None]
                    out[t] = out[t] + jnp.sum(res * s, axis=0)
                    acc = acc + s * gx[t][None]
                    u = u * (fac * keep_g[r : r + 1][None]) + g[r][None]
                    adj[r] = adj[r] + jnp.sum(res * u, axis=0)
                state[here, :] = s.reshape(GROUP * SUBS, LANES)
                costate[here, :] = u.reshape(GROUP * SUBS, LANES)
                res_sum[here, :] = acc.reshape(GROUP * SUBS, LANES)
            output[at_x, :] = jnp.stack(out).reshape(SUBS * SUBS, LANES)
            adjoint[at_g, :] = jnp.stack(adj).reshape(SUBS * SUBS, LANES)
            skip_sum[both, :] = skip_sum[both, :] + jnp.sum(x * gx, axis=0)
            return c

        lax.fori_loop(0, steps, chunk, 0)

    raise_powers(0)
    half_sweep(0)
    raise_powers(1)

    wait_all(first_in, 4, ctx - 1)

    def scan(k, w):
        prefixes[k] = w
        here = jnp.where(low16, first_in[k].astype(F32), first_in[ctx - 1 - k].astype(F32))
        return joins[k] * w + here

    lax.fori_loop(0, ctx, scan, jnp.zeros((poles, LANES), F32), unroll=True)

    def pack_carry(k, c):
        carry_out[k] = jnp.where(low16, prefixes[k], prefixes[ctx - 1 - k]).astype(BF16)
        return c

    lax.fori_loop(0, ctx, pack_carry, 0, unroll=True)
    send_slots(carry_out, carry_in, 5, 0, groups)

    half_sweep(1)

    def pack_res(s, c):
        i = group_of(s)
        a = res_sum[strided(s, poles, pole_rows), :]
        low, high = split_pair(a[:SUBS], a[SUBS:])
        res_part_out[2 * i] = low
        res_part_out[2 * i + 1] = high
        return c

    lax.fori_loop(0, groups, pack_res, 0, unroll=True)
    send_slots(res_part_out, res_part_in, 6, 0, groups)

    def carried_terms(k, acc):
        return acc + keeps[k] * prefixes[k] * swap_halves(first_in[k].astype(F32))

    res_carried = fold(lax.fori_loop(0, ctx, carried_terms, jnp.zeros((poles, LANES), F32)))

    wait_all(carry_in, 5, ctx - 1)

    def unpack_carry(s, c):
        i = group_of(s)
        low, high = carry_in[2 * i].astype(F32), carry_in[2 * i + 1].astype(F32)
        state[strided(s, poles, pole_rows), :] = join_pair(low, high, True)
        costate[strided(s, poles, pole_rows), :] = join_pair(low, high, False)
        return c

    lax.fori_loop(0, groups, unpack_carry, 0, unroll=True)

    for h in range(halves):
        pole_at = pl.ds(h * pole_rows, pole_rows)
        s = state[pole_at, :].reshape(poles, SUBS, LANES)
        u = costate[pole_at, :].reshape(poles, SUBS, LANES)

        fac = decay[pole_at, :].reshape(poles, SUBS, LANES)

        def add_carry(k, c):
            for j in range(4):
                e = powers[pl.ds(pl.multiple_of((h * (rows // 2) + k * 4 + j) * pole_rows, pole_rows), pole_rows), :]
                e = e.reshape(poles, SUBS, LANES)
                for e, t in ((e, k * 8 + 2 * j), (e * fac, k * 8 + 2 * j + 1)):
                    r = rows - 1 - t
                    at_t = pl.ds(pl.multiple_of(h * half_rows + t * SUBS, SUBS), SUBS)
                    at_r = pl.ds(pl.multiple_of(h * half_rows + r * SUBS, SUBS), SUBS)
                    output[at_t, :] = output[at_t, :] + masks[8, pl.ds(t, 1), :] * jnp.sum(e * s, axis=0)
                    adjoint[at_r, :] = adjoint[at_r, :] + masks[9, pl.ds(r, 1), :] * jnp.sum(e * u, axis=0)
            return c

        lax.fori_loop(0, rows // 8, add_carry, 0)

    first_keep, first_both, second_both = masks[0, 0:1, :], masks[1, 0:1, :], masks[1, 1:2, :]
    def team_group(o):
        k, j = lax.div(o, NEAR), lax.rem(o, NEAR)
        x_off = 2 + (1 - 2 * lax.rem(k, 2)) * lax.div(k + 1, 2)
        y_off = 2 + (1 - 2 * lax.rem(j, 2)) * lax.div(j + 1, 2)
        return lax.rem(my_row + y_off, NEAR) * NEAR + lax.rem(my_x + x_off, NEAR)

    def slot_of(i):
        t = lax.rem(lax.div(i, NEAR) + NEAR - my_y + 2, NEAR)
        z_off = lax.rem(lax.rem(i, NEAR) + NEAR - my_z, NEAR)
        upper = lax.div(z_off, 2)
        return ((1 - upper) * (3 - z_off) + upper * (z_off - 2)) * NEAR + t

    def send_part(j):
        remote(part_out.at[j], part_in.at[my_member], 9, member(j)).start()

    first_row, second_row = head == 0, head == 1
    last_row, last_two = head == SUBS - 1, head >= SUBS - 2

    def above(x, after, by):
        edge = last_row if by == 1 else last_two
        return jnp.where(edge, pltpu.roll(after, SUBS - by, 0), pltpu.roll(x, SUBS - by, 0))

    def leave(o):
        i = team_group(o)
        s = slot_of(i)
        here = pl.ds(at(i, 0), LANES)
        thirds = [pl.ds(at(i, third), LANES) for third in range(3)]
        base = lax.div(s, SUBS) * half_rows + lax.rem(s, SUBS)
        sums = [jnp.zeros((SUBS, LANES), F32)] * 9
        after = [jnp.zeros((SUBS, LANES), F32)] * 3
        for pair in reversed(range(rows // 16)):
            rows16 = pl.ds(pair * 16, 16)
            up16 = upstream[rows16, here].astype(F32)
            f16 = [feats[rows16, lanes].astype(F32) for lanes in thirds]
            for half in (1, 0):
                r = pair * 16 + half * SUBS
                tile = pl.ds(r, SUBS)
                picked = pl.ds(base + r * SUBS, SUBS, stride=SUBS)
                out = output[picked, :].astype(BF16).astype(F32)
                mixed = adjoint[picked, :].astype(BF16).astype(F32)
                part = slice(half * SUBS, (half + 1) * SUBS)
                post = [up16[part] * out, mixed * values[tile, here], mixed * keys[tile, here]]
                next_one, next_two = masks[6, tile, :], masks[7, tile, :]
                for third in range(3):
                    f = f16[third][part]
                    posts[tile, thirds[third]] = post[third]
                    sums[3 * third] = sums[3 * third] + post[third] * f
                    sums[3 * third + 1] = sums[3 * third + 1] + next_one * above(post[third], after[third], 1) * f
                    sums[3 * third + 2] = sums[3 * third + 2] + next_two * above(post[third], after[third], 2) * f
                after = post
        for third, lanes in enumerate(thirds):
            edge_out[:, lanes] = after[third][0:2]
            h1, h2 = halo[1:2, lanes], halo[0:1, lanes]
            sums[3 * third + 1] = sums[3 * third + 1] + jnp.where(first_row, after[third] * first_keep * h1, 0.0)
            sums[3 * third + 2] = (
                sums[3 * third + 2]
                + jnp.where(first_row, after[third] * first_both * h2, 0.0)
                + jnp.where(second_row, after[third] * second_both * h1, 0.0)
            )
        sums = [jnp.sum(x, axis=0, keepdims=True) for x in sums]
        top = jnp.concatenate(sums[:SUBS], axis=0)
        rest = jnp.concatenate([sums[SUBS], skip_sum[pl.ds(s, 1), :]] + sums[:6], axis=0)
        low, high = split_pair(top, rest)
        part_out[2 * i] = low
        part_out[2 * i + 1] = high

    def send_group(o):
        j = team_group(o)
        send_part(2 * j)
        send_part(2 * j + 1)

    def send_and_leave(k, c):
        send_group(2 * k - 2)
        send_group(2 * k - 1)
        leave(2 * k)
        leave(2 * k + 1)
        return c

    leave(0)
    leave(1)
    lax.fori_loop(1, groups // 2, send_and_leave, 0)
    send_group(groups - 2)
    mate = my_member + 1 - 2 * lax.rem(my_member, 2)
    send_part(mate)
    part_in[pl.ds(my_member, 1)] = part_out[pl.ds(my_member, 1)]
    edge_copy = remote(edge_out, edge_in, 8, {"ctx": peer_of(ctx - 1)})
    edge_copy.start()

    def sum_slots(buf, count):
        return lax.fori_loop(0, count, lambda k, acc: acc + buf[k], jnp.zeros((SUBS, LANES), F32), unroll=True)

    wait_all(res_part_in, 6, ctx - 1)
    res_dp_out[...] = sum_slots(res_part_in, ctx) + res_carried

    def send_res(o, c):
        remote(res_dp_out, res_dp_in.at[my_dp], 7, {"dp": dp_peer(o)}).start()
        return c

    lax.fori_loop(1, dp, send_res, 0)
    res_dp_in[pl.ds(my_dp, 1)] = res_dp_out[...][None]

    wait_all(part_in, 9, ctx - 1)
    column_out[...] = sum_slots(part_in, ctx)

    def send_column(o, c):
        remote(column_out, column_in.at[my_column], 10, column_peer(o)).start()
        return c

    lax.fori_loop(1, 8, send_column, 0)
    column_in[pl.ds(my_column, 1)] = column_out[...][None]
    wait_all(column_in, 10, 7)
    whole = sum_slots(column_in, 8) * scale
    tap_out[...] = whole

    for to in far_team:
        remote(tap_out, tap_in.at[my_member], 11, to).start()
    tap_in[pl.ds(my_member, 1)] = whole[None]

    edge_copy.wait()

    def finish(i, c):
        thirds = [pl.ds(at(i, third), LANES) for third in range(3)]
        after = [jnp.where(first_row, edge_in[0:1, lanes], edge_in[1:2, lanes]) for lanes in thirds]
        for pair in reversed(range(rows // 16)):
            done = [[], [], []]
            for half in (1, 0):
                tile = pl.ds(pair * 16 + half * SUBS, SUBS)
                one, two = masks[2, tile, :], masks[3, tile, :]
                for third, lanes in enumerate(thirds):
                    post = posts[tile, lanes]
                    back = (
                        taps[0:1, lanes] * post
                        + taps[1:2, lanes] * (one * above(post, after[third], 1))
                        + taps[2:3, lanes] * (two * above(post, after[third], 2))
                    )
                    done[third].insert(0, back)
                    after[third] = post
            for third, lanes in enumerate(thirds):
                grad_feats[pl.ds(pair * 16, 16), lanes] = jnp.concatenate(done[third], axis=0).astype(BF16)
        return c

    lax.fori_loop(0, groups, finish, 0)
    wait_all(res_dp_in, 7, dp - 1)
    res_whole = sum_slots(res_dp_in, dp) * scale
    grad_res[:SUBS, :] = res_whole[:, : LANES // 2]
    grad_res[SUBS:, :] = swap_halves(res_whole)[:, : LANES // 2]
    for k, buf, slots in [
        (1, rates, ctx),
        (2, residues, ctx),
        (3, skips, ctx),
        (4, first_in, ctx),
        (5, carry_in, ctx),
        (6, res_part_in, ctx),
        (7, res_dp_in, dp),
        (9, part_in, ctx),
        (10, column_in, 8),
        (11, tap_in, ctx),
    ]:
        all_slots(buf, send_sem.at[k], slots - 1)

    wait_all(tap_in, 11, ctx - 1)
    grad_skip[...] = swap_halves(tap_in[me])[1:2, : LANES // 2]

    def place_taps(i, c):
        low, high = tap_in[2 * i], tap_in[2 * i + 1]
        first = join_pair(low, high, True)
        last_row = join_pair(low, high, False)[0:1]
        for third in range(3):
            for j in range(3):
                r = third * 3 + j
                grad_taps[j : j + 1, pl.ds(at(i, third), LANES)] = first[r : r + 1] if r < SUBS else last_row
        return c

    lax.fori_loop(0, groups, place_taps, 0, unroll=True)


def write_out(*refs):
    count = (len(refs) - 1) // 2
    sems = refs[-1]
    copies = [pltpu.make_async_copy(refs[k], refs[count + k], sems.at[k]) for k in range(count)]
    for copy in copies:
        copy.start()
    for copy in copies:
        copy.wait()


def per_device(features, upstream, lengths, conv_taps, residues, log_rate, skip_gain):
    rows, width = features.shape[1:]
    channels = upstream.shape[2]
    poles, owned = residues.shape
    ctx = lax.axis_size("ctx")
    dp = lax.axis_size("dp")
    scale = 1.0 / math.sqrt(rows * ctx * dp)
    groups = channels // LANES
    vmem = pl.BlockSpec(memory_space=pltpu.VMEM)
    smem = pl.BlockSpec(memory_space=pltpu.SMEM)
    hbm = pl.BlockSpec(memory_space=pltpu.HBM)
    slab = (ctx, poles, LANES)
    folded = (ctx, SUBS, LANES)
    wide = pltpu.VMEM((rows * groups, LANES), F32)
    per_pole = pltpu.VMEM((poles * groups, LANES), F32)
    scratch = [
        pltpu.VMEM((rows, width), BF16),
        pltpu.VMEM((rows, channels), BF16),
        pltpu.VMEM((3, width), F32),
        pltpu.VMEM((poles, owned), F32),
        pltpu.VMEM((poles, owned), F32),
        pltpu.VMEM((1, owned), F32),
        pltpu.VMEM((SUBS, LANES), F32),
        pltpu.VMEM((SUBS, LANES), F32),
        pltpu.VMEM((1, LANES), F32),
        pltpu.VMEM(folded, F32),
        pltpu.VMEM(folded, F32),
        pltpu.VMEM((ctx, 1, LANES), F32),
        pltpu.VMEM((2, width), F32),
        pltpu.VMEM((2, width), F32),
        pltpu.VMEM(slab, BF16),
        pltpu.VMEM(slab, BF16),
        pltpu.VMEM(slab, BF16),
        pltpu.VMEM(slab, BF16),
        pltpu.VMEM(slab, F32),
        pltpu.VMEM(slab, F32),
        pltpu.VMEM(slab, F32),
        wide,
        wide,
        wide,
        wide,
        pltpu.VMEM((SUBS, channels), F32),
        pltpu.VMEM((rows, channels), F32),
        pltpu.VMEM((rows, channels), F32),
        per_pole,
        per_pole,
        pltpu.VMEM((rows // 2 * poles * groups, LANES), F32),
        pltpu.VMEM((groups, LANES), F32),
        per_pole,
        per_pole,
        per_pole,
        pltpu.VMEM((groups, LANES), F32),
        pltpu.VMEM((12, rows, LANES), F32),
        pltpu.VMEM((2, width), F32),
        pltpu.VMEM((2, width), F32),
        pltpu.VMEM((rows, width), F32),
        pltpu.VMEM(folded, F32),
        pltpu.VMEM(folded, F32),
        pltpu.VMEM((SUBS, LANES), F32),
        pltpu.VMEM((dp, SUBS, LANES), F32),
        pltpu.VMEM(folded, F32),
        pltpu.VMEM(folded, F32),
        pltpu.VMEM((SUBS, LANES), F32),
        pltpu.VMEM((8, SUBS, LANES), F32),
        pltpu.VMEM((SUBS, LANES), F32),
        pltpu.VMEM(folded, F32),
        pltpu.SemaphoreType.DMA((6,)),
        pltpu.SemaphoreType.DMA((12,)),
        pltpu.SemaphoreType.DMA((12,)),
    ]
    results = (
        jax.ShapeDtypeStruct((rows, width), BF16),
        jax.ShapeDtypeStruct((3, width), F32),
        jax.ShapeDtypeStruct((poles, owned), F32),
        jax.ShapeDtypeStruct((1, owned), F32),
    )
    held = pl.pallas_call(
        functools.partial(kernel, ctx, dp, scale),
        out_shape=results,
        in_specs=[smem] + [hbm] * 6,
        out_specs=(vmem,) * 4,
        scratch_shapes=scratch,
        compiler_params=pltpu.CompilerParams(
            collective_id=0, has_side_effects=True, vmem_limit_bytes=44 * 1024 * 1024
        ),
        name="conv_block",
    )(
        *(
            pltpu.with_memory_space_constraint(x, pltpu.HBM)
            for x in (lengths, features[0], upstream[0], conv_taps, residues, log_rate, skip_gain[None])
        )
    )
    grad_feats, grad_taps, grad_res, grad_skip = pl.pallas_call(
        write_out,
        out_shape=results,
        in_specs=[vmem] * 4,
        out_specs=(hbm,) * 4,
        scratch_shapes=[pltpu.SemaphoreType.DMA((4,))],
        compiler_params=pltpu.CompilerParams(vmem_limit_bytes=8 * 1024 * 1024),
        name="write_out",
    )(*held)
    return (grad_feats[None], grad_taps, grad_res, grad_skip[0])


def solution(mesh):
    return jax.shard_map(
        per_device,
        mesh=mesh,
        in_specs=(
            P("dp", "ctx", None),
            P("dp", "ctx", None),
            P("dp", None),
            P(),
            P(None, "ctx"),
            P(None, "ctx"),
            P("ctx"),
        ),
        out_specs=(P("dp", "ctx", None), P(), P(None, "ctx"), P("ctx")),
        check_vma=False,
    )
```

```python
import functools
import math

import jax
import jax.numpy as jnp
from jax import lax
from jax.experimental import pallas as pl
from jax.experimental.pallas import tpu as pltpu
from jax.sharding import PartitionSpec as P

MESH = pl.DeviceIdType.MESH
F32 = jnp.float32
BF16 = jnp.bfloat16
LANES = 128
SUBS = 8
GROUP = 4
NEAR = 4


def row_iota(rows):
    return lax.broadcasted_iota(jnp.int32, (rows, LANES), 0)


def lane_low(rows):
    return lax.broadcasted_iota(jnp.int32, (rows, LANES), 1) < LANES // 2


def swap_halves(x):
    return pltpu.roll(x, LANES // 2, 1)


def join_pair(low, high, first):
    mask = lane_low(low.shape[0])
    if first:
        return jnp.where(mask, low, swap_halves(high))
    return jnp.where(mask, swap_halves(low), high)


def split_pair(a, b):
    mask = lane_low(a.shape[0])
    return jnp.where(mask, a, swap_halves(b)), jnp.where(mask, swap_halves(a), b)


def unfold(low, high):
    return jnp.concatenate([join_pair(low, high, True), join_pair(low, high, False)], axis=0)


def fold(x):
    return jnp.where(lane_low(SUBS), x[:SUBS], swap_halves(x[SUBS:]))


FAR_Z = (4, 3, 5, 2, 6, 1, 7, 0)
FAR = (2, 1, 3, 0)


def free_of(bounds, low, high):
    clear = None
    for bound in bounds:
        one = (low > bound) | (high < bound)
        clear = one if clear is None else clear & one
    return jnp.where(clear, 1.0, 0.0).astype(F32)


def kernel(
    ctx,
    dp,
    scale,
    lengths,
    feats_in,
    upstream_in,
    taps_in,
    res_in,
    rate_in,
    skip_in,
    grad_feats,
    grad_taps,
    grad_res,
    grad_skip,
    feats,
    upstream,
    taps,
    own_res,
    own_rate,
    own_skip,
    rate_out,
    res_out,
    skip_out,
    rates,
    residues,
    skips,
    halo_out,
    halo,
    first_out,
    first_in,
    carry_out,
    carry_in,
    prefixes,
    joins,
    keeps,
    source,
    gradient,
    output,
    adjoint,
    queries,
    keys,
    values,
    decay,
    coeff,
    powers,
    gain,
    state,
    costate,
    res_sum,
    skip_sum,
    masks,
    edge_out,
    edge_in,
    posts,
    res_part_out,
    res_part_in,
    res_dp_out,
    res_dp_in,
    part_out,
    part_in,
    column_out,
    column_in,
    tap_out,
    tap_in,
    load_sem,
    send_sem,
    recv_sem,
):
    rows, channels = upstream.shape
    poles = own_res.shape[0]
    groups = channels // LANES
    halves = groups // SUBS
    half_rows = rows * SUBS
    pole_rows = poles * SUBS
    steps = rows // SUBS
    window = rows * ctx
    me = lax.axis_index("ctx")
    my_dp = lax.axis_index("dp")

    def peer_of(o):
        return lax.rem(me + o, ctx)

    def far_first(o):
        k, j = lax.div(o, 4), lax.rem(o, 4)
        z_off = 4 + (1 - 2 * lax.rem(k, 2)) * lax.div(k + 1, 2)
        y_off = 2 + (1 - 2 * lax.rem(j, 2)) * lax.div(j + 1, 2)
        y = lax.rem(lax.div(me, 8) + y_off, 4)
        return y * 8 + lax.rem(lax.rem(me, 8) + z_off, 8)

    def dp_peer(o):
        return lax.rem(my_dp + o, dp)

    my_column, my_row = lax.rem(me, 8), lax.div(me, 8)
    my_member = my_row * dp + my_dp
    my_x, my_core = lax.div(my_dp, 2), lax.rem(my_dp, 2)
    row_at = [lax.rem(my_row + k, 4) for k in range(4)]
    column_at = [lax.rem(my_column + k, 8) for k in range(8)]
    x_at = [lax.rem(my_x + k, 4) * 2 for k in range(4)]
    core_at = [my_core, 1 - my_core]
    far_ctx = [{"ctx": row_at[y] * 8 + column_at[z]} for z in FAR_Z for y in FAR if y or z]
    far_team = [
        {"ctx": row_at[y] * 8 + my_column, "dp": x_at[x] + core_at[c]}
        for x in FAR
        for y in FAR
        for c in (1, 0)
        if x or y or c
    ]

    def member(j):
        return {"ctx": lax.div(j, dp) * 8 + my_column, "dp": lax.rem(j, dp)}

    def column_peer(o):
        return {"ctx": my_row * 8 + lax.rem(my_column + o, 8)}

    loads = [
        pltpu.make_async_copy(src, dst, load_sem.at[k])
        for k, (src, dst) in enumerate(
            [
                (rate_in, own_rate),
                (res_in, own_res),
                (skip_in, own_skip),
                (taps_in, taps),
                (feats_in, feats),
                (upstream_in, upstream),
            ]
        )
    ]
    for load in loads:
        load.start()

    barrier = pltpu.get_barrier_semaphore()

    for to in far_ctx + far_team:
        pl.semaphore_signal(barrier, inc=1, device_id=to, device_id_type=MESH)

    for load in loads[:3]:
        load.wait()
    rate_out[...] = jnp.concatenate([own_rate[:SUBS, :], own_rate[SUBS:, :]], axis=1)
    res_out[...] = jnp.concatenate([own_res[:SUBS, :], own_res[SUBS:, :]], axis=1)
    skip_out[...] = jnp.concatenate([own_skip[...], own_skip[...]], axis=1)

    bounds = [0]
    total = 0
    for j in range(lengths.shape[1] - 1):
        total = total + lengths[0, j]
        bounds.append(total)
    bounds.append(window)
    start = me * rows
    row = row_iota(rows)
    pos = start + row
    flat = 0 * row
    next_one = free_of(bounds, pos + 1, pos + 1)
    next_two = free_of(bounds, pos + 1, pos + 2)
    masks[0] = free_of(bounds, pos, pos)
    masks[1] = free_of(bounds, pos - 1, pos)
    masks[2] = next_one
    masks[3] = next_two

    masks[10] = jnp.where(row > 0, masks[0], 0.0)
    masks[11] = jnp.where(row > 1, masks[1], 0.0)

    my_y, my_z = lax.div(me, 2 * NEAR), lax.rem(lax.div(me, 2), NEAR)

    def group_of(s):
        b, t = lax.div(s, NEAR), lax.rem(s, NEAR)
        upper = lax.div(b, 2)
        z_off = (1 - upper) * (b + 2) + upper * (3 - b)
        y = lax.rem(my_y + t + 2, NEAR)
        return y * NEAR + lax.rem(my_z + z_off, NEAR)

    def at(i, third):
        return pl.multiple_of(third * channels + i * LANES, LANES)

    def strided(s, count, stride_rows):
        return pl.ds(lax.div(s, SUBS) * stride_rows + lax.rem(s, SUBS), count, stride=SUBS)

    for load in loads[3:]:
        load.wait()

    def featured(off):
        lanes = pl.ds(off, LANES)
        f = feats[:, lanes].astype(F32)
        one = masks[10] * pltpu.roll(f, 1, 0)
        two = masks[11] * pltpu.roll(f, 2, 0)
        halo_out[:, lanes] = f[rows - 2 :]
        return taps[0:1, lanes] * f + taps[1:2, lanes] * one + taps[2:3, lanes] * two

    def enter(s, c):
        i = group_of(s)
        query, key, value = (featured(at(i, third)) for third in range(3))
        lanes = pl.ds(at(i, 0), LANES)
        up = upstream[:, lanes].astype(F32)
        keys[:, lanes] = key
        values[:, lanes] = value
        queries[:, lanes] = query[:SUBS]
        source[strided(s, rows, half_rows), :] = (key * value).astype(BF16).astype(F32)
        gradient[strided(s, rows, half_rows), :] = (up * query).astype(BF16).astype(F32)
        return c

    lax.fori_loop(0, groups, enter, 0)

    pl.semaphore_wait(barrier, 2 * (ctx - 1))

    def remote(src, dst, k, to):
        return pltpu.make_async_remote_copy(
            src_ref=src, dst_ref=dst, send_sem=send_sem.at[k], recv_sem=recv_sem.at[k], device_id=to, device_id_type=MESH
        )

    for to in far_ctx:
        remote(rate_out, rates.at[me], 1, to).start()
    halo_copy = remote(halo_out, halo, 0, {"ctx": peer_of(1)})
    halo_copy.start()

    def send_others(o, c):
        remote(res_out, residues.at[me], 2, {"ctx": far_first(o)}).start()
        remote(skip_out, skips.at[me], 3, {"ctx": far_first(o)}).start()
        return c

    lax.fori_loop(0, ctx - 1, send_others, 0)
    rates[pl.ds(me, 1)] = rate_out[...][None]
    residues[pl.ds(me, 1)] = res_out[...][None]
    skips[pl.ds(me, 1)] = skip_out[...][None]

    masks[4] = free_of(bounds, pos + 1, flat + (start + rows - 1))
    masks[5] = free_of(bounds, flat + (start + 1), pos)
    masks[6] = jnp.where(row < rows - 1, next_one, 0.0)
    masks[7] = jnp.where(row < rows - 2, next_two, 0.0)
    masks[8] = free_of(bounds, flat + start, pos)
    masks[9] = free_of(bounds, pos + 1, flat + (start + rows))

    low16 = lane_low(poles)
    my_rate = jnp.concatenate([own_rate[...], own_rate[...]], axis=1)
    my_decay = jnp.exp(-jnp.exp(my_rate))
    block_decay = jnp.exp(-jnp.exp(my_rate) * rows)

    def join_masks(k, c):
        low = jnp.where(low16, k * rows, (ctx - 1 - k) * rows + 1)
        joins[k] = free_of(bounds, low, low + (rows - 1)) * block_decay
        keeps[k] = free_of(bounds, low, low) * my_decay
        return c

    lax.fori_loop(0, ctx, join_masks, 0)

    halo_copy.wait()
    head = row_iota(SUBS)
    on_first = jnp.where(head == 0, masks[0, :SUBS, :], 0.0)
    both_first = jnp.where(head == 0, masks[1, :SUBS, :], 0.0)
    both_second = jnp.where(head == 1, masks[1, :SUBS, :], 0.0)

    def mend(s, c):
        i = group_of(s)
        here = pl.ds(at(i, 0), LANES)
        parts = []
        for third, buf in enumerate((queries, keys, values)):
            lanes = pl.ds(at(i, third), LANES)
            one, two = taps[1:2, lanes], taps[2:3, lanes]
            h1, h2 = halo[1:2, lanes], halo[0:1, lanes]
            parts.append(buf[:SUBS, here] + (on_first * one + both_second * two) * h1 + (both_first * two) * h2)
        query, key, value = parts
        keys[:SUBS, here] = key
        values[:SUBS, here] = value
        up = upstream[: 2 * SUBS, here].astype(F32)[:SUBS]
        source[strided(s, SUBS, half_rows), :] = (key * value).astype(BF16).astype(F32)
        gradient[strided(s, SUBS, half_rows), :] = (up * query).astype(BF16).astype(F32)
        return c

    lax.fori_loop(0, groups, mend, 0, unroll=True)

    def all_slots(buf, sem, slots):
        pltpu.make_async_copy(buf.at[pl.ds(0, slots)], buf.at[pl.ds(0, slots)], sem).wait()

    def wait_all(buf, k, slots):
        all_slots(buf, recv_sem.at[k], slots)

    wait_all(rates, 1, ctx - 1)

    def spread_rates(s, c):
        i = group_of(s)
        decay[strided(s, poles, pole_rows), :] = jnp.exp(-jnp.exp(unfold(rates[2 * i], rates[2 * i + 1])))
        return c

    lax.fori_loop(0, groups, spread_rates, 0, unroll=True)

    own_slot = 14

    def send_slots(out, into, k, low, high):
        for s in range(low, high):
            b, t = divmod(s, NEAR)
            i = row_at[(t + 2) % NEAR] * NEAR + lax.rem(my_z + (2, 3, 1, 0)[b], NEAR)
            if s == own_slot:
                mate = me + 1 - 2 * lax.rem(me, 2)
                remote(out.at[mate], into.at[me], k, {"ctx": mate}).start()
                into[pl.ds(me, 1)] = out[pl.ds(me, 1)]
            else:
                for j in (2 * i, 2 * i + 1):
                    remote(out.at[j], into.at[me], k, {"ctx": j}).start()

    for h in range(halves):
        pole_at = pl.ds(h * pole_rows, pole_rows)
        fac = decay[pole_at, :].reshape(poles, SUBS, LANES)

        def chunk(k, carry):
            s, u = carry
            back = steps - 1 - k
            x = source[pl.ds(pl.multiple_of(h * half_rows + k * 64, 64), 64), :].reshape(SUBS, SUBS, LANES)
            g = gradient[pl.ds(pl.multiple_of(h * half_rows + back * 64, 64), 64), :].reshape(SUBS, SUBS, LANES)
            mx = masks[4, pl.ds(pl.multiple_of(k * SUBS, SUBS), SUBS), :]
            mg = masks[5, pl.ds(pl.multiple_of(back * SUBS, SUBS), SUBS), :]
            for t in range(SUBS):
                r = SUBS - 1 - t
                s = s * fac + (x[t] * mx[t : t + 1])[None]
                u = u * fac + (g[r] * mg[r : r + 1])[None]
            return s, u

        zero = jnp.zeros((poles, SUBS, LANES), F32)
        s, u = lax.fori_loop(0, steps, chunk, (zero, zero))
        state[pole_at, :] = s.reshape(pole_rows, LANES)
        costate[pole_at, :] = u.reshape(pole_rows, LANES)

        def pack_first(s, c):
            i = group_of(s)
            low, high = split_pair(state[strided(s, poles, pole_rows), :], costate[strided(s, poles, pole_rows), :])
            first_out[2 * i] = low.astype(BF16)
            first_out[2 * i + 1] = high.astype(BF16)
            return c

        lax.fori_loop(h * SUBS, (h + 1) * SUBS, pack_first, 0, unroll=True)
        send_slots(first_out, first_in, 4, h * SUBS, (h + 1) * SUBS)

    wait_all(residues, 2, ctx - 1)
    wait_all(skips, 3, ctx - 1)

    def spread_others(s, c):
        i = group_of(s)
        coeff[strided(s, poles, pole_rows), :] = unfold(residues[2 * i], residues[2 * i + 1])
        low_s = jnp.broadcast_to(skips[2 * i], (SUBS, LANES))
        high_s = jnp.broadcast_to(skips[2 * i + 1], (SUBS, LANES))
        gain[pl.ds(s, 1), :] = join_pair(low_s, high_s, True)[0:1]
        return c

    lax.fori_loop(0, groups, spread_others, 0, unroll=True)
    state[...] = jnp.zeros_like(state)
    costate[...] = jnp.zeros_like(costate)
    res_sum[...] = jnp.zeros_like(res_sum)
    skip_sum[...] = jnp.zeros_like(skip_sum)

    def raise_powers(h):
        pole_at = pl.ds(h * pole_rows, pole_rows)
        fac = decay[pole_at, :].reshape(poles, SUBS, LANES)
        twice = fac * fac

        def step(k, e):
            for t in range(4):
                to = pl.multiple_of((h * (rows // 2) + k * 4 + t) * pole_rows, pole_rows)
                powers[pl.ds(to, pole_rows), :] = e.reshape(pole_rows, LANES)
                e = e * twice
            return e

        lax.fori_loop(0, rows // 8, step, coeff[pole_at, :].reshape(poles, SUBS, LANES) * fac)

    def half_sweep(h):
        both = pl.ds(h * SUBS, SUBS)
        skip = gain[both, :]

        def chunk(k, c):
            back = steps - 1 - k
            at_x = pl.ds(pl.multiple_of(h * half_rows + k * 64, 64), 64)
            at_g = pl.ds(pl.multiple_of(h * half_rows + back * 64, 64), 64)
            x = source[at_x, :].reshape(SUBS, SUBS, LANES)
            gx = gradient[at_x, :].reshape(SUBS, SUBS, LANES)
            g = gradient[at_g, :].reshape(SUBS, SUBS, LANES)
            keep = masks[0, pl.ds(pl.multiple_of(k * SUBS, SUBS), SUBS), :]
            keep_g = masks[2, pl.ds(pl.multiple_of(back * SUBS, SUBS), SUBS), :]
            out = [skip * x[t] for t in range(SUBS)]
            adj = [skip * g[t] for t in range(SUBS)]
            for p in range(0, poles, GROUP):
                here = pl.ds(h * pole_rows + p * SUBS, GROUP * SUBS)
                shape = (GROUP, SUBS, LANES)
                s = state[here, :].reshape(shape)
                u = costate[here, :].reshape(shape)
                fac = decay[here, :].reshape(shape)
                res = coeff[here, :].reshape(shape)
                acc = res_sum[here, :].reshape(shape)
                for t in range(SUBS):
                    r = SUBS - 1 - t
                    s = s * (fac * keep[t : t + 1][None]) + x[t][None]
                    out[t] = out[t] + jnp.sum(res * s, axis=0)
                    acc = acc + s * gx[t][None]
                    u = u * (fac * keep_g[r : r + 1][None]) + g[r][None]
                    adj[r] = adj[r] + jnp.sum(res * u, axis=0)
                state[here, :] = s.reshape(GROUP * SUBS, LANES)
                costate[here, :] = u.reshape(GROUP * SUBS, LANES)
                res_sum[here, :] = acc.reshape(GROUP * SUBS, LANES)
            output[at_x, :] = jnp.stack(out).reshape(SUBS * SUBS, LANES)
            adjoint[at_g, :] = jnp.stack(adj).reshape(SUBS * SUBS, LANES)
            skip_sum[both, :] = skip_sum[both, :] + jnp.sum(x * gx, axis=0)
            return c

        lax.fori_loop(0, steps, chunk, 0)

    raise_powers(0)
    half_sweep(0)
    raise_powers(1)

    wait_all(first_in, 4, ctx - 1)

    def scan(k, w):
        prefixes[k] = w
        here = jnp.where(low16, first_in[k].astype(F32), first_in[ctx - 1 - k].astype(F32))
        return joins[k] * w + here

    lax.fori_loop(0, ctx, scan, jnp.zeros((poles, LANES), F32), unroll=True)

    def pack_carry(k, c):
        carry_out[k] = jnp.where(low16, prefixes[k], prefixes[ctx - 1 - k]).astype(BF16)
        return c

    lax.fori_loop(0, ctx, pack_carry, 0, unroll=True)
    send_slots(carry_out, carry_in, 5, 0, groups)

    half_sweep(1)

    def pack_res(s, c):
        i = group_of(s)
        a = res_sum[strided(s, poles, pole_rows), :]
        low, high = split_pair(a[:SUBS], a[SUBS:])
        res_part_out[2 * i] = low
        res_part_out[2 * i + 1] = high
        return c

    lax.fori_loop(0, groups, pack_res, 0, unroll=True)
    send_slots(res_part_out, res_part_in, 6, 0, groups)

    def carried_terms(k, acc):
        return acc + keeps[k] * prefixes[k] * swap_halves(first_in[k].astype(F32))

    res_carried = fold(lax.fori_loop(0, ctx, carried_terms, jnp.zeros((poles, LANES), F32)))

    wait_all(carry_in, 5, ctx - 1)

    def unpack_carry(s, c):
        i = group_of(s)
        low, high = carry_in[2 * i].astype(F32), carry_in[2 * i + 1].astype(F32)
        state[strided(s, poles, pole_rows), :] = join_pair(low, high, True)
        costate[strided(s, poles, pole_rows), :] = join_pair(low, high, False)
        return c

    lax.fori_loop(0, groups, unpack_carry, 0, unroll=True)

    for h in range(halves):
        pole_at = pl.ds(h * pole_rows, pole_rows)
        s = state[pole_at, :].reshape(poles, SUBS, LANES)
        u = costate[pole_at, :].reshape(poles, SUBS, LANES)

        fac = decay[pole_at, :].reshape(poles, SUBS, LANES)

        def add_carry(k, c):
            for j in range(4):
                e = powers[pl.ds(pl.multiple_of((h * (rows // 2) + k * 4 + j) * pole_rows, pole_rows), pole_rows), :]
                e = e.reshape(poles, SUBS, LANES)
                for e, t in ((e, k * 8 + 2 * j), (e * fac, k * 8 + 2 * j + 1)):
                    r = rows - 1 - t
                    at_t = pl.ds(pl.multiple_of(h * half_rows + t * SUBS, SUBS), SUBS)
                    at_r = pl.ds(pl.multiple_of(h * half_rows + r * SUBS, SUBS), SUBS)
                    output[at_t, :] = output[at_t, :] + masks[8, pl.ds(t, 1), :] * jnp.sum(e * s, axis=0)
                    adjoint[at_r, :] = adjoint[at_r, :] + masks[9, pl.ds(r, 1), :] * jnp.sum(e * u, axis=0)
            return c

        lax.fori_loop(0, rows // 8, add_carry, 0)

    first_keep, first_both, second_both = masks[0, 0:1, :], masks[1, 0:1, :], masks[1, 1:2, :]
    def team_group(o):
        k, j = lax.div(o, NEAR), lax.rem(o, NEAR)
        x_off = 2 + (1 - 2 * lax.rem(k, 2)) * lax.div(k + 1, 2)
        y_off = 2 + (1 - 2 * lax.rem(j, 2)) * lax.div(j + 1, 2)
        return lax.rem(my_row + y_off, NEAR) * NEAR + lax.rem(my_x + x_off, NEAR)

    def slot_of(i):
        t = lax.rem(lax.div(i, NEAR) + NEAR - my_y + 2, NEAR)
        z_off = lax.rem(lax.rem(i, NEAR) + NEAR - my_z, NEAR)
        upper = lax.div(z_off, 2)
        return ((1 - upper) * (3 - z_off) + upper * (z_off - 2)) * NEAR + t

    def send_part(j):
        remote(part_out.at[j], part_in.at[my_member], 9, member(j)).start()

    first_row, second_row = head == 0, head == 1
    last_row, last_two = head == SUBS - 1, head >= SUBS - 2

    def above(x, after, by):
        edge = last_row if by == 1 else last_two
        return jnp.where(edge, pltpu.roll(after, SUBS - by, 0), pltpu.roll(x, SUBS - by, 0))

    def leave(o):
        i = team_group(o)
        s = slot_of(i)
        here = pl.ds(at(i, 0), LANES)
        thirds = [pl.ds(at(i, third), LANES) for third in range(3)]
        base = lax.div(s, SUBS) * half_rows + lax.rem(s, SUBS)
        sums = [jnp.zeros((SUBS, LANES), F32)] * 9
        after = [jnp.zeros((SUBS, LANES), F32)] * 3
        for pair in reversed(range(rows // 16)):
            rows16 = pl.ds(pair * 16, 16)
            up16 = upstream[rows16, here].astype(F32)
            f16 = [feats[rows16, lanes].astype(F32) for lanes in thirds]
            for half in (1, 0):
                r = pair * 16 + half * SUBS
                tile = pl.ds(r, SUBS)
                picked = pl.ds(base + r * SUBS, SUBS, stride=SUBS)
                out = output[picked, :].astype(BF16).astype(F32)
                mixed = adjoint[picked, :].astype(BF16).astype(F32)
                part = slice(half * SUBS, (half + 1) * SUBS)
                post = [up16[part] * out, mixed * values[tile, here], mixed * keys[tile, here]]
                next_one, next_two = masks[6, tile, :], masks[7, tile, :]
                for third in range(3):
                    f = f16[third][part]
                    posts[tile, thirds[third]] = post[third]
                    sums[3 * third] = sums[3 * third] + post[third] * f
                    sums[3 * third + 1] = sums[3 * third + 1] + next_one * above(post[third], after[third], 1) * f
                    sums[3 * third + 2] = sums[3 * third + 2] + next_two * above(post[third], after[third], 2) * f
                after = post
        for third, lanes in enumerate(thirds):
            edge_out[:, lanes] = after[third][0:2]
            h1, h2 = halo[1:2, lanes], halo[0:1, lanes]
            sums[3 * third + 1] = sums[3 * third + 1] + jnp.where(first_row, after[third] * first_keep * h1, 0.0)
            sums[3 * third + 2] = (
                sums[3 * third + 2]
                + jnp.where(first_row, after[third] * first_both * h2, 0.0)
                + jnp.where(second_row, after[third] * second_both * h1, 0.0)
            )
        sums = [jnp.sum(x, axis=0, keepdims=True) for x in sums]
        top = jnp.concatenate(sums[:SUBS], axis=0)
        rest = jnp.concatenate([sums[SUBS], skip_sum[pl.ds(s, 1), :]] + sums[:6], axis=0)
        low, high = split_pair(top, rest)
        part_out[2 * i] = low
        part_out[2 * i + 1] = high

    def send_group(o):
        j = team_group(o)
        send_part(2 * j)
        send_part(2 * j + 1)

    def send_and_leave(k, c):
        send_group(2 * k - 2)
        send_group(2 * k - 1)
        leave(2 * k)
        leave(2 * k + 1)
        return c

    leave(0)
    leave(1)
    lax.fori_loop(1, groups // 2, send_and_leave, 0)
    send_group(groups - 2)
    mate = my_member + 1 - 2 * lax.rem(my_member, 2)
    send_part(mate)
    part_in[pl.ds(my_member, 1)] = part_out[pl.ds(my_member, 1)]
    edge_copy = remote(edge_out, edge_in, 8, {"ctx": peer_of(ctx - 1)})
    edge_copy.start()

    def sum_slots(buf, count):
        return lax.fori_loop(0, count, lambda k, acc: acc + buf[k], jnp.zeros((SUBS, LANES), F32), unroll=True)

    wait_all(res_part_in, 6, ctx - 1)
    res_dp_out[...] = sum_slots(res_part_in, ctx) + res_carried

    def send_res(o, c):
        remote(res_dp_out, res_dp_in.at[my_dp], 7, {"dp": dp_peer(o)}).start()
        return c

    lax.fori_loop(1, dp, send_res, 0)
    res_dp_in[pl.ds(my_dp, 1)] = res_dp_out[...][None]

    wait_all(part_in, 9, ctx - 1)
    column_out[...] = sum_slots(part_in, ctx)

    def send_column(o, c):
        remote(column_out, column_in.at[my_column], 10, column_peer(o)).start()
        return c

    lax.fori_loop(1, 8, send_column, 0)
    column_in[pl.ds(my_column, 1)] = column_out[...][None]
    wait_all(column_in, 10, 7)
    whole = sum_slots(column_in, 8) * scale
    tap_out[...] = whole

    for to in far_team:
        remote(tap_out, tap_in.at[my_member], 11, to).start()
    tap_in[pl.ds(my_member, 1)] = whole[None]

    edge_copy.wait()

    def finish(i, c):
        thirds = [pl.ds(at(i, third), LANES) for third in range(3)]
        after = [jnp.where(first_row, edge_in[0:1, lanes], edge_in[1:2, lanes]) for lanes in thirds]
        for pair in reversed(range(rows // 16)):
            done = [[], [], []]
            for half in (1, 0):
                tile = pl.ds(pair * 16 + half * SUBS, SUBS)
                one, two = masks[2, tile, :], masks[3, tile, :]
                for third, lanes in enumerate(thirds):
                    post = posts[tile, lanes]
                    back = (
                        taps[0:1, lanes] * post
                        + taps[1:2, lanes] * (one * above(post, after[third], 1))
                        + taps[2:3, lanes] * (two * above(post, after[third], 2))
                    )
                    done[third].insert(0, back)
                    after[third] = post
            for third, lanes in enumerate(thirds):
                grad_feats[pl.ds(pair * 16, 16), lanes] = jnp.concatenate(done[third], axis=0).astype(BF16)
        return c

    lax.fori_loop(0, groups, finish, 0)
    wait_all(res_dp_in, 7, dp - 1)
    res_whole = sum_slots(res_dp_in, dp) * scale
    grad_res[:SUBS, :] = res_whole[:, : LANES // 2]
    grad_res[SUBS:, :] = swap_halves(res_whole)[:, : LANES // 2]
    for k, buf, slots in [
        (1, rates, ctx),
        (2, residues, ctx),
        (3, skips, ctx),
        (4, first_in, ctx),
        (5, carry_in, ctx),
        (6, res_part_in, ctx),
        (7, res_dp_in, dp),
        (9, part_in, ctx),
        (10, column_in, 8),
        (11, tap_in, ctx),
    ]:
        all_slots(buf, send_sem.at[k], slots - 1)

    wait_all(tap_in, 11, ctx - 1)
    grad_skip[...] = swap_halves(tap_in[me])[1:2, : LANES // 2]

    def place_taps(i, c):
        low, high = tap_in[2 * i], tap_in[2 * i + 1]
        first = join_pair(low, high, True)
        last_row = join_pair(low, high, False)[0:1]
        for third in range(3):
            for j in range(3):
                r = third * 3 + j
                grad_taps[j : j + 1, pl.ds(at(i, third), LANES)] = first[r : r + 1] if r < SUBS else last_row
        return c

    lax.fori_loop(0, groups, place_taps, 0, unroll=True)


def write_out(*refs):
    count = (len(refs) - 1) // 2
    sems = refs[-1]
    copies = [pltpu.make_async_copy(refs[k], refs[count + k], sems.at[k]) for k in range(1, count)]
    quarter = refs[0].shape[0] // 4
    for k in range(4):
        part = pl.ds(k * quarter, quarter)
        copies.append(pltpu.make_async_copy(refs[0].at[part], refs[count].at[part], sems.at[count + k]))
    for copy in copies:
        copy.start()
    for copy in copies:
        copy.wait()


def per_device(features, upstream, lengths, conv_taps, residues, log_rate, skip_gain):
    rows, width = features.shape[1:]
    channels = upstream.shape[2]
    poles, owned = residues.shape
    ctx = lax.axis_size("ctx")
    dp = lax.axis_size("dp")
    scale = 1.0 / math.sqrt(rows * ctx * dp)
    groups = channels // LANES
    vmem = pl.BlockSpec(memory_space=pltpu.VMEM)
    smem = pl.BlockSpec(memory_space=pltpu.SMEM)
    hbm = pl.BlockSpec(memory_space=pltpu.HBM)
    slab = (ctx, poles, LANES)
    folded = (ctx, SUBS, LANES)
    wide = pltpu.VMEM((rows * groups, LANES), F32)
    per_pole = pltpu.VMEM((poles * groups, LANES), F32)
    scratch = [
        pltpu.VMEM((rows, width), BF16),
        pltpu.VMEM((rows, channels), BF16),
        pltpu.VMEM((3, width), F32),
        pltpu.VMEM((poles, owned), F32),
        pltpu.VMEM((poles, owned), F32),
        pltpu.VMEM((1, owned), F32),
        pltpu.VMEM((SUBS, LANES), F32),
        pltpu.VMEM((SUBS, LANES), F32),
        pltpu.VMEM((1, LANES), F32),
        pltpu.VMEM(folded, F32),
        pltpu.VMEM(folded, F32),
        pltpu.VMEM((ctx, 1, LANES), F32),
        pltpu.VMEM((2, width), F32),
        pltpu.VMEM((2, width), F32),
        pltpu.VMEM(slab, BF16),
        pltpu.VMEM(slab, BF16),
        pltpu.VMEM(slab, BF16),
        pltpu.VMEM(slab, BF16),
        pltpu.VMEM(slab, F32),
        pltpu.VMEM(slab, F32),
        pltpu.VMEM(slab, F32),
        wide,
        wide,
        wide,
        wide,
        pltpu.VMEM((SUBS, channels), F32),
        pltpu.VMEM((rows, channels), F32),
        pltpu.VMEM((rows, channels), F32),
        per_pole,
        per_pole,
        pltpu.VMEM((rows // 2 * poles * groups, LANES), F32),
        pltpu.VMEM((groups, LANES), F32),
        per_pole,
        per_pole,
        per_pole,
        pltpu.VMEM((groups, LANES), F32),
        pltpu.VMEM((12, rows, LANES), F32),
        pltpu.VMEM((2, width), F32),
        pltpu.VMEM((2, width), F32),
        pltpu.VMEM((rows, width), F32),
        pltpu.VMEM(folded, F32),
        pltpu.VMEM(folded, F32),
        pltpu.VMEM((SUBS, LANES), F32),
        pltpu.VMEM((dp, SUBS, LANES), F32),
        pltpu.VMEM(folded, F32),
        pltpu.VMEM(folded, F32),
        pltpu.VMEM((SUBS, LANES), F32),
        pltpu.VMEM((8, SUBS, LANES), F32),
        pltpu.VMEM((SUBS, LANES), F32),
        pltpu.VMEM(folded, F32),
        pltpu.SemaphoreType.DMA((6,)),
        pltpu.SemaphoreType.DMA((12,)),
        pltpu.SemaphoreType.DMA((12,)),
    ]
    results = (
        jax.ShapeDtypeStruct((rows, width), BF16),
        jax.ShapeDtypeStruct((3, width), F32),
        jax.ShapeDtypeStruct((poles, owned), F32),
        jax.ShapeDtypeStruct((1, owned), F32),
    )
    held = pl.pallas_call(
        functools.partial(kernel, ctx, dp, scale),
        out_shape=results,
        in_specs=[smem] + [hbm] * 6,
        out_specs=(vmem,) * 4,
        scratch_shapes=scratch,
        compiler_params=pltpu.CompilerParams(
            collective_id=0, has_side_effects=True, vmem_limit_bytes=44 * 1024 * 1024
        ),
        name="conv_block",
    )(
        *(
            pltpu.with_memory_space_constraint(x, pltpu.HBM)
            for x in (lengths, features[0], upstream[0], conv_taps, residues, log_rate, skip_gain[None])
        )
    )
    grad_feats, grad_taps, grad_res, grad_skip = pl.pallas_call(
        write_out,
        out_shape=results,
        in_specs=[vmem] * 4,
        out_specs=(hbm,) * 4,
        scratch_shapes=[pltpu.SemaphoreType.DMA((8,))],
        compiler_params=pltpu.CompilerParams(vmem_limit_bytes=8 * 1024 * 1024),
        name="write_out",
    )(*held)
    return (grad_feats[None], grad_taps, grad_res, grad_skip[0])


def solution(mesh):
    return jax.shard_map(
        per_device,
        mesh=mesh,
        in_specs=(
            P("dp", "ctx", None),
            P("dp", "ctx", None),
            P("dp", None),
            P(),
            P(None, "ctx"),
            P(None, "ctx"),
            P("ctx"),
        ),
        out_specs=(P("dp", "ctx", None), P(), P(None, "ctx"), P("ctx")),
        check_vma=False,
    )
```

```python
import functools
import math

import jax
import jax.numpy as jnp
from jax import lax
from jax.experimental import pallas as pl
from jax.experimental.pallas import tpu as pltpu
from jax.sharding import PartitionSpec as P

MESH = pl.DeviceIdType.MESH
F32 = jnp.float32
BF16 = jnp.bfloat16
LANES = 128
SUBS = 8
GROUP = 4
NEAR = 4


def row_iota(rows):
    return lax.broadcasted_iota(jnp.int32, (rows, LANES), 0)


def lane_low(rows):
    return lax.broadcasted_iota(jnp.int32, (rows, LANES), 1) < LANES // 2


def swap_halves(x):
    return pltpu.roll(x, LANES // 2, 1)


def join_pair(low, high, first):
    mask = lane_low(low.shape[0])
    if first:
        return jnp.where(mask, low, swap_halves(high))
    return jnp.where(mask, swap_halves(low), high)


def split_pair(a, b):
    mask = lane_low(a.shape[0])
    return jnp.where(mask, a, swap_halves(b)), jnp.where(mask, swap_halves(a), b)


def unfold(low, high):
    return jnp.concatenate([join_pair(low, high, True), join_pair(low, high, False)], axis=0)


def fold(x):
    return jnp.where(lane_low(SUBS), x[:SUBS], swap_halves(x[SUBS:]))


FAR_Z = (4, 3, 5, 2, 6, 1, 7, 0)
FAR = (2, 1, 3, 0)
TEAM_X = sum(v << (2 * k) for k, v in enumerate((2, 2, 2, 1, 3, 2, 0, 1, 1, 3, 3, 1, 3, 0, 0, 0)))
TEAM_Y = sum(v << (2 * k) for k, v in enumerate((2, 1, 3, 2, 2, 0, 2, 1, 3, 1, 3, 0, 0, 1, 3, 0)))


def free_of(bounds, low, high):
    clear = None
    for bound in bounds:
        one = (low > bound) | (high < bound)
        clear = one if clear is None else clear & one
    return jnp.where(clear, 1.0, 0.0).astype(F32)


def kernel(
    ctx,
    dp,
    scale,
    lengths,
    feats_in,
    upstream_in,
    taps_in,
    res_in,
    rate_in,
    skip_in,
    grad_feats,
    grad_taps,
    grad_res,
    grad_skip,
    feats,
    upstream,
    taps,
    own_res,
    own_rate,
    own_skip,
    rate_out,
    res_out,
    skip_out,
    rates,
    residues,
    skips,
    halo_out,
    halo,
    first_out,
    first_in,
    carry_out,
    carry_in,
    prefixes,
    joins,
    keeps,
    source,
    gradient,
    output,
    adjoint,
    queries,
    keys,
    values,
    decay,
    coeff,
    powers,
    gain,
    state,
    costate,
    res_sum,
    skip_sum,
    masks,
    edge_out,
    edge_in,
    posts,
    res_part_out,
    res_part_in,
    res_dp_out,
    res_dp_in,
    part_out,
    part_in,
    column_out,
    column_in,
    tap_out,
    tap_in,
    load_sem,
    send_sem,
    recv_sem,
):
    rows, channels = upstream.shape
    poles = own_res.shape[0]
    groups = channels // LANES
    halves = groups // SUBS
    half_rows = rows * SUBS
    pole_rows = poles * SUBS
    steps = rows // SUBS
    window = rows * ctx
    me = lax.axis_index("ctx")
    my_dp = lax.axis_index("dp")

    def peer_of(o):
        return lax.rem(me + o, ctx)

    def far_first(o):
        k, j = lax.div(o, 4), lax.rem(o, 4)
        z_off = 4 + (1 - 2 * lax.rem(k, 2)) * lax.div(k + 1, 2)
        y_off = 2 + (1 - 2 * lax.rem(j, 2)) * lax.div(j + 1, 2)
        y = lax.rem(lax.div(me, 8) + y_off, 4)
        return y * 8 + lax.rem(lax.rem(me, 8) + z_off, 8)

    def dp_peer(o):
        return lax.rem(my_dp + o, dp)

    my_column, my_row = lax.rem(me, 8), lax.div(me, 8)
    my_member = my_row * dp + my_dp
    my_x, my_core = lax.div(my_dp, 2), lax.rem(my_dp, 2)
    row_at = [lax.rem(my_row + k, 4) for k in range(4)]
    column_at = [lax.rem(my_column + k, 8) for k in range(8)]
    x_at = [lax.rem(my_x + k, 4) * 2 for k in range(4)]
    core_at = [my_core, 1 - my_core]
    far_ctx = [{"ctx": row_at[y] * 8 + column_at[z]} for z in FAR_Z for y in FAR if y or z]
    far_team = [
        {"ctx": row_at[y] * 8 + my_column, "dp": x_at[x] + core_at[c]}
        for x in FAR
        for y in FAR
        for c in (1, 0)
        if x or y or c
    ]

    def member(j):
        return {"ctx": lax.div(j, dp) * 8 + my_column, "dp": lax.rem(j, dp)}

    def column_peer(o):
        return {"ctx": my_row * 8 + lax.rem(my_column + o, 8)}

    loads = [
        pltpu.make_async_copy(src, dst, load_sem.at[k])
        for k, (src, dst) in enumerate(
            [
                (rate_in, own_rate),
                (res_in, own_res),
                (skip_in, own_skip),
                (taps_in, taps),
                (feats_in, feats),
                (upstream_in, upstream),
            ]
        )
    ]
    for load in loads:
        load.start()

    barrier = pltpu.get_barrier_semaphore()

    for to in far_ctx + far_team:
        pl.semaphore_signal(barrier, inc=1, device_id=to, device_id_type=MESH)

    for load in loads[:3]:
        load.wait()
    rate_out[...] = jnp.concatenate([own_rate[:SUBS, :], own_rate[SUBS:, :]], axis=1)
    res_out[...] = jnp.concatenate([own_res[:SUBS, :], own_res[SUBS:, :]], axis=1)
    skip_out[...] = jnp.concatenate([own_skip[...], own_skip[...]], axis=1)

    pl.semaphore_wait(barrier, 2 * (ctx - 1))

    def remote(src, dst, k, to):
        return pltpu.make_async_remote_copy(
            src_ref=src, dst_ref=dst, send_sem=send_sem.at[k], recv_sem=recv_sem.at[k], device_id=to, device_id_type=MESH
        )

    for to in far_ctx:
        remote(rate_out, rates.at[me], 1, to).start()
    for load in loads[3:]:
        load.wait()
    halo_out[...] = feats[rows - 16 :, :].astype(F32)[14:]
    halo_copy = remote(halo_out, halo, 0, {"ctx": peer_of(1)})

    def send_others(o, c):
        remote(res_out, residues.at[me], 2, {"ctx": far_first(o)}).start()
        remote(skip_out, skips.at[me], 3, {"ctx": far_first(o)}).start()
        return c

    lax.fori_loop(0, ctx - 1, send_others, 0)
    halo_copy.start()
    rates[pl.ds(me, 1)] = rate_out[...][None]
    residues[pl.ds(me, 1)] = res_out[...][None]
    skips[pl.ds(me, 1)] = skip_out[...][None]

    bounds = [0]
    total = 0
    for j in range(lengths.shape[1] - 1):
        total = total + lengths[0, j]
        bounds.append(total)
    bounds.append(window)
    start = me * rows
    row = row_iota(rows)
    pos = start + row
    flat = 0 * row
    next_one = free_of(bounds, pos + 1, pos + 1)
    next_two = free_of(bounds, pos + 1, pos + 2)
    masks[0] = free_of(bounds, pos, pos)
    masks[1] = free_of(bounds, pos - 1, pos)
    masks[2] = next_one
    masks[3] = next_two

    masks[10] = jnp.where(row > 0, masks[0], 0.0)
    masks[11] = jnp.where(row > 1, masks[1], 0.0)

    my_y, my_z = lax.div(me, 2 * NEAR), lax.rem(lax.div(me, 2), NEAR)

    def group_of(s):
        b, t = lax.div(s, NEAR), lax.rem(s, NEAR)
        upper = lax.div(b, 2)
        z_off = (1 - upper) * (b + 2) + upper * (3 - b)
        y = lax.rem(my_y + t + 2, NEAR)
        return y * NEAR + lax.rem(my_z + z_off, NEAR)

    def at(i, third):
        return pl.multiple_of(third * channels + i * LANES, LANES)

    def strided(s, count, stride_rows):
        return pl.ds(lax.div(s, SUBS) * stride_rows + lax.rem(s, SUBS), count, stride=SUBS)

    def featured(off):
        lanes = pl.ds(off, LANES)
        f = feats[:, lanes].astype(F32)
        one = masks[10] * pltpu.roll(f, 1, 0)
        two = masks[11] * pltpu.roll(f, 2, 0)
        return taps[0:1, lanes] * f + taps[1:2, lanes] * one + taps[2:3, lanes] * two

    def enter(s, c):
        i = group_of(s)
        query, key, value = (featured(at(i, third)) for third in range(3))
        lanes = pl.ds(at(i, 0), LANES)
        up = upstream[:, lanes].astype(F32)
        keys[:, lanes] = key
        values[:, lanes] = value
        queries[:, lanes] = query[:SUBS]
        source[strided(s, rows, half_rows), :] = (key * value).astype(BF16).astype(F32)
        gradient[strided(s, rows, half_rows), :] = (up * query).astype(BF16).astype(F32)
        return c

    lax.fori_loop(0, groups, enter, 0)

    masks[4] = free_of(bounds, pos + 1, flat + (start + rows - 1))
    masks[5] = free_of(bounds, flat + (start + 1), pos)
    masks[6] = jnp.where(row < rows - 1, next_one, 0.0)
    masks[7] = jnp.where(row < rows - 2, next_two, 0.0)
    masks[8] = free_of(bounds, flat + start, pos)
    masks[9] = free_of(bounds, pos + 1, flat + (start + rows))

    low16 = lane_low(poles)
    my_rate = jnp.concatenate([own_rate[...], own_rate[...]], axis=1)
    my_decay = jnp.exp(-jnp.exp(my_rate))
    block_decay = jnp.exp(-jnp.exp(my_rate) * rows)

    def join_masks(k, c):
        low = jnp.where(low16, k * rows, (ctx - 1 - k) * rows + 1)
        joins[k] = free_of(bounds, low, low + (rows - 1)) * block_decay
        keeps[k] = free_of(bounds, low, low) * my_decay
        return c

    lax.fori_loop(0, ctx, join_masks, 0)

    halo_copy.wait()
    head = row_iota(SUBS)
    on_first = jnp.where(head == 0, masks[0, :SUBS, :], 0.0)
    both_first = jnp.where(head == 0, masks[1, :SUBS, :], 0.0)
    both_second = jnp.where(head == 1, masks[1, :SUBS, :], 0.0)

    def mend(s, c):
        i = group_of(s)
        here = pl.ds(at(i, 0), LANES)
        parts = []
        for third, buf in enumerate((queries, keys, values)):
            lanes = pl.ds(at(i, third), LANES)
            one, two = taps[1:2, lanes], taps[2:3, lanes]
            h1, h2 = halo[1:2, lanes], halo[0:1, lanes]
            parts.append(buf[:SUBS, here] + (on_first * one + both_second * two) * h1 + (both_first * two) * h2)
        query, key, value = parts
        keys[:SUBS, here] = key
        values[:SUBS, here] = value
        up = upstream[: 2 * SUBS, here].astype(F32)[:SUBS]
        source[strided(s, SUBS, half_rows), :] = (key * value).astype(BF16).astype(F32)
        gradient[strided(s, SUBS, half_rows), :] = (up * query).astype(BF16).astype(F32)
        return c

    lax.fori_loop(0, groups, mend, 0, unroll=True)

    def all_slots(buf, sem, slots):
        pltpu.make_async_copy(buf.at[pl.ds(0, slots)], buf.at[pl.ds(0, slots)], sem).wait()

    def wait_all(buf, k, slots):
        all_slots(buf, recv_sem.at[k], slots)

    wait_all(rates, 1, ctx - 1)

    def spread_rates(s, c):
        i = group_of(s)
        decay[strided(s, poles, pole_rows), :] = jnp.exp(-jnp.exp(unfold(rates[2 * i], rates[2 * i + 1])))
        return c

    lax.fori_loop(0, groups, spread_rates, 0, unroll=True)

    own_slot = 14

    def send_slots(out, into, k, low, high):
        for s in range(low, high):
            b, t = divmod(s, NEAR)
            i = row_at[(t + 2) % NEAR] * NEAR + lax.rem(my_z + (2, 3, 1, 0)[b], NEAR)
            if s == own_slot:
                mate = me + 1 - 2 * lax.rem(me, 2)
                remote(out.at[mate], into.at[me], k, {"ctx": mate}).start()
                into[pl.ds(me, 1)] = out[pl.ds(me, 1)]
            else:
                for j in (2 * i, 2 * i + 1):
                    remote(out.at[j], into.at[me], k, {"ctx": j}).start()

    for h in range(halves):
        pole_at = pl.ds(h * pole_rows, pole_rows)
        fac = decay[pole_at, :].reshape(poles, SUBS, LANES)

        def chunk(k, carry):
            s, u = carry
            back = steps - 1 - k
            x = source[pl.ds(pl.multiple_of(h * half_rows + k * 64, 64), 64), :].reshape(SUBS, SUBS, LANES)
            g = gradient[pl.ds(pl.multiple_of(h * half_rows + back * 64, 64), 64), :].reshape(SUBS, SUBS, LANES)
            mx = masks[4, pl.ds(pl.multiple_of(k * SUBS, SUBS), SUBS), :]
            mg = masks[5, pl.ds(pl.multiple_of(back * SUBS, SUBS), SUBS), :]
            for t in range(SUBS):
                r = SUBS - 1 - t
                s = s * fac + (x[t] * mx[t : t + 1])[None]
                u = u * fac + (g[r] * mg[r : r + 1])[None]
            return s, u

        zero = jnp.zeros((poles, SUBS, LANES), F32)
        s, u = lax.fori_loop(0, steps, chunk, (zero, zero))
        state[pole_at, :] = s.reshape(pole_rows, LANES)
        costate[pole_at, :] = u.reshape(pole_rows, LANES)

        def pack_first(s, c):
            i = group_of(s)
            low, high = split_pair(state[strided(s, poles, pole_rows), :], costate[strided(s, poles, pole_rows), :])
            first_out[2 * i] = low.astype(BF16)
            first_out[2 * i + 1] = high.astype(BF16)
            return c

        lax.fori_loop(h * SUBS, (h + 1) * SUBS, pack_first, 0, unroll=True)
        send_slots(first_out, first_in, 4, h * SUBS, (h + 1) * SUBS)

    wait_all(residues, 2, ctx - 1)
    wait_all(skips, 3, ctx - 1)

    def spread_others(s, c):
        i = group_of(s)
        coeff[strided(s, poles, pole_rows), :] = unfold(residues[2 * i], residues[2 * i + 1])
        low_s = jnp.broadcast_to(skips[2 * i], (SUBS, LANES))
        high_s = jnp.broadcast_to(skips[2 * i + 1], (SUBS, LANES))
        gain[pl.ds(s, 1), :] = join_pair(low_s, high_s, True)[0:1]
        return c

    lax.fori_loop(0, groups, spread_others, 0, unroll=True)
    state[...] = jnp.zeros_like(state)
    costate[...] = jnp.zeros_like(costate)
    res_sum[...] = jnp.zeros_like(res_sum)
    skip_sum[...] = jnp.zeros_like(skip_sum)

    def raise_powers(h):
        pole_at = pl.ds(h * pole_rows, pole_rows)
        fac = decay[pole_at, :].reshape(poles, SUBS, LANES)
        twice = fac * fac

        def step(k, e):
            for t in range(4):
                to = pl.multiple_of((h * (rows // 2) + k * 4 + t) * pole_rows, pole_rows)
                powers[pl.ds(to, pole_rows), :] = e.reshape(pole_rows, LANES)
                e = e * twice
            return e

        lax.fori_loop(0, rows // 8, step, coeff[pole_at, :].reshape(poles, SUBS, LANES) * fac)

    def half_sweep(h):
        both = pl.ds(h * SUBS, SUBS)
        skip = gain[both, :]

        def chunk(k, c):
            back = steps - 1 - k
            at_x = pl.ds(pl.multiple_of(h * half_rows + k * 64, 64), 64)
            at_g = pl.ds(pl.multiple_of(h * half_rows + back * 64, 64), 64)
            x = source[at_x, :].reshape(SUBS, SUBS, LANES)
            gx = gradient[at_x, :].reshape(SUBS, SUBS, LANES)
            g = gradient[at_g, :].reshape(SUBS, SUBS, LANES)
            keep = masks[0, pl.ds(pl.multiple_of(k * SUBS, SUBS), SUBS), :]
            keep_g = masks[2, pl.ds(pl.multiple_of(back * SUBS, SUBS), SUBS), :]
            out = [skip * x[t] for t in range(SUBS)]
            adj = [skip * g[t] for t in range(SUBS)]
            for p in range(0, poles, GROUP):
                here = pl.ds(h * pole_rows + p * SUBS, GROUP * SUBS)
                shape = (GROUP, SUBS, LANES)
                s = state[here, :].reshape(shape)
                u = costate[here, :].reshape(shape)
                fac = decay[here, :].reshape(shape)
                res = coeff[here, :].reshape(shape)
                acc = res_sum[here, :].reshape(shape)
                for t in range(SUBS):
                    r = SUBS - 1 - t
                    s = s * (fac * keep[t : t + 1][None]) + x[t][None]
                    out[t] = out[t] + jnp.sum(res * s, axis=0)
                    acc = acc + s * gx[t][None]
                    u = u * (fac * keep_g[r : r + 1][None]) + g[r][None]
                    adj[r] = adj[r] + jnp.sum(res * u, axis=0)
                state[here, :] = s.reshape(GROUP * SUBS, LANES)
                costate[here, :] = u.reshape(GROUP * SUBS, LANES)
                res_sum[here, :] = acc.reshape(GROUP * SUBS, LANES)
            output[at_x, :] = jnp.stack(out).reshape(SUBS * SUBS, LANES)
            adjoint[at_g, :] = jnp.stack(adj).reshape(SUBS * SUBS, LANES)
            skip_sum[both, :] = skip_sum[both, :] + jnp.sum(x * gx, axis=0)
            return c

        lax.fori_loop(0, steps, chunk, 0)

    raise_powers(0)
    half_sweep(0)
    raise_powers(1)

    wait_all(first_in, 4, ctx - 1)

    def scan(k, w):
        prefixes[k] = w
        here = jnp.where(low16, first_in[k].astype(F32), first_in[ctx - 1 - k].astype(F32))
        return joins[k] * w + here

    lax.fori_loop(0, ctx, scan, jnp.zeros((poles, LANES), F32), unroll=True)

    def pack_carry(k, c):
        carry_out[k] = jnp.where(low16, prefixes[k], prefixes[ctx - 1 - k]).astype(BF16)
        return c

    lax.fori_loop(0, ctx, pack_carry, 0, unroll=True)
    send_slots(carry_out, carry_in, 5, 0, groups)

    half_sweep(1)

    def pack_res(s, c):
        i = group_of(s)
        a = res_sum[strided(s, poles, pole_rows), :]
        low, high = split_pair(a[:SUBS], a[SUBS:])
        res_part_out[2 * i] = low
        res_part_out[2 * i + 1] = high
        return c

    lax.fori_loop(0, groups, pack_res, 0, unroll=True)
    send_slots(res_part_out, res_part_in, 6, 0, groups)

    def carried_terms(k, acc):
        return acc + keeps[k] * prefixes[k] * swap_halves(first_in[k].astype(F32))

    res_carried = fold(lax.fori_loop(0, ctx, carried_terms, jnp.zeros((poles, LANES), F32)))

    wait_all(carry_in, 5, ctx - 1)

    def unpack_carry(s, c):
        i = group_of(s)
        low, high = carry_in[2 * i].astype(F32), carry_in[2 * i + 1].astype(F32)
        state[strided(s, poles, pole_rows), :] = join_pair(low, high, True)
        costate[strided(s, poles, pole_rows), :] = join_pair(low, high, False)
        return c

    lax.fori_loop(0, groups, unpack_carry, 0, unroll=True)

    for h in range(halves):
        pole_at = pl.ds(h * pole_rows, pole_rows)
        s = state[pole_at, :].reshape(poles, SUBS, LANES)
        u = costate[pole_at, :].reshape(poles, SUBS, LANES)

        fac = decay[pole_at, :].reshape(poles, SUBS, LANES)

        def add_carry(k, c):
            for j in range(4):
                e = powers[pl.ds(pl.multiple_of((h * (rows // 2) + k * 4 + j) * pole_rows, pole_rows), pole_rows), :]
                e = e.reshape(poles, SUBS, LANES)
                for e, t in ((e, k * 8 + 2 * j), (e * fac, k * 8 + 2 * j + 1)):
                    r = rows - 1 - t
                    at_t = pl.ds(pl.multiple_of(h * half_rows + t * SUBS, SUBS), SUBS)
                    at_r = pl.ds(pl.multiple_of(h * half_rows + r * SUBS, SUBS), SUBS)
                    output[at_t, :] = output[at_t, :] + masks[8, pl.ds(t, 1), :] * jnp.sum(e * s, axis=0)
                    adjoint[at_r, :] = adjoint[at_r, :] + masks[9, pl.ds(r, 1), :] * jnp.sum(e * u, axis=0)
            return c

        lax.fori_loop(0, rows // 8, add_carry, 0)

    first_keep, first_both, second_both = masks[0, 0:1, :], masks[1, 0:1, :], masks[1, 1:2, :]
    def team_group(o):
        shift = jnp.int32(2) * o
        x_off = (jnp.int32(TEAM_X) >> shift) & 3
        y_off = (jnp.int32(TEAM_Y) >> shift) & 3
        return lax.rem(my_row + y_off, NEAR) * NEAR + lax.rem(my_x + x_off, NEAR)

    def slot_of(i):
        t = lax.rem(lax.div(i, NEAR) + NEAR - my_y + 2, NEAR)
        z_off = lax.rem(lax.rem(i, NEAR) + NEAR - my_z, NEAR)
        upper = lax.div(z_off, 2)
        return ((1 - upper) * (3 - z_off) + upper * (z_off - 2)) * NEAR + t

    def send_part(j):
        remote(part_out.at[j], part_in.at[my_member], 9, member(j)).start()

    first_row, second_row = head == 0, head == 1
    last_row, last_two = head == SUBS - 1, head >= SUBS - 2

    def above(x, after, by):
        edge = last_row if by == 1 else last_two
        return jnp.where(edge, pltpu.roll(after, SUBS - by, 0), pltpu.roll(x, SUBS - by, 0))

    def leave(o):
        i = team_group(o)
        s = slot_of(i)
        here = pl.ds(at(i, 0), LANES)
        thirds = [pl.ds(at(i, third), LANES) for third in range(3)]
        base = lax.div(s, SUBS) * half_rows + lax.rem(s, SUBS)
        sums = [jnp.zeros((SUBS, LANES), F32)] * 9
        after = [jnp.zeros((SUBS, LANES), F32)] * 3
        for pair in reversed(range(rows // 16)):
            rows16 = pl.ds(pair * 16, 16)
            up16 = upstream[rows16, here].astype(F32)
            f16 = [feats[rows16, lanes].astype(F32) for lanes in thirds]
            for half in (1, 0):
                r = pair * 16 + half * SUBS
                tile = pl.ds(r, SUBS)
                picked = pl.ds(base + r * SUBS, SUBS, stride=SUBS)
                out = output[picked, :].astype(BF16).astype(F32)
                mixed = adjoint[picked, :].astype(BF16).astype(F32)
                part = slice(half * SUBS, (half + 1) * SUBS)
                post = [up16[part] * out, mixed * values[tile, here], mixed * keys[tile, here]]
                next_one, next_two = masks[6, tile, :], masks[7, tile, :]
                for third in range(3):
                    f = f16[third][part]
                    posts[tile, thirds[third]] = post[third]
                    sums[3 * third] = sums[3 * third] + post[third] * f
                    sums[3 * third + 1] = sums[3 * third + 1] + next_one * above(post[third], after[third], 1) * f
                    sums[3 * third + 2] = sums[3 * third + 2] + next_two * above(post[third], after[third], 2) * f
                after = post
        for third, lanes in enumerate(thirds):
            edge_out[:, lanes] = after[third][0:2]
            h1, h2 = halo[1:2, lanes], halo[0:1, lanes]
            sums[3 * third + 1] = sums[3 * third + 1] + jnp.where(first_row, after[third] * first_keep * h1, 0.0)
            sums[3 * third + 2] = (
                sums[3 * third + 2]
                + jnp.where(first_row, after[third] * first_both * h2, 0.0)
                + jnp.where(second_row, after[third] * second_both * h1, 0.0)
            )
        sums = [jnp.sum(x, axis=0, keepdims=True) for x in sums]
        top = jnp.concatenate(sums[:SUBS], axis=0)
        rest = jnp.concatenate([sums[SUBS], skip_sum[pl.ds(s, 1), :]] + sums[:6], axis=0)
        low, high = split_pair(top, rest)
        part_out[2 * i] = low
        part_out[2 * i + 1] = high

    def send_group(o):
        j = team_group(o)
        send_part(2 * j)
        send_part(2 * j + 1)

    def send_and_leave(k, c):
        send_group(2 * k - 2)
        send_group(2 * k - 1)
        leave(2 * k)
        leave(2 * k + 1)
        return c

    leave(0)
    leave(1)
    lax.fori_loop(1, groups // 2, send_and_leave, 0)
    send_group(groups - 2)
    mate = my_member + 1 - 2 * lax.rem(my_member, 2)
    send_part(mate)
    part_in[pl.ds(my_member, 1)] = part_out[pl.ds(my_member, 1)]
    edge_copy = remote(edge_out, edge_in, 8, {"ctx": peer_of(ctx - 1)})
    edge_copy.start()

    def sum_slots(buf, count):
        return lax.fori_loop(0, count, lambda k, acc: acc + buf[k], jnp.zeros((SUBS, LANES), F32), unroll=True)

    wait_all(res_part_in, 6, ctx - 1)
    res_dp_out[...] = sum_slots(res_part_in, ctx) + res_carried

    def send_res(o, c):
        remote(res_dp_out, res_dp_in.at[my_dp], 7, {"dp": dp_peer(o)}).start()
        return c

    lax.fori_loop(1, dp, send_res, 0)
    res_dp_in[pl.ds(my_dp, 1)] = res_dp_out[...][None]

    wait_all(part_in, 9, ctx - 1)
    column_out[...] = sum_slots(part_in, ctx)

    def send_column(o, c):
        remote(column_out, column_in.at[my_column], 10, column_peer(o)).start()
        return c

    lax.fori_loop(1, 8, send_column, 0)
    column_in[pl.ds(my_column, 1)] = column_out[...][None]
    wait_all(column_in, 10, 7)
    whole = sum_slots(column_in, 8) * scale
    tap_out[...] = whole

    for to in far_team:
        remote(tap_out, tap_in.at[my_member], 11, to).start()
    tap_in[pl.ds(my_member, 1)] = whole[None]

    edge_copy.wait()

    def finish(i, c):
        thirds = [pl.ds(at(i, third), LANES) for third in range(3)]
        after = [jnp.where(first_row, edge_in[0:1, lanes], edge_in[1:2, lanes]) for lanes in thirds]
        for pair in reversed(range(rows // 16)):
            done = [[], [], []]
            for half in (1, 0):
                tile = pl.ds(pair * 16 + half * SUBS, SUBS)
                one, two = masks[2, tile, :], masks[3, tile, :]
                for third, lanes in enumerate(thirds):
                    post = posts[tile, lanes]
                    back = (
                        taps[0:1, lanes] * post
                        + taps[1:2, lanes] * (one * above(post, after[third], 1))
                        + taps[2:3, lanes] * (two * above(post, after[third], 2))
                    )
                    done[third].insert(0, back)
                    after[third] = post
            for third, lanes in enumerate(thirds):
                grad_feats[pl.ds(pair * 16, 16), lanes] = jnp.concatenate(done[third], axis=0).astype(BF16)
        return c

    lax.fori_loop(0, groups, finish, 0)
    wait_all(res_dp_in, 7, dp - 1)
    res_whole = sum_slots(res_dp_in, dp) * scale
    grad_res[:SUBS, :] = res_whole[:, : LANES // 2]
    grad_res[SUBS:, :] = swap_halves(res_whole)[:, : LANES // 2]
    for k, buf, slots in [
        (1, rates, ctx),
        (2, residues, ctx),
        (3, skips, ctx),
        (4, first_in, ctx),
        (5, carry_in, ctx),
        (6, res_part_in, ctx),
        (7, res_dp_in, dp),
        (9, part_in, ctx),
        (10, column_in, 8),
        (11, tap_in, ctx),
    ]:
        all_slots(buf, send_sem.at[k], slots - 1)

    wait_all(tap_in, 11, ctx - 1)
    grad_skip[...] = swap_halves(tap_in[me])[1:2, : LANES // 2]

    def place_taps(i, c):
        low, high = tap_in[2 * i], tap_in[2 * i + 1]
        first = join_pair(low, high, True)
        last_row = join_pair(low, high, False)[0:1]
        for third in range(3):
            for j in range(3):
                r = third * 3 + j
                grad_taps[j : j + 1, pl.ds(at(i, third), LANES)] = first[r : r + 1] if r < SUBS else last_row
        return c

    lax.fori_loop(0, groups, place_taps, 0, unroll=True)


def write_out(*refs):
    count = (len(refs) - 1) // 2
    sems = refs[-1]
    copies = [pltpu.make_async_copy(refs[k], refs[count + k], sems.at[k]) for k in range(1, count)]
    quarter = refs[0].shape[0] // 4
    for k in range(4):
        part = pl.ds(k * quarter, quarter)
        copies.append(pltpu.make_async_copy(refs[0].at[part], refs[count].at[part], sems.at[count + k]))
    for copy in copies:
        copy.start()
    for copy in copies:
        copy.wait()


def per_device(features, upstream, lengths, conv_taps, residues, log_rate, skip_gain):
    rows, width = features.shape[1:]
    channels = upstream.shape[2]
    poles, owned = residues.shape
    ctx = lax.axis_size("ctx")
    dp = lax.axis_size("dp")
    scale = 1.0 / math.sqrt(rows * ctx * dp)
    groups = channels // LANES
    vmem = pl.BlockSpec(memory_space=pltpu.VMEM)
    smem = pl.BlockSpec(memory_space=pltpu.SMEM)
    hbm = pl.BlockSpec(memory_space=pltpu.HBM)
    slab = (ctx, poles, LANES)
    folded = (ctx, SUBS, LANES)
    wide = pltpu.VMEM((rows * groups, LANES), F32)
    per_pole = pltpu.VMEM((poles * groups, LANES), F32)
    scratch = [
        pltpu.VMEM((rows, width), BF16),
        pltpu.VMEM((rows, channels), BF16),
        pltpu.VMEM((3, width), F32),
        pltpu.VMEM((poles, owned), F32),
        pltpu.VMEM((poles, owned), F32),
        pltpu.VMEM((1, owned), F32),
        pltpu.VMEM((SUBS, LANES), F32),
        pltpu.VMEM((SUBS, LANES), F32),
        pltpu.VMEM((1, LANES), F32),
        pltpu.VMEM(folded, F32),
        pltpu.VMEM(folded, F32),
        pltpu.VMEM((ctx, 1, LANES), F32),
        pltpu.VMEM((2, width), F32),
        pltpu.VMEM((2, width), F32),
        pltpu.VMEM(slab, BF16),
        pltpu.VMEM(slab, BF16),
        pltpu.VMEM(slab, BF16),
        pltpu.VMEM(slab, BF16),
        pltpu.VMEM(slab, F32),
        pltpu.VMEM(slab, F32),
        pltpu.VMEM(slab, F32),
        wide,
        wide,
        wide,
        wide,
        pltpu.VMEM((SUBS, channels), F32),
        pltpu.VMEM((rows, channels), F32),
        pltpu.VMEM((rows, channels), F32),
        per_pole,
        per_pole,
        pltpu.VMEM((rows // 2 * poles * groups, LANES), F32),
        pltpu.VMEM((groups, LANES), F32),
        per_pole,
        per_pole,
        per_pole,
        pltpu.VMEM((groups, LANES), F32),
        pltpu.VMEM((12, rows, LANES), F32),
        pltpu.VMEM((2, width), F32),
        pltpu.VMEM((2, width), F32),
        pltpu.VMEM((rows, width), F32),
        pltpu.VMEM(folded, F32),
        pltpu.VMEM(folded, F32),
        pltpu.VMEM((SUBS, LANES), F32),
        pltpu.VMEM((dp, SUBS, LANES), F32),
        pltpu.VMEM(folded, F32),
        pltpu.VMEM(folded, F32),
        pltpu.VMEM((SUBS, LANES), F32),
        pltpu.VMEM((8, SUBS, LANES), F32),
        pltpu.VMEM((SUBS, LANES), F32),
        pltpu.VMEM(folded, F32),
        pltpu.SemaphoreType.DMA((6,)),
        pltpu.SemaphoreType.DMA((12,)),
        pltpu.SemaphoreType.DMA((12,)),
    ]
    results = (
        jax.ShapeDtypeStruct((rows, width), BF16),
        jax.ShapeDtypeStruct((3, width), F32),
        jax.ShapeDtypeStruct((poles, owned), F32),
        jax.ShapeDtypeStruct((1, owned), F32),
    )
    held = pl.pallas_call(
        functools.partial(kernel, ctx, dp, scale),
        out_shape=results,
        in_specs=[smem] + [hbm] * 6,
        out_specs=(vmem,) * 4,
        scratch_shapes=scratch,
        compiler_params=pltpu.CompilerParams(
            collective_id=0, has_side_effects=True, vmem_limit_bytes=44 * 1024 * 1024
        ),
        name="conv_block",
    )(
        *(
            pltpu.with_memory_space_constraint(x, pltpu.HBM)
            for x in (lengths, features[0], upstream[0], conv_taps, residues, log_rate, skip_gain[None])
        )
    )
    grad_feats, grad_taps, grad_res, grad_skip = pl.pallas_call(
        write_out,
        out_shape=results,
        in_specs=[vmem] * 4,
        out_specs=(hbm,) * 4,
        scratch_shapes=[pltpu.SemaphoreType.DMA((8,))],
        compiler_params=pltpu.CompilerParams(vmem_limit_bytes=8 * 1024 * 1024),
        name="write_out",
    )(*held)
    return (grad_feats[None], grad_taps, grad_res, grad_skip[0])


def solution(mesh):
    return jax.shard_map(
        per_device,
        mesh=mesh,
        in_specs=(
            P("dp", "ctx", None),
            P("dp", "ctx", None),
            P("dp", None),
            P(),
            P(None, "ctx"),
            P(None, "ctx"),
            P("ctx"),
        ),
        out_specs=(P("dp", "ctx", None), P(), P(None, "ctx"), P("ctx")),
        check_vma=False,
    )
```

```python
import functools
import math

import jax
import jax.numpy as jnp
from jax import lax
from jax.experimental import pallas as pl
from jax.experimental.pallas import tpu as pltpu
from jax.sharding import PartitionSpec as P

MESH = pl.DeviceIdType.MESH
F32 = jnp.float32
BF16 = jnp.bfloat16
LANES = 128
SUBS = 8
GROUP = 4
NEAR = 4


def row_iota(rows):
    return lax.broadcasted_iota(jnp.int32, (rows, LANES), 0)


def lane_low(rows):
    return lax.broadcasted_iota(jnp.int32, (rows, LANES), 1) < LANES // 2


def swap_halves(x):
    return pltpu.roll(x, LANES // 2, 1)


def join_pair(low, high, first):
    mask = lane_low(low.shape[0])
    if first:
        return jnp.where(mask, low, swap_halves(high))
    return jnp.where(mask, swap_halves(low), high)


def split_pair(a, b):
    mask = lane_low(a.shape[0])
    return jnp.where(mask, a, swap_halves(b)), jnp.where(mask, swap_halves(a), b)


def unfold(low, high):
    return jnp.concatenate([join_pair(low, high, True), join_pair(low, high, False)], axis=0)


def fold(x):
    return jnp.where(lane_low(SUBS), x[:SUBS], swap_halves(x[SUBS:]))


FAR_Z = (4, 3, 5, 2, 6, 1, 7, 0)
FAR = (2, 1, 3, 0)
TEAM_X = sum(v << (2 * k) for k, v in enumerate((2, 2, 2, 1, 3, 2, 0, 1, 1, 3, 3, 1, 3, 0, 0, 0)))
TEAM_Y = sum(v << (2 * k) for k, v in enumerate((2, 1, 3, 2, 2, 0, 2, 1, 3, 1, 3, 0, 0, 1, 3, 0)))


def free_of(bounds, low, high):
    clear = None
    for bound in bounds:
        one = (low > bound) | (high < bound)
        clear = one if clear is None else clear & one
    return jnp.where(clear, 1.0, 0.0).astype(F32)


def kernel(
    ctx,
    dp,
    scale,
    lengths,
    feats_in,
    upstream_in,
    taps_in,
    res_in,
    rate_in,
    skip_in,
    grad_feats,
    grad_taps,
    grad_res,
    grad_skip,
    feats,
    upstream,
    taps,
    own_res,
    own_rate,
    own_skip,
    rate_out,
    res_out,
    skip_out,
    rates,
    residues,
    skips,
    halo_out,
    halo,
    first_out,
    first_in,
    carry_out,
    carry_in,
    prefixes,
    joins,
    keeps,
    source,
    gradient,
    output,
    adjoint,
    queries,
    keys,
    values,
    decay,
    coeff,
    powers,
    gain,
    state,
    costate,
    res_sum,
    skip_sum,
    masks,
    edge_out,
    edge_in,
    posts,
    res_part_out,
    res_part_in,
    res_dp_out,
    res_dp_in,
    part_out,
    part_in,
    column_out,
    column_in,
    tap_out,
    tap_in,
    load_sem,
    send_sem,
    recv_sem,
):
    rows, channels = upstream.shape
    poles = own_res.shape[0]
    groups = channels // LANES
    halves = groups // SUBS
    half_rows = rows * SUBS
    pole_rows = poles * SUBS
    steps = rows // SUBS
    window = rows * ctx
    me = lax.axis_index("ctx")
    my_dp = lax.axis_index("dp")

    def peer_of(o):
        return lax.rem(me + o, ctx)

    def far_first(o):
        k, j = lax.div(o, 4), lax.rem(o, 4)
        z_off = 4 + (1 - 2 * lax.rem(k, 2)) * lax.div(k + 1, 2)
        y_off = 2 + (1 - 2 * lax.rem(j, 2)) * lax.div(j + 1, 2)
        y = lax.rem(lax.div(me, 8) + y_off, 4)
        return y * 8 + lax.rem(lax.rem(me, 8) + z_off, 8)

    def dp_peer(o):
        return lax.rem(my_dp + o, dp)

    my_column, my_row = lax.rem(me, 8), lax.div(me, 8)
    my_member = my_row * dp + my_dp
    my_x, my_core = lax.div(my_dp, 2), lax.rem(my_dp, 2)
    row_at = [lax.rem(my_row + k, 4) for k in range(4)]
    column_at = [lax.rem(my_column + k, 8) for k in range(8)]
    x_at = [lax.rem(my_x + k, 4) * 2 for k in range(4)]
    core_at = [my_core, 1 - my_core]
    far_ctx = [{"ctx": row_at[y] * 8 + column_at[z]} for z in FAR_Z for y in FAR if y or z]
    far_team = [
        {"ctx": row_at[y] * 8 + my_column, "dp": x_at[x] + core_at[c]}
        for x in FAR
        for y in FAR
        for c in (1, 0)
        if x or y or c
    ]

    def member(j):
        return {"ctx": lax.div(j, dp) * 8 + my_column, "dp": lax.rem(j, dp)}

    def column_peer(o):
        return {"ctx": my_row * 8 + lax.rem(my_column + o, 8)}

    loads = [
        pltpu.make_async_copy(src, dst, load_sem.at[k])
        for k, (src, dst) in enumerate(
            [
                (rate_in, own_rate),
                (res_in, own_res),
                (skip_in, own_skip),
                (taps_in, taps),
                (feats_in, feats),
                (upstream_in, upstream),
            ]
        )
    ]
    for load in loads:
        load.start()

    barrier = pltpu.get_barrier_semaphore()

    for to in far_ctx + far_team:
        pl.semaphore_signal(barrier, inc=1, device_id=to, device_id_type=MESH)

    for load in loads[:3]:
        load.wait()
    rate_out[...] = jnp.concatenate([own_rate[:SUBS, :], own_rate[SUBS:, :]], axis=1)
    res_out[...] = jnp.concatenate([own_res[:SUBS, :], own_res[SUBS:, :]], axis=1)
    skip_out[...] = jnp.concatenate([own_skip[...], own_skip[...]], axis=1)

    bounds = [0]
    total = 0
    for j in range(lengths.shape[1] - 1):
        total = total + lengths[0, j]
        bounds.append(total)
    bounds.append(window)
    start = me * rows
    row = row_iota(rows)
    pos = start + row
    flat = 0 * row
    next_one = free_of(bounds, pos + 1, pos + 1)
    next_two = free_of(bounds, pos + 1, pos + 2)
    masks[0] = free_of(bounds, pos, pos)
    masks[1] = free_of(bounds, pos - 1, pos)
    masks[2] = next_one
    masks[3] = next_two

    masks[10] = jnp.where(row > 0, masks[0], 0.0)
    masks[11] = jnp.where(row > 1, masks[1], 0.0)

    my_y, my_z = lax.div(me, 2 * NEAR), lax.rem(lax.div(me, 2), NEAR)

    def group_of(s):
        b, t = lax.div(s, NEAR), lax.rem(s, NEAR)
        upper = lax.div(b, 2)
        z_off = (1 - upper) * (b + 2) + upper * (3 - b)
        y = lax.rem(my_y + t + 2, NEAR)
        return y * NEAR + lax.rem(my_z + z_off, NEAR)

    def at(i, third):
        return pl.multiple_of(third * channels + i * LANES, LANES)

    def strided(s, count, stride_rows):
        return pl.ds(lax.div(s, SUBS) * stride_rows + lax.rem(s, SUBS), count, stride=SUBS)

    for load in loads[3:]:
        load.wait()

    def featured(off):
        lanes = pl.ds(off, LANES)
        f = feats[:, lanes].astype(F32)
        one = masks[10] * pltpu.roll(f, 1, 0)
        two = masks[11] * pltpu.roll(f, 2, 0)
        halo_out[:, lanes] = f[rows - 2 :]
        return taps[0:1, lanes] * f + taps[1:2, lanes] * one + taps[2:3, lanes] * two

    def enter(s, c):
        i = group_of(s)
        query, key, value = (featured(at(i, third)) for third in range(3))
        lanes = pl.ds(at(i, 0), LANES)
        up = upstream[:, lanes].astype(F32)
        keys[:, lanes] = key
        values[:, lanes] = value
        queries[:, lanes] = query[:SUBS]
        source[strided(s, rows, half_rows), :] = (key * value).astype(BF16).astype(F32)
        gradient[strided(s, rows, half_rows), :] = (up * query).astype(BF16).astype(F32)
        return c

    lax.fori_loop(0, groups, enter, 0)

    pl.semaphore_wait(barrier, 2 * (ctx - 1))

    def remote(src, dst, k, to):
        return pltpu.make_async_remote_copy(
            src_ref=src, dst_ref=dst, send_sem=send_sem.at[k], recv_sem=recv_sem.at[k], device_id=to, device_id_type=MESH
        )

    for to in far_ctx:
        remote(rate_out, rates.at[me], 1, to).start()
    halo_copy = remote(halo_out, halo, 0, {"ctx": peer_of(1)})
    halo_copy.start()

    def send_others(o, c):
        remote(res_out, residues.at[me], 2, {"ctx": far_first(o)}).start()
        remote(skip_out, skips.at[me], 3, {"ctx": far_first(o)}).start()
        return c

    lax.fori_loop(0, ctx - 1, send_others, 0)
    rates[pl.ds(me, 1)] = rate_out[...][None]
    residues[pl.ds(me, 1)] = res_out[...][None]
    skips[pl.ds(me, 1)] = skip_out[...][None]

    masks[4] = free_of(bounds, pos + 1, flat + (start + rows - 1))
    masks[5] = free_of(bounds, flat + (start + 1), pos)
    masks[6] = jnp.where(row < rows - 1, next_one, 0.0)
    masks[7] = jnp.where(row < rows - 2, next_two, 0.0)
    masks[8] = free_of(bounds, flat + start, pos)
    masks[9] = free_of(bounds, pos + 1, flat + (start + rows))

    low16 = lane_low(poles)
    my_rate = jnp.concatenate([own_rate[...], own_rate[...]], axis=1)
    my_decay = jnp.exp(-jnp.exp(my_rate))
    block_decay = jnp.exp(-jnp.exp(my_rate) * rows)

    def join_masks(k, c):
        low = jnp.where(low16, k * rows, (ctx - 1 - k) * rows + 1)
        joins[k] = free_of(bounds, low, low + (rows - 1)) * block_decay
        keeps[k] = free_of(bounds, low, low) * my_decay
        return c

    lax.fori_loop(0, ctx, join_masks, 0)

    halo_copy.wait()
    head = row_iota(SUBS)
    on_first = jnp.where(head == 0, masks[0, :SUBS, :], 0.0)
    both_first = jnp.where(head == 0, masks[1, :SUBS, :], 0.0)
    both_second = jnp.where(head == 1, masks[1, :SUBS, :], 0.0)

    def mend(s, c):
        i = group_of(s)
        here = pl.ds(at(i, 0), LANES)
        parts = []
        for third, buf in enumerate((queries, keys, values)):
            lanes = pl.ds(at(i, third), LANES)
            one, two = taps[1:2, lanes], taps[2:3, lanes]
            h1, h2 = halo[1:2, lanes], halo[0:1, lanes]
            parts.append(buf[:SUBS, here] + (on_first * one + both_second * two) * h1 + (both_first * two) * h2)
        query, key, value = parts
        keys[:SUBS, here] = key
        values[:SUBS, here] = value
        up = upstream[: 2 * SUBS, here].astype(F32)[:SUBS]
        source[strided(s, SUBS, half_rows), :] = (key * value).astype(BF16).astype(F32)
        gradient[strided(s, SUBS, half_rows), :] = (up * query).astype(BF16).astype(F32)
        return c

    lax.fori_loop(0, groups, mend, 0, unroll=True)

    def all_slots(buf, sem, slots):
        pltpu.make_async_copy(buf.at[pl.ds(0, slots)], buf.at[pl.ds(0, slots)], sem).wait()

    def wait_all(buf, k, slots):
        all_slots(buf, recv_sem.at[k], slots)

    wait_all(rates, 1, ctx - 1)

    def spread_rates(s, c):
        i = group_of(s)
        decay[strided(s, poles, pole_rows), :] = jnp.exp(-jnp.exp(unfold(rates[2 * i], rates[2 * i + 1])))
        return c

    lax.fori_loop(0, groups, spread_rates, 0, unroll=True)

    own_slot = 14

    def send_slots(out, into, k, low, high):
        for s in range(low, high):
            b, t = divmod(s, NEAR)
            i = row_at[(t + 2) % NEAR] * NEAR + lax.rem(my_z + (2, 3, 1, 0)[b], NEAR)
            if s == own_slot:
                mate = me + 1 - 2 * lax.rem(me, 2)
                remote(out.at[mate], into.at[me], k, {"ctx": mate}).start()
                into[pl.ds(me, 1)] = out[pl.ds(me, 1)]
            else:
                for j in (2 * i, 2 * i + 1):
                    remote(out.at[j], into.at[me], k, {"ctx": j}).start()

    for h in range(halves):
        pole_at = pl.ds(h * pole_rows, pole_rows)
        fac = decay[pole_at, :].reshape(poles, SUBS, LANES)

        def chunk(k, carry):
            s, u = carry
            back = steps - 1 - k
            x = source[pl.ds(pl.multiple_of(h * half_rows + k * 64, 64), 64), :].reshape(SUBS, SUBS, LANES)
            g = gradient[pl.ds(pl.multiple_of(h * half_rows + back * 64, 64), 64), :].reshape(SUBS, SUBS, LANES)
            mx = masks[4, pl.ds(pl.multiple_of(k * SUBS, SUBS), SUBS), :]
            mg = masks[5, pl.ds(pl.multiple_of(back * SUBS, SUBS), SUBS), :]
            for t in range(SUBS):
                r = SUBS - 1 - t
                s = s * fac + (x[t] * mx[t : t + 1])[None]
                u = u * fac + (g[r] * mg[r : r + 1])[None]
            return s, u

        zero = jnp.zeros((poles, SUBS, LANES), F32)
        s, u = lax.fori_loop(0, steps, chunk, (zero, zero))
        state[pole_at, :] = s.reshape(pole_rows, LANES)
        costate[pole_at, :] = u.reshape(pole_rows, LANES)

        def pack_first(s, c):
            i = group_of(s)
            low, high = split_pair(state[strided(s, poles, pole_rows), :], costate[strided(s, poles, pole_rows), :])
            first_out[2 * i] = low.astype(BF16)
            first_out[2 * i + 1] = high.astype(BF16)
            return c

        lax.fori_loop(h * SUBS, (h + 1) * SUBS, pack_first, 0, unroll=True)
        send_slots(first_out, first_in, 4, h * SUBS, (h + 1) * SUBS)

    wait_all(residues, 2, ctx - 1)
    wait_all(skips, 3, ctx - 1)

    def spread_others(s, c):
        i = group_of(s)
        coeff[strided(s, poles, pole_rows), :] = unfold(residues[2 * i], residues[2 * i + 1])
        low_s = jnp.broadcast_to(skips[2 * i], (SUBS, LANES))
        high_s = jnp.broadcast_to(skips[2 * i + 1], (SUBS, LANES))
        gain[pl.ds(s, 1), :] = join_pair(low_s, high_s, True)[0:1]
        return c

    lax.fori_loop(0, groups, spread_others, 0, unroll=True)
    state[...] = jnp.zeros_like(state)
    costate[...] = jnp.zeros_like(costate)
    res_sum[...] = jnp.zeros_like(res_sum)
    skip_sum[...] = jnp.zeros_like(skip_sum)

    def raise_powers(h):
        pole_at = pl.ds(h * pole_rows, pole_rows)
        fac = decay[pole_at, :].reshape(poles, SUBS, LANES)
        twice = fac * fac

        def step(k, e):
            for t in range(4):
                to = pl.multiple_of((h * (rows // 2) + k * 4 + t) * pole_rows, pole_rows)
                powers[pl.ds(to, pole_rows), :] = e.reshape(pole_rows, LANES)
                e = e * twice
            return e

        lax.fori_loop(0, rows // 8, step, coeff[pole_at, :].reshape(poles, SUBS, LANES) * fac)

    def half_sweep(h):
        both = pl.ds(h * SUBS, SUBS)
        skip = gain[both, :]

        def chunk(k, c):
            back = steps - 1 - k
            at_x = pl.ds(pl.multiple_of(h * half_rows + k * 64, 64), 64)
            at_g = pl.ds(pl.multiple_of(h * half_rows + back * 64, 64), 64)
            x = source[at_x, :].reshape(SUBS, SUBS, LANES)
            gx = gradient[at_x, :].reshape(SUBS, SUBS, LANES)
            g = gradient[at_g, :].reshape(SUBS, SUBS, LANES)
            keep = masks[0, pl.ds(pl.multiple_of(k * SUBS, SUBS), SUBS), :]
            keep_g = masks[2, pl.ds(pl.multiple_of(back * SUBS, SUBS), SUBS), :]
            out = [skip * x[t] for t in range(SUBS)]
            adj = [skip * g[t] for t in range(SUBS)]
            for p in range(0, poles, GROUP):
                here = pl.ds(h * pole_rows + p * SUBS, GROUP * SUBS)
                shape = (GROUP, SUBS, LANES)
                s = state[here, :].reshape(shape)
                u = costate[here, :].reshape(shape)
                fac = decay[here, :].reshape(shape)
                res = coeff[here, :].reshape(shape)
                acc = res_sum[here, :].reshape(shape)
                for t in range(SUBS):
                    r = SUBS - 1 - t
                    s = s * (fac * keep[t : t + 1][None]) + x[t][None]
                    out[t] = out[t] + jnp.sum(res * s, axis=0)
                    acc = acc + s * gx[t][None]
                    u = u * (fac * keep_g[r : r + 1][None]) + g[r][None]
                    adj[r] = adj[r] + jnp.sum(res * u, axis=0)
                state[here, :] = s.reshape(GROUP * SUBS, LANES)
                costate[here, :] = u.reshape(GROUP * SUBS, LANES)
                res_sum[here, :] = acc.reshape(GROUP * SUBS, LANES)
            output[at_x, :] = jnp.stack(out).reshape(SUBS * SUBS, LANES)
            adjoint[at_g, :] = jnp.stack(adj).reshape(SUBS * SUBS, LANES)
            skip_sum[both, :] = skip_sum[both, :] + jnp.sum(x * gx, axis=0)
            return c

        lax.fori_loop(0, steps, chunk, 0)

    raise_powers(0)
    half_sweep(0)
    raise_powers(1)

    wait_all(first_in, 4, ctx - 1)

    def scan(k, w):
        prefixes[k] = w
        here = jnp.where(low16, first_in[k].astype(F32), first_in[ctx - 1 - k].astype(F32))
        return joins[k] * w + here

    lax.fori_loop(0, ctx, scan, jnp.zeros((poles, LANES), F32), unroll=True)

    def pack_carry(k, c):
        carry_out[k] = jnp.where(low16, prefixes[k], prefixes[ctx - 1 - k]).astype(BF16)
        return c

    lax.fori_loop(0, ctx, pack_carry, 0, unroll=True)
    send_slots(carry_out, carry_in, 5, 0, groups)

    half_sweep(1)

    def pack_res(s, c):
        i = group_of(s)
        a = res_sum[strided(s, poles, pole_rows), :]
        low, high = split_pair(a[:SUBS], a[SUBS:])
        res_part_out[2 * i] = low
        res_part_out[2 * i + 1] = high
        return c

    lax.fori_loop(0, groups, pack_res, 0, unroll=True)
    send_slots(res_part_out, res_part_in, 6, 0, groups)

    def carried_terms(k, acc):
        return acc + keeps[k] * prefixes[k] * swap_halves(first_in[k].astype(F32))

    res_carried = fold(lax.fori_loop(0, ctx, carried_terms, jnp.zeros((poles, LANES), F32)))

    wait_all(carry_in, 5, ctx - 1)

    def unpack_carry(s, c):
        i = group_of(s)
        low, high = carry_in[2 * i].astype(F32), carry_in[2 * i + 1].astype(F32)
        state[strided(s, poles, pole_rows), :] = join_pair(low, high, True)
        costate[strided(s, poles, pole_rows), :] = join_pair(low, high, False)
        return c

    lax.fori_loop(0, groups, unpack_carry, 0, unroll=True)

    for h in range(halves):
        pole_at = pl.ds(h * pole_rows, pole_rows)
        s = state[pole_at, :].reshape(poles, SUBS, LANES)
        u = costate[pole_at, :].reshape(poles, SUBS, LANES)

        fac = decay[pole_at, :].reshape(poles, SUBS, LANES)

        def add_carry(k, c):
            for j in range(4):
                e = powers[pl.ds(pl.multiple_of((h * (rows // 2) + k * 4 + j) * pole_rows, pole_rows), pole_rows), :]
                e = e.reshape(poles, SUBS, LANES)
                for e, t in ((e, k * 8 + 2 * j), (e * fac, k * 8 + 2 * j + 1)):
                    r = rows - 1 - t
                    at_t = pl.ds(pl.multiple_of(h * half_rows + t * SUBS, SUBS), SUBS)
                    at_r = pl.ds(pl.multiple_of(h * half_rows + r * SUBS, SUBS), SUBS)
                    output[at_t, :] = output[at_t, :] + masks[8, pl.ds(t, 1), :] * jnp.sum(e * s, axis=0)
                    adjoint[at_r, :] = adjoint[at_r, :] + masks[9, pl.ds(r, 1), :] * jnp.sum(e * u, axis=0)
            return c

        lax.fori_loop(0, rows // 8, add_carry, 0)

    first_keep, first_both, second_both = masks[0, 0:1, :], masks[1, 0:1, :], masks[1, 1:2, :]
    def team_group(o):
        shift = jnp.int32(2) * o
        x_off = (jnp.int32(TEAM_X) >> shift) & 3
        y_off = (jnp.int32(TEAM_Y) >> shift) & 3
        return lax.rem(my_row + y_off, NEAR) * NEAR + lax.rem(my_x + x_off, NEAR)

    def slot_of(i):
        t = lax.rem(lax.div(i, NEAR) + NEAR - my_y + 2, NEAR)
        z_off = lax.rem(lax.rem(i, NEAR) + NEAR - my_z, NEAR)
        upper = lax.div(z_off, 2)
        return ((1 - upper) * (3 - z_off) + upper * (z_off - 2)) * NEAR + t

    def send_part(j):
        remote(part_out.at[j], part_in.at[my_member], 9, member(j)).start()

    first_row, second_row = head == 0, head == 1
    last_row, last_two = head == SUBS - 1, head >= SUBS - 2

    def above(x, after, by):
        edge = last_row if by == 1 else last_two
        return jnp.where(edge, pltpu.roll(after, SUBS - by, 0), pltpu.roll(x, SUBS - by, 0))

    def leave(o):
        i = team_group(o)
        s = slot_of(i)
        here = pl.ds(at(i, 0), LANES)
        thirds = [pl.ds(at(i, third), LANES) for third in range(3)]
        base = lax.div(s, SUBS) * half_rows + lax.rem(s, SUBS)
        sums = [jnp.zeros((SUBS, LANES), F32)] * 9
        after = [jnp.zeros((SUBS, LANES), F32)] * 3
        for pair in reversed(range(rows // 16)):
            rows16 = pl.ds(pair * 16, 16)
            up16 = upstream[rows16, here].astype(F32)
            f16 = [feats[rows16, lanes].astype(F32) for lanes in thirds]
            for half in (1, 0):
                r = pair * 16 + half * SUBS
                tile = pl.ds(r, SUBS)
                picked = pl.ds(base + r * SUBS, SUBS, stride=SUBS)
                out = output[picked, :].astype(BF16).astype(F32)
                mixed = adjoint[picked, :].astype(BF16).astype(F32)
                part = slice(half * SUBS, (half + 1) * SUBS)
                post = [up16[part] * out, mixed * values[tile, here], mixed * keys[tile, here]]
                next_one, next_two = masks[6, tile, :], masks[7, tile, :]
                for third in range(3):
                    f = f16[third][part]
                    posts[tile, thirds[third]] = post[third]
                    sums[3 * third] = sums[3 * third] + post[third] * f
                    sums[3 * third + 1] = sums[3 * third + 1] + next_one * above(post[third], after[third], 1) * f
                    sums[3 * third + 2] = sums[3 * third + 2] + next_two * above(post[third], after[third], 2) * f
                after = post
        for third, lanes in enumerate(thirds):
            edge_out[:, lanes] = after[third][0:2]
            h1, h2 = halo[1:2, lanes], halo[0:1, lanes]
            sums[3 * third + 1] = sums[3 * third + 1] + jnp.where(first_row, after[third] * first_keep * h1, 0.0)
            sums[3 * third + 2] = (
                sums[3 * third + 2]
                + jnp.where(first_row, after[third] * first_both * h2, 0.0)
                + jnp.where(second_row, after[third] * second_both * h1, 0.0)
            )
        sums = [jnp.sum(x, axis=0, keepdims=True) for x in sums]
        top = jnp.concatenate(sums[:SUBS], axis=0)
        rest = jnp.concatenate([sums[SUBS], skip_sum[pl.ds(s, 1), :]] + sums[:6], axis=0)
        low, high = split_pair(top, rest)
        part_out[2 * i] = low
        part_out[2 * i + 1] = high

    def send_group(o):
        j = team_group(o)
        send_part(2 * j)
        send_part(2 * j + 1)

    def send_and_leave(k, c):
        send_group(2 * k - 2)
        send_group(2 * k - 1)
        leave(2 * k)
        leave(2 * k + 1)
        return c

    leave(0)
    leave(1)
    lax.fori_loop(1, groups // 2, send_and_leave, 0)
    send_group(groups - 2)
    mate = my_member + 1 - 2 * lax.rem(my_member, 2)
    send_part(mate)
    part_in[pl.ds(my_member, 1)] = part_out[pl.ds(my_member, 1)]
    edge_copy = remote(edge_out, edge_in, 8, {"ctx": peer_of(ctx - 1)})
    edge_copy.start()

    def sum_slots(buf, count):
        return lax.fori_loop(0, count, lambda k, acc: acc + buf[k], jnp.zeros((SUBS, LANES), F32), unroll=True)

    wait_all(res_part_in, 6, ctx - 1)
    res_dp_out[...] = sum_slots(res_part_in, ctx) + res_carried

    def send_res(o, c):
        remote(res_dp_out, res_dp_in.at[my_dp], 7, {"dp": dp_peer(o)}).start()
        return c

    lax.fori_loop(1, dp, send_res, 0)
    res_dp_in[pl.ds(my_dp, 1)] = res_dp_out[...][None]

    wait_all(part_in, 9, ctx - 1)
    column_out[...] = sum_slots(part_in, ctx)

    def send_column(o, c):
        remote(column_out, column_in.at[my_column], 10, column_peer(o)).start()
        return c

    lax.fori_loop(1, 8, send_column, 0)
    column_in[pl.ds(my_column, 1)] = column_out[...][None]
    wait_all(column_in, 10, 7)
    whole = sum_slots(column_in, 8) * scale
    tap_out[...] = whole

    for to in far_team:
        remote(tap_out, tap_in.at[my_member], 11, to).start()
    tap_in[pl.ds(my_member, 1)] = whole[None]

    edge_copy.wait()

    def finish(i, c):
        thirds = [pl.ds(at(i, third), LANES) for third in range(3)]
        after = [jnp.where(first_row, edge_in[0:1, lanes], edge_in[1:2, lanes]) for lanes in thirds]
        for pair in reversed(range(rows // 16)):
            done = [[], [], []]
            for half in (1, 0):
                tile = pl.ds(pair * 16 + half * SUBS, SUBS)
                one, two = masks[2, tile, :], masks[3, tile, :]
                for third, lanes in enumerate(thirds):
                    post = posts[tile, lanes]
                    back = (
                        taps[0:1, lanes] * post
                        + taps[1:2, lanes] * (one * above(post, after[third], 1))
                        + taps[2:3, lanes] * (two * above(post, after[third], 2))
                    )
                    done[third].insert(0, back)
                    after[third] = post
            for third, lanes in enumerate(thirds):
                grad_feats[pl.ds(pair * 16, 16), lanes] = jnp.concatenate(done[third], axis=0).astype(BF16)
        return c

    lax.fori_loop(0, groups, finish, 0)
    wait_all(res_dp_in, 7, dp - 1)
    res_whole = sum_slots(res_dp_in, dp) * scale
    grad_res[:SUBS, :] = res_whole[:, : LANES // 2]
    grad_res[SUBS:, :] = swap_halves(res_whole)[:, : LANES // 2]
    for k, buf, slots in [
        (1, rates, ctx),
        (2, residues, ctx),
        (3, skips, ctx),
        (4, first_in, ctx),
        (5, carry_in, ctx),
        (6, res_part_in, ctx),
        (7, res_dp_in, dp),
        (9, part_in, ctx),
        (10, column_in, 8),
        (11, tap_in, ctx),
    ]:
        all_slots(buf, send_sem.at[k], slots - 1)

    wait_all(tap_in, 11, ctx - 1)
    grad_skip[...] = swap_halves(tap_in[me])[1:2, : LANES // 2]

    def place_taps(i, c):
        low, high = tap_in[2 * i], tap_in[2 * i + 1]
        first = join_pair(low, high, True)
        last_row = join_pair(low, high, False)[0:1]
        for third in range(3):
            for j in range(3):
                r = third * 3 + j
                grad_taps[j : j + 1, pl.ds(at(i, third), LANES)] = first[r : r + 1] if r < SUBS else last_row
        return c

    lax.fori_loop(0, groups, place_taps, 0, unroll=True)


def write_out(*refs):
    count = (len(refs) - 1) // 2
    sems = refs[-1]
    copies = [pltpu.make_async_copy(refs[k], refs[count + k], sems.at[k]) for k in range(1, count)]
    quarter = refs[0].shape[0] // 4
    for k in range(4):
        part = pl.ds(k * quarter, quarter)
        copies.append(pltpu.make_async_copy(refs[0].at[part], refs[count].at[part], sems.at[count + k]))
    for copy in copies:
        copy.start()
    for copy in copies:
        copy.wait()


def per_device(features, upstream, lengths, conv_taps, residues, log_rate, skip_gain):
    rows, width = features.shape[1:]
    channels = upstream.shape[2]
    poles, owned = residues.shape
    ctx = lax.axis_size("ctx")
    dp = lax.axis_size("dp")
    scale = 1.0 / math.sqrt(rows * ctx * dp)
    groups = channels // LANES
    vmem = pl.BlockSpec(memory_space=pltpu.VMEM)
    smem = pl.BlockSpec(memory_space=pltpu.SMEM)
    hbm = pl.BlockSpec(memory_space=pltpu.HBM)
    slab = (ctx, poles, LANES)
    folded = (ctx, SUBS, LANES)
    wide = pltpu.VMEM((rows * groups, LANES), F32)
    per_pole = pltpu.VMEM((poles * groups, LANES), F32)
    scratch = [
        pltpu.VMEM((rows, width), BF16),
        pltpu.VMEM((rows, channels), BF16),
        pltpu.VMEM((3, width), F32),
        pltpu.VMEM((poles, owned), F32),
        pltpu.VMEM((poles, owned), F32),
        pltpu.VMEM((1, owned), F32),
        pltpu.VMEM((SUBS, LANES), F32),
        pltpu.VMEM((SUBS, LANES), F32),
        pltpu.VMEM((1, LANES), F32),
        pltpu.VMEM(folded, F32),
        pltpu.VMEM(folded, F32),
        pltpu.VMEM((ctx, 1, LANES), F32),
        pltpu.VMEM((2, width), F32),
        pltpu.VMEM((2, width), F32),
        pltpu.VMEM(slab, BF16),
        pltpu.VMEM(slab, BF16),
        pltpu.VMEM(slab, BF16),
        pltpu.VMEM(slab, BF16),
        pltpu.VMEM(slab, F32),
        pltpu.VMEM(slab, F32),
        pltpu.VMEM(slab, F32),
        wide,
        wide,
        wide,
        wide,
        pltpu.VMEM((SUBS, channels), F32),
        pltpu.VMEM((rows, channels), F32),
        pltpu.VMEM((rows, channels), F32),
        per_pole,
        per_pole,
        pltpu.VMEM((rows // 2 * poles * groups, LANES), F32),
        pltpu.VMEM((groups, LANES), F32),
        per_pole,
        per_pole,
        per_pole,
        pltpu.VMEM((groups, LANES), F32),
        pltpu.VMEM((12, rows, LANES), F32),
        pltpu.VMEM((2, width), F32),
        pltpu.VMEM((2, width), F32),
        pltpu.VMEM((rows, width), F32),
        pltpu.VMEM(folded, F32),
        pltpu.VMEM(folded, F32),
        pltpu.VMEM((SUBS, LANES), F32),
        pltpu.VMEM((dp, SUBS, LANES), F32),
        pltpu.VMEM(folded, F32),
        pltpu.VMEM(folded, F32),
        pltpu.VMEM((SUBS, LANES), F32),
        pltpu.VMEM((8, SUBS, LANES), F32),
        pltpu.VMEM((SUBS, LANES), F32),
        pltpu.VMEM(folded, F32),
        pltpu.SemaphoreType.DMA((6,)),
        pltpu.SemaphoreType.DMA((12,)),
        pltpu.SemaphoreType.DMA((12,)),
    ]
    results = (
        jax.ShapeDtypeStruct((rows, width), BF16),
        jax.ShapeDtypeStruct((3, width), F32),
        jax.ShapeDtypeStruct((poles, owned), F32),
        jax.ShapeDtypeStruct((1, owned), F32),
    )
    held = pl.pallas_call(
        functools.partial(kernel, ctx, dp, scale),
        out_shape=results,
        in_specs=[smem] + [hbm] * 6,
        out_specs=(vmem,) * 4,
        scratch_shapes=scratch,
        compiler_params=pltpu.CompilerParams(
            collective_id=0, has_side_effects=True, vmem_limit_bytes=44 * 1024 * 1024
        ),
        name="conv_block",
    )(
        *(
            pltpu.with_memory_space_constraint(x, pltpu.HBM)
            for x in (lengths, features[0], upstream[0], conv_taps, residues, log_rate, skip_gain[None])
        )
    )
    grad_feats, grad_taps, grad_res, grad_skip = pl.pallas_call(
        write_out,
        out_shape=results,
        in_specs=[vmem] * 4,
        out_specs=(hbm,) * 4,
        scratch_shapes=[pltpu.SemaphoreType.DMA((8,))],
        compiler_params=pltpu.CompilerParams(vmem_limit_bytes=8 * 1024 * 1024),
        name="write_out",
    )(*held)
    return (grad_feats[None], grad_taps, grad_res, grad_skip[0])


def solution(mesh):
    return jax.shard_map(
        per_device,
        mesh=mesh,
        in_specs=(
            P("dp", "ctx", None),
            P("dp", "ctx", None),
            P("dp", None),
            P(),
            P(None, "ctx"),
            P(None, "ctx"),
            P("ctx"),
        ),
        out_specs=(P("dp", "ctx", None), P(), P(None, "ctx"), P("ctx")),
        check_vma=False,
    )
```
